256 devices in a mesh: doc: 64 (over z, y, core), feat: 4 (over x).
Axes of the slice: x: 4, y: 4, z: 8, core: 2. Of those that a mesh axis runs over, the one named last changes fastest.
Arguments:
- scores: float32 [768, 128], P('doc'), may hold values from -6 to 6
- clicks: int32 [768, 128], P('doc'), may hold values from 0 to 1, as said below
- lengths: int32 [768], P('doc'), may hold values from 2 to 128, as said below
- t_plus_old: float32 [128], replicated, may hold values from 0.1 to 1
- t_minus_old: float32 [128], replicated, may hold values from 0.1 to 1
- leaf: int32 [98304], P('doc'), may hold values from 0 to 31
- bins: int32 [512, 98304], P('feat', 'doc'), may hold values from 0 to 255
Outputs:
- t_plus: float32 [128], replicated
- t_minus: float32 [128], replicated
- gradients: float32 [2, 98304], P(None, 'doc')
- hist: float32 [512, 64, 256], P(('feat', 'doc'))
The draws below stay inside these ranges and needn't reach their ends.
Inputs may be any that keep to these rules, and one draw needn't show every extreme that they name: Query q shows its first lengths[q] slots; the first two queries of each block of 12 queries show all 128. `clicks`: values at or beyond a query's length carry no meaning. In the first query of each block of 12 queries the even positions are clicked and the odd ones not; in the second the reverse.
All inputs are finite; a program needn't handle non-finite values.
Results may differ from the reference program's by a relative error of at most 0.0024.
Values may be sent and summed in bfloat16 or wider, within the bound.
No kernel may reach another device: no remote copies, remote signals or barrier semaphores. Data moves between devices by JAX's collectives and lax.ppermute only.
A program may use at most 64 MiB of HBM per device.

```python
import math
import jax
import jax.numpy as jnp
from jax import lax

POS = 128
F = 512
BINS = 256
LEAVES = 32
Q_DEV = 12
QUERIES = 768
DOCS = 98304


def shared_layout(key):
    key_size = jax.random.fold_in(key, 11)
    key_click = jax.random.fold_in(key, 12)
    query_index = jnp.arange(QUERIES, dtype=jnp.int32)
    inside = query_index % Q_DEV
    drawn_count = jax.random.randint(key_size, (QUERIES,), 2, POS + 1, dtype=jnp.int32)
    drawn_count = jnp.where(inside < 2, POS, drawn_count).astype(jnp.int32)
    places = jnp.arange(POS, dtype=jnp.int32)
    whole = QUERIES * POS
    reach = whole - jnp.minimum(whole, 2 * places[None, :] * query_index[:, None])
    permille = 50 + 350 * reach // whole
    draws = jax.random.randint(key_click, (QUERIES, POS), 0, 1000, dtype=jnp.int32)
    labels = jnp.where(draws < permille, 1, 0)
    even_mark = jnp.where(places % 2 == 0, 1, 0)
    labels = jnp.where((inside == 0)[:, None], even_mark[None, :], labels)
    labels = jnp.where((inside == 1)[:, None], 1 - even_mark[None, :], labels)
    return (drawn_count, labels.astype(jnp.int32))


def draw_lengths(key, part):
    return shared_layout(key)[0]


def draw_clicks(key, part):
    return shared_layout(key)[1]


def touch_ends(values, own_key, least, top_value):
    extent = values.shape
    spot = [jax.random.randint(jax.random.fold_in(own_key, axis), (), 0, extent[axis]) for axis in range(len(extent))]
    values = values.at[tuple(spot)].set(least)
    longest = extent.index(max(extent))
    spot[longest] = (spot[longest] + 1) % extent[longest]
    return values.at[tuple(spot)].set(top_value)


def steps_of(key, dims, pieces, low, largest):
    gain, own = 1.0, jax.random.fold_in(key, 6)
    for axis_at, shards_of in pieces:
        heights = jnp.exp(jax.random.uniform(jax.random.fold_in(own, axis_at), (shards_of,), jnp.float32, low / len(pieces), largest / len(pieces)))
        gain = gain * jnp.repeat(heights, dims[axis_at] // shards_of).reshape([-1 if axis == axis_at else 1 for axis in range(len(dims))])
    return gain


def centred(rng, shape, width, most, pieces=(), kind=jnp.bfloat16):
    array = jax.random.normal(rng, shape, jnp.float32) * width
    if len(pieces) > 0:
        array = steps_of(rng, shape, pieces, -0.22, 0.18) * array
    return jnp.clip(array, min=-most, max=most).astype(kind)


def setup_inputs(seed: int = 0) -> dict:
    seeds = jax.random.split(jax.random.key(seed), 8)
    return {
        "scores": centred(seeds[0], (QUERIES, POS), 1.0, 6.0, ((0, 64),), jnp.float32),
        "clicks": draw_clicks(jax.random.fold_in(seeds[7], 71), 0),
        "lengths": draw_lengths(jax.random.fold_in(seeds[7], 71), 0),
        "t_plus_old": jnp.clip(jnp.exp(jax.random.uniform(seeds[3], (POS,), jnp.float32, math.log(0.1), math.log(1.0))), 0.1, 1.0),
        "t_minus_old": jnp.clip(jnp.exp(jax.random.uniform(seeds[4], (POS,), jnp.float32, math.log(0.1), math.log(1.0))), 0.1, 1.0),
        "leaf": touch_ends(jax.random.randint(seeds[5], (DOCS,), 0, LEAVES), jax.random.fold_in(seeds[5], 1), 0, LEAVES - 1).astype(jnp.int32),
        "bins": touch_ends(jax.random.randint(seeds[6], (F, DOCS), 0, BINS), jax.random.fold_in(seeds[6], 1), 0, BINS - 1).astype(jnp.int32),
    }


def pair_terms(scores, clicks, lengths, t_plus_old, t_minus_old):
    npos = scores.shape[1]
    places = jnp.arange(npos)
    shown_mask = places[None, :] < lengths[:, None]
    clicked = jnp.where((clicks == 1) & shown_mask, 1.0, 0.0).astype(jnp.float32)
    skipped = jnp.where((clicks == 0) & shown_mask, 1.0, 0.0).astype(jnp.float32)
    paired = clicked[:, :, None] * skipped[:, None, :]
    discount = 1.0 / jnp.log2(2.0 + places.astype(jnp.float32))
    clicks_count = lax.optimization_barrier(jnp.sum(clicked, axis=1))
    ideal_gain = lax.optimization_barrier(jnp.sum(jnp.where(places[None, :].astype(jnp.float32) < clicks_count[:, None], discount[None, :], 0.0), axis=1))
    ideal_gain = jnp.maximum(ideal_gain, 1.0)
    change = paired * jnp.abs(discount[:, None] - discount[None, :])[None] / ideal_gain[:, None, None]
    spread = scores[:, :, None] - scores[:, None, :]
    weighted = change * jax.nn.softplus(-spread)
    plus_part = lax.optimization_barrier(jnp.sum(weighted / t_minus_old[None, None, :], axis=(0, 2)))
    minus_part = lax.optimization_barrier(jnp.sum(weighted / t_plus_old[None, :, None], axis=(0, 1)))
    return (change, spread, plus_part, minus_part)

def lambda_terms(change, spread, t_plus, t_minus):
    scaled = change / (t_plus[None, :, None] * t_minus[None, None, :])
    chance = jax.nn.sigmoid(-spread)
    lambda_pair = scaled * chance
    second = lambda_pair * (1.0 - chance)
    slopes = lax.optimization_barrier(jnp.sum(lambda_pair, axis=1)) - lax.optimization_barrier(jnp.sum(lambda_pair, axis=2))
    curvature = lax.optimization_barrier(jnp.sum(second, axis=1)) + lax.optimization_barrier(jnp.sum(second, axis=2))
    return (slopes, curvature)

def reference(scores, clicks, lengths, t_plus_old, t_minus_old, leaf, bins):
    change, spread, plus_sum, minus_sum = pair_terms(scores, clicks, lengths, t_plus_old, t_minus_old)
    t_plus = jnp.sqrt(plus_sum / plus_sum[0])
    t_minus = jnp.sqrt(minus_sum / minus_sum[0])
    slopes, curvature = lambda_terms(change, spread, t_plus, t_minus)
    gradients = jnp.stack([slopes.reshape(-1), curvature.reshape(-1)])
    rounded = lax.optimization_barrier(gradients.astype(jnp.bfloat16)).astype(jnp.float32)
    values = jnp.transpose(rounded)

    def one_feature(column):
        segment_ids = leaf * BINS + column
        summed = jax.ops.segment_sum(values, segment_ids, num_segments=LEAVES * BINS)
        summed = summed.reshape(LEAVES, BINS, 2)
        return jnp.transpose(summed, (2, 0, 1)).reshape(2 * LEAVES, BINS)
    hist = lax.map(one_feature, bins)
    return (t_plus, t_minus, gradients, hist)
```

```python
import jax
import jax.numpy as jnp
from jax import lax
from jax.experimental import pallas as pl
from jax.experimental.pallas import tpu as pltpu
from jax.sharding import PartitionSpec as P

BINS = 256
LEAVES = 32
POS = 128


def pair_terms(scores, clicks, lengths, t_plus_old, t_minus_old):
    npos = scores.shape[1]
    places = jnp.arange(npos)
    shown_mask = places[None, :] < lengths[:, None]
    clicked = jnp.where((clicks == 1) & shown_mask, 1.0, 0.0).astype(jnp.float32)
    skipped = jnp.where((clicks == 0) & shown_mask, 1.0, 0.0).astype(jnp.float32)
    paired = clicked[:, :, None] * skipped[:, None, :]
    discount = 1.0 / jnp.log2(2.0 + places.astype(jnp.float32))
    clicks_count = jnp.sum(clicked, axis=1)
    ideal_gain = jnp.sum(
        jnp.where(
            places[None, :].astype(jnp.float32) < clicks_count[:, None], discount[None, :], 0.0
        ),
        axis=1,
    )
    ideal_gain = jnp.maximum(ideal_gain, 1.0)
    change = (
        paired * jnp.abs(discount[:, None] - discount[None, :])[None] / ideal_gain[:, None, None]
    )
    spread = scores[:, :, None] - scores[:, None, :]
    weighted = change * jax.nn.softplus(-spread)
    plus_part = jnp.sum(weighted / t_minus_old[None, None, :], axis=(0, 2))
    minus_part = jnp.sum(weighted / t_plus_old[None, :, None], axis=(0, 1))
    return (change, spread, plus_part, minus_part)


def lambda_rows(change, spread, plus_sum, minus_sum):
    t_plus = jnp.sqrt(plus_sum / plus_sum[0])
    t_minus = jnp.sqrt(minus_sum / minus_sum[0])
    scaled = change / (t_plus[None, :, None] * t_minus[None, None, :])
    chance = jax.nn.sigmoid(-spread)
    lambda_pair = scaled * chance
    second = lambda_pair * (1.0 - chance)
    slopes = jnp.sum(lambda_pair, axis=1) - jnp.sum(lambda_pair, axis=2)
    curvature = jnp.sum(second, axis=1) + jnp.sum(second, axis=2)
    own_rows = jnp.stack([slopes.reshape(-1), curvature.reshape(-1)])
    return (t_plus, t_minus, own_rows)


def hist_kernel(data_ref, grad_ref, out_ref):
    blocks, rows, width = data_ref.shape
    owned = rows - 1
    out_ref[...] = jnp.zeros_like(out_ref)
    leaves = lax.broadcasted_iota(jnp.int32, (LEAVES, width), 0).astype(jnp.bfloat16)
    levels = lax.broadcasted_iota(jnp.int32, (BINS, width), 0).astype(jnp.bfloat16)

    def one_block(block, carry):
        rows_here = data_ref[block]
        grads = grad_ref[block]
        hit = rows_here[owned : owned + 1] == leaves
        zero = jnp.zeros((), jnp.bfloat16)
        one = jnp.ones((), jnp.bfloat16)
        weights = jnp.concatenate(
            [jnp.where(hit, grads[0:1], zero), jnp.where(hit, grads[1:2], zero)], axis=0
        )
        for feature in range(owned):
            one_hot = jnp.where(rows_here[feature : feature + 1] == levels, one, zero)
            out_ref[feature] += lax.dot_general(
                weights, one_hot, (((1,), (1,)), ((), ())), preferred_element_type=jnp.float32
            )
        return carry

    lax.fori_loop(0, blocks, one_block, 0)


def owned_hist(data, grads):
    owned = data.shape[1] - 1
    vmem = pl.BlockSpec(memory_space=pltpu.VMEM)
    return pl.pallas_call(
        hist_kernel,
        out_shape=jax.ShapeDtypeStruct((owned, 2 * LEAVES, BINS), jnp.float32),
        in_specs=[vmem, vmem],
        out_specs=vmem,
        name="hist",
    )(data, grads)


def body(scores, clicks, lengths, t_plus_old, t_minus_old, leaf, bins):
    shards = lax.axis_size("doc")
    width = leaf.shape[0]
    owned = bins.shape[0] // shards
    rows = jnp.concatenate(
        [
            bins.reshape(shards, owned, width),
            jnp.broadcast_to(leaf[None, None, :], (shards, 1, width)),
        ],
        axis=1,
    ).astype(jnp.bfloat16)
    data = lax.all_to_all(rows, "doc", 0, 0, tiled=True)
    change, spread, plus_part, minus_part = pair_terms(
        scores, clicks, lengths, t_plus_old, t_minus_old
    )
    parts = jnp.concatenate([plus_part, minus_part])
    parts = lax.all_to_all(
        jnp.broadcast_to(parts[None], (shards,) + parts.shape), "doc", 0, 0, tiled=True
    )
    sums = jnp.sum(parts, axis=0)
    t_plus, t_minus, gradients = lambda_rows(change, spread, sums[:POS], sums[POS:])
    rounded = gradients.astype(jnp.bfloat16)
    grads = lax.all_to_all(
        jnp.broadcast_to(rounded[None], (shards,) + rounded.shape), "doc", 0, 0, tiled=True
    )
    hist = owned_hist(data, grads)
    return (t_plus, t_minus, gradients, hist)


def solution(mesh):
    placed = (P("doc", None), P("doc", None), P("doc"), P(), P(), P("doc"), P("feat", "doc"))
    return jax.shard_map(
        body,
        mesh=mesh,
        in_specs=placed,
        out_specs=(P(), P(), P(None, "doc"), P(("feat", "doc"), None, None)),
        check_vma=False,
    )
```

```python
import jax
import jax.numpy as jnp
from jax import lax
from jax.experimental import pallas as pl
from jax.experimental.pallas import tpu as pltpu
from jax.sharding import PartitionSpec as P

BINS = 256
LEAVES = 32
POS = 128
HALF = BINS // 2
PER = 4


def pair_terms(scores, clicks, lengths, t_plus_old, t_minus_old):
    npos = scores.shape[1]
    places = jnp.arange(npos)
    shown_mask = places[None, :] < lengths[:, None]
    clicked = jnp.where((clicks == 1) & shown_mask, 1.0, 0.0).astype(jnp.float32)
    skipped = jnp.where((clicks == 0) & shown_mask, 1.0, 0.0).astype(jnp.float32)
    paired = clicked[:, :, None] * skipped[:, None, :]
    discount = 1.0 / jnp.log2(2.0 + places.astype(jnp.float32))
    clicks_count = jnp.sum(clicked, axis=1)
    ideal_gain = jnp.sum(
        jnp.where(
            places[None, :].astype(jnp.float32) < clicks_count[:, None], discount[None, :], 0.0
        ),
        axis=1,
    )
    ideal_gain = jnp.maximum(ideal_gain, 1.0)
    change = (
        paired * jnp.abs(discount[:, None] - discount[None, :])[None] / ideal_gain[:, None, None]
    )
    spread = scores[:, :, None] - scores[:, None, :]
    weighted = change * jax.nn.softplus(-spread)
    plus_part = jnp.sum(weighted / t_minus_old[None, None, :], axis=(0, 2))
    minus_part = jnp.sum(weighted / t_plus_old[None, :, None], axis=(0, 1))
    return (change, spread, plus_part, minus_part)


def lambda_rows(change, spread, plus_sum, minus_sum):
    t_plus = jnp.sqrt(plus_sum / plus_sum[0])
    t_minus = jnp.sqrt(minus_sum / minus_sum[0])
    scaled = change / (t_plus[None, :, None] * t_minus[None, None, :])
    chance = jax.nn.sigmoid(-spread)
    lambda_pair = scaled * chance
    second = lambda_pair * (1.0 - chance)
    slopes = jnp.sum(lambda_pair, axis=1) - jnp.sum(lambda_pair, axis=2)
    curvature = jnp.sum(second, axis=1) + jnp.sum(second, axis=2)
    own_rows = jnp.stack([slopes.reshape(-1), curvature.reshape(-1)])
    return (t_plus, t_minus, own_rows)


def accumulate(core, data_ref, side_ref, acc):
    blocks, _, wide = side_ref.shape
    width = wide * 2 // 3
    rows_a = lax.broadcasted_iota(jnp.int32, (2 * LEAVES, width), 0).astype(jnp.bfloat16)
    rows_b = lax.broadcasted_iota(jnp.int32, (HALF, width), 0).astype(jnp.bfloat16)
    zero = jnp.zeros((), jnp.bfloat16)
    one = jnp.ones((), jnp.bfloat16)

    def some_blocks(step, carry):
        left = [[], []]
        right = [[], []]
        for at in range(PER):
            block = step * PER + at
            side = side_ref[block]
            bins = data_ref[2 * block + core][:, :width]
            leaf = jnp.concatenate([side[0:1, width:], side[1:2, width:]], axis=1)
            for feature in range(2):
                row = bins[feature : feature + 1]
                high = row >= jnp.asarray(HALF, jnp.bfloat16)
                hit = jnp.where(high, leaf + jnp.asarray(LEAVES, jnp.bfloat16), leaf) == rows_a
                low = jnp.where(high, row - jnp.asarray(HALF, jnp.bfloat16), row)
                left[feature].append(
                    jnp.concatenate(
                        [
                            jnp.where(hit, side[0:1, :width], zero),
                            jnp.where(hit, side[1:2, :width], zero),
                        ],
                        axis=0,
                    )
                )
                right[feature].append(jnp.where(low == rows_b, one, zero))
        for feature in range(2):
            acc[feature] += lax.dot_general(
                jnp.concatenate(left[feature], axis=1),
                jnp.concatenate(right[feature], axis=1),
                (((1,), (1,)), ((), ())),
                preferred_element_type=jnp.float32,
            )
        return carry

    lax.fori_loop(0, blocks // PER, some_blocks, 0)


def first_kernel(core_ref, data_ref, side_ref, out_ref):
    out_ref[...] = jnp.zeros_like(out_ref)
    accumulate(core_ref[0], data_ref, side_ref, out_ref)


def second_kernel(core_ref, data_ref, side_ref, before_ref, out_ref, acc):
    acc[...] = before_ref[...]
    accumulate(core_ref[0], data_ref, side_ref, acc)
    for feature in range(2):
        for which in range(2):
            for high in range(2):
                out_ref[
                    feature,
                    which * LEAVES : (which + 1) * LEAVES,
                    high * HALF : (high + 1) * HALF,
                ] = acc[feature, (2 * which + high) * LEAVES : (2 * which + high + 1) * LEAVES, :]


def hist_of(core, data, side, before=None):
    vmem = pl.BlockSpec(memory_space=pltpu.VMEM)
    smem = pl.BlockSpec(memory_space=pltpu.SMEM)
    part = (2, 4 * LEAVES, HALF)
    if before is None:
        return pl.pallas_call(
            first_kernel,
            out_shape=jax.ShapeDtypeStruct(part, jnp.float32),
            in_specs=[smem, vmem, vmem],
            out_specs=vmem,
            name="first_half",
        )(core, data, side)
    return pl.pallas_call(
        second_kernel,
        out_shape=jax.ShapeDtypeStruct((2, 2 * LEAVES, BINS), jnp.float32),
        in_specs=[smem, vmem, vmem, vmem],
        out_specs=vmem,
        scratch_shapes=[pltpu.VMEM(part, jnp.float32)],
        name="second_half",
    )(core, data, side, before)


def body(scores, clicks, lengths, t_plus_old, t_minus_old, leaf, bins):
    shards = lax.axis_size("doc")
    width = leaf.shape[0]
    change, spread, plus_part, minus_part = pair_terms(
        scores, clicks, lengths, t_plus_old, t_minus_old
    )
    parts = jnp.concatenate([plus_part, minus_part])
    parts_high = parts.astype(jnp.bfloat16)
    parts_rest = (parts - parts_high.astype(jnp.float32)).astype(jnp.bfloat16)
    parts = jnp.stack([parts_high, parts_rest])
    sent = jnp.concatenate(
        [
            bins.astype(jnp.bfloat16).reshape(shards, 2, width),
            jnp.broadcast_to(parts[None], (shards,) + parts.shape),
        ],
        axis=2,
    )
    data = lax.all_to_all(sent, "doc", 0, 0, tiled=True)
    sums = jnp.sum(data[:, :, width:].astype(jnp.float32), axis=(0, 1))
    t_plus, t_minus, gradients = lambda_rows(change, spread, sums[:POS], sums[POS:])
    side = jnp.concatenate(
        [gradients.astype(jnp.bfloat16), leaf.astype(jnp.bfloat16).reshape(2, width // 2)], axis=1
    )
    same_core = [[2 * chip + core for chip in range(shards // 2)] for core in range(2)]
    side = lax.all_to_all(
        jnp.broadcast_to(side[None], (shards // 2,) + side.shape),
        "doc",
        0,
        0,
        axis_index_groups=same_core,
        tiled=True,
    )
    other_side = lax.ppermute(side, "doc", [(at, at ^ 1) for at in range(shards)])
    core = lax.axis_index("doc") % 2
    partial = hist_of(core.reshape(1), data, side)
    hist = hist_of((1 - core).reshape(1), data, other_side, partial)
    return (t_plus, t_minus, gradients, hist)


def solution(mesh):
    placed = (P("doc", None), P("doc", None), P("doc"), P(), P(), P("doc"), P("feat", "doc"))
    return jax.shard_map(
        body,
        mesh=mesh,
        in_specs=placed,
        out_specs=(P(), P(), P(None, "doc"), P(("feat", "doc"), None, None)),
        check_vma=False,
    )
```

```python
import jax
import jax.numpy as jnp
import numpy as np
from jax import lax
from jax.experimental import pallas as pl
from jax.experimental.pallas import tpu as pltpu
from jax.sharding import PartitionSpec as P

BINS = 256
LEAVES = 32
POS = 128
HALF = BINS // 2
TILE = 256
STEP = 4


def query_rows(scores, clicks, lengths_ref, queries, discount_row):
    lane = lax.broadcasted_iota(jnp.int32, (queries, POS), 1)
    row = lax.broadcasted_iota(jnp.int32, (queries, POS), 0)
    length = jnp.zeros((queries, POS), jnp.int32)
    for query in range(queries):
        length = jnp.where(row == query, lengths_ref[query], length)
    shown = lane < length
    clicked = shown & (clicks == 1)
    skipped = shown & (clicks == 0)
    count = jnp.sum(jnp.where(clicked, 1.0, 0.0), axis=1, keepdims=True)
    ideal = jnp.sum(
        jnp.where(lane.astype(jnp.float32) < count, discount_row, 0.0), axis=1, keepdims=True
    )
    ideal = jnp.maximum(ideal, 1.0)
    side = jnp.where(clicked, 1.0, jnp.where(skipped, -1.0, 0.0))
    return clicked, skipped, side, side * scores, ideal


def turned(rows):
    queries = rows[0].shape[0]
    pad = jnp.zeros((POS - queries * len(rows), POS), jnp.float32)
    return jnp.transpose(jnp.concatenate(list(rows) + [pad], axis=0))


def pair_kernel(gap_ref, discount_ref, scores_ref, clicks_ref, lengths_ref, plus_ref, minus_ref, bins_ref, parts_ref,
                bins_out_ref, packed):
    queries = scores_ref.shape[0]
    discount_row = discount_ref[...]
    clicked, skipped, side, signed, ideal = query_rows(
        scores_ref[...], clicks_ref[...], lengths_ref, queries, discount_row
    )
    weight = jnp.where(clicked, 1.0 / plus_ref[...], jnp.where(skipped, -1.0 / minus_ref[...], 0.0))
    columns = turned([signed, weight])
    scale = 1.0 / ideal
    plus = jnp.zeros((1, POS), jnp.float32)
    minus = jnp.zeros((1, POS), jnp.float32)
    for query in range(queries):
        other = columns[:, query : query + 1]
        strength = columns[:, queries + query : queries + query + 1]
        spread = other + signed[query : query + 1]
        cross = jnp.maximum(strength * -side[query : query + 1], 0.0)
        loss = jnp.maximum(-spread, 0.0) + jnp.log1p(jnp.exp(-jnp.abs(spread)))
        total = jnp.sum(cross * gap_ref[...] * loss, axis=0, keepdims=True)
        total = total * scale[query : query + 1]
        plus += jnp.where(side[query : query + 1] > 0.0, total, 0.0)
        minus += jnp.where(side[query : query + 1] < 0.0, total, 0.0)
    parts_ref[0:1] = plus
    parts_ref[1:2] = minus

    features, slots = bins_ref.shape
    packed[...] = jnp.full(packed.shape, -1.0, jnp.float32)
    lane = lax.broadcasted_iota(jnp.int32, (1, POS), 1)
    start = jnp.int32(0)
    for query in range(queries):
        group = start // POS
        shift = start - group * POS
        length = lengths_ref[query]
        moved = pltpu.roll(
            bins_ref[:, query * POS : (query + 1) * POS].astype(jnp.float32), shift, 1
        )
        here = (lane >= shift) & (lane < shift + length)
        there = lane < shift + length - POS
        packed[group] = jnp.where(here, moved, packed[group])
        packed[group + 1] = jnp.where(there, moved, packed[group + 1])
        start += length
    for group in range(slots // POS):
        bins_out_ref[:, group * POS : (group + 1) * POS] = packed[group].astype(jnp.bfloat16)


def lambda_kernel(gap_ref, discount_ref, scores_ref, clicks_ref, lengths_ref, leaf_ref, sums_ref, plus_ref, minus_ref,
                  grad_ref, side_ref, packed, flat):
    queries = scores_ref.shape[0]
    discount_row = discount_ref[...]
    plus_sum = sums_ref[:, :POS]
    minus_sum = sums_ref[:, POS:]
    plus = jnp.sqrt(plus_sum / plus_sum[:, 0:1])
    minus = jnp.sqrt(minus_sum / minus_sum[:, 0:1])
    plus_ref[...] = plus
    minus_ref[...] = minus
    clicked, skipped, side, signed, ideal = query_rows(
        scores_ref[...], clicks_ref[...], lengths_ref, queries, discount_row
    )
    weight = jnp.where(clicked, 1.0 / plus, jnp.where(skipped, -1.0 / minus, 0.0))
    columns = turned([signed, weight])
    outer = jnp.abs(weight) / ideal
    packed[...] = jnp.zeros_like(packed)
    lane = lax.broadcasted_iota(jnp.int32, (1, POS), 1)
    start = jnp.int32(0)
    for query in range(queries):
        other = columns[:, query : query + 1]
        strength = columns[:, queries + query : queries + query + 1]
        spread = other + signed[query : query + 1]
        cross = jnp.maximum(strength * -side[query : query + 1], 0.0)
        grown = jnp.exp(spread)
        chance = 1.0 / (1.0 + grown)
        first = cross * gap_ref[...] * chance
        second = first * (grown * chance)
        slope = jnp.sum(first, axis=0, keepdims=True) * outer[query : query + 1]
        slope = slope * -side[query : query + 1]
        curve = jnp.sum(second, axis=0, keepdims=True) * outer[query : query + 1]
        grad_ref[0:1, query * POS : (query + 1) * POS] = slope
        grad_ref[1:2, query * POS : (query + 1) * POS] = curve
        group = start // POS
        shift = start - group * POS
        length = lengths_ref[query]
        rows = jnp.concatenate(
            [slope, curve, leaf_ref[query : query + 1].astype(jnp.float32),
             jnp.zeros((5, POS), jnp.float32)], axis=0
        )
        moved = pltpu.roll(rows, shift, 1)
        here = (lane >= shift) & (lane < shift + length)
        there = lane < shift + length - POS
        packed[group] = jnp.where(here, moved, packed[group])
        packed[group + 1] = jnp.where(there, moved, packed[group + 1])
        start += length
    for tile in range(queries * POS // TILE):
        at = 3 * POS * tile
        for half in range(2):
            rows = packed[2 * tile + half]
            flat[:, at + half * POS : at + (half + 1) * POS] = rows[0:2]
            flat[half : half + 1, at + 2 * POS : at + 3 * POS] = rows[2:3]
    side_ref[...] = flat[...].astype(jnp.bfloat16)


def plan_kernel(filled_ref, list_ref, total_ref):
    chips = filled_ref.shape[0] // 2
    tiles = (list_ref.shape[0] // 2 - STEP) // chips
    for core in range(2):
        base = core * (chips * tiles + STEP)

        def one_block(chip, carry):
            at, spare = carry
            used = filled_ref[2 * chip + core]
            for tile in range(tiles):
                list_ref[base + at] = chip * 8 + tile
                at = at + jnp.where(tile < used, 1, 0)
            return at, jnp.where(used < tiles, chip * 8 + tiles - 1, spare)

        at, spare = lax.fori_loop(0, chips, one_block, (jnp.int32(0), jnp.int32(0)))
        for extra in range(STEP):
            list_ref[base + at + extra] = spare
        total_ref[core] = (at + STEP - 1) // STEP


def accumulate(core, list_ref, total_ref, data_ref, side_ref, acc):
    base = core * (list_ref.shape[0] // 2)
    rows_a = lax.broadcasted_iota(jnp.int32, (2 * LEAVES, TILE), 0).astype(jnp.bfloat16)
    rows_b = lax.broadcasted_iota(jnp.int32, (HALF, TILE), 0).astype(jnp.bfloat16)
    zero = jnp.zeros((), jnp.bfloat16)
    one = jnp.ones((), jnp.bfloat16)

    def some_tiles(step, carry):
        left = [[], []]
        right = [[], []]
        for at in range(STEP):
            entry = list_ref[base + step * STEP + at]
            chip = entry // 8
            tile = entry - chip * 8
            bins = data_ref[2 * chip + core, :, pl.ds(pl.multiple_of(tile * TILE, TILE), TILE)]
            side = side_ref[chip, :, pl.ds(pl.multiple_of(tile * 3 * POS, POS), 3 * POS)]
            leaf = jnp.concatenate([side[0:1, TILE:], side[1:2, TILE:]], axis=1)
            for feature in range(2):
                row = bins[feature : feature + 1]
                high = row >= jnp.asarray(HALF, jnp.bfloat16)
                hit = jnp.where(high, leaf + jnp.asarray(LEAVES, jnp.bfloat16), leaf) == rows_a
                low = jnp.where(high, row - jnp.asarray(HALF, jnp.bfloat16), row)
                left[feature].append(
                    jnp.concatenate(
                        [
                            jnp.where(hit, side[0:1, :TILE], zero),
                            jnp.where(hit, side[1:2, :TILE], zero),
                        ],
                        axis=0,
                    )
                )
                right[feature].append(jnp.where(low == rows_b, one, zero))
        for feature in range(2):
            acc[feature] += lax.dot_general(
                jnp.concatenate(left[feature], axis=1),
                jnp.concatenate(right[feature], axis=1),
                (((1,), (1,)), ((), ())),
                preferred_element_type=jnp.float32,
            )
        return carry

    lax.fori_loop(0, total_ref[core], some_tiles, 0)


def first_kernel(core_ref, list_ref, total_ref, data_ref, side_ref, out_ref):
    out_ref[...] = jnp.zeros_like(out_ref)
    accumulate(core_ref[0], list_ref, total_ref, data_ref, side_ref, out_ref)


def second_kernel(core_ref, list_ref, total_ref, data_ref, side_ref, before_ref, out_ref, acc):
    acc[...] = before_ref[...]
    accumulate(core_ref[0], list_ref, total_ref, data_ref, side_ref, acc)
    for feature in range(2):
        for which in range(2):
            for high in range(2):
                out_ref[
                    feature,
                    which * LEAVES : (which + 1) * LEAVES,
                    high * HALF : (high + 1) * HALF,
                ] = acc[feature, (2 * which + high) * LEAVES : (2 * which + high + 1) * LEAVES, :]


VMEM = pl.BlockSpec(memory_space=pltpu.VMEM)
SMEM = pl.BlockSpec(memory_space=pltpu.SMEM)


def hist_of(core, plan, data, side, before=None):
    part = (2, 4 * LEAVES, HALF)
    if before is None:
        return pl.pallas_call(
            first_kernel,
            out_shape=jax.ShapeDtypeStruct(part, jnp.float32),
            in_specs=[SMEM, SMEM, SMEM, VMEM, VMEM],
            out_specs=VMEM,
            name="first_half",
        )(core, *plan, data, side)
    return pl.pallas_call(
        second_kernel,
        out_shape=jax.ShapeDtypeStruct((2, 2 * LEAVES, BINS), jnp.float32),
        in_specs=[SMEM, SMEM, SMEM, VMEM, VMEM, VMEM],
        out_specs=VMEM,
        scratch_shapes=[pltpu.VMEM(part, jnp.float32)],
        name="second_half",
    )(core, *plan, data, side, before)


def body(scores, clicks, lengths, t_plus_old, t_minus_old, leaf, bins):
    shards = lax.axis_size("doc")
    queries = scores.shape[0]
    slots = leaf.shape[0]
    tiles = slots // TILE
    places = np.arange(POS, dtype=np.float32)
    discount = (1.0 / np.log2(2.0 + places)).astype(np.float32)
    gap = jnp.asarray(np.abs(discount[:, None] - discount[None, :]))
    discount = jnp.asarray(discount[None])
    f32 = jnp.float32
    parts, packed = pl.pallas_call(
        pair_kernel,
        out_shape=(
            jax.ShapeDtypeStruct((2, POS), f32),
            jax.ShapeDtypeStruct(bins.shape, jnp.bfloat16),
        ),
        in_specs=[VMEM, VMEM, VMEM, VMEM, SMEM, VMEM, VMEM, VMEM],
        out_specs=(VMEM, VMEM),
        scratch_shapes=[pltpu.VMEM((slots // POS + 1, bins.shape[0], POS), f32)],
        name="pair_terms",
    )(gap, discount, scores, clicks, lengths, t_plus_old[None], t_minus_old[None], bins)
    parts = parts.reshape(2 * POS)
    parts_high = parts.astype(jnp.bfloat16)
    parts_rest = (parts - parts_high.astype(f32)).astype(jnp.bfloat16)
    parts = jnp.stack([parts_high, parts_rest])
    sent = jnp.concatenate(
        [
            packed.reshape(shards, 2, slots),
            jnp.broadcast_to(parts[None], (shards,) + parts.shape),
        ],
        axis=2,
    )
    data = lax.all_to_all(sent, "doc", 0, 0, tiled=True)
    sums = jnp.sum(data[:, :, slots:].astype(f32), axis=(0, 1))
    t_plus, t_minus, gradients, side = pl.pallas_call(
        lambda_kernel,
        out_shape=(
            jax.ShapeDtypeStruct((1, POS), f32),
            jax.ShapeDtypeStruct((1, POS), f32),
            jax.ShapeDtypeStruct((2, slots), f32),
            jax.ShapeDtypeStruct((2, 3 * slots // 2), jnp.bfloat16),
        ),
        in_specs=[VMEM, VMEM, VMEM, VMEM, SMEM, VMEM, VMEM],
        out_specs=(VMEM,) * 4,
        scratch_shapes=[
            pltpu.VMEM((queries + 1, 8, POS), f32),
            pltpu.VMEM((2, 3 * slots // 2), f32),
        ],
        name="lambdas",
    )(gap, discount, scores, clicks, lengths, leaf.reshape(queries, POS), sums[None])
    same_core = [[2 * chip + core for chip in range(shards // 2)] for core in range(2)]
    side = lax.all_to_all(
        jnp.broadcast_to(side[None], (shards // 2,) + side.shape),
        "doc",
        0,
        0,
        axis_index_groups=same_core,
        tiled=True,
    )
    shown = jnp.sum((data[:, 0, :slots] >= 0).astype(f32), axis=1).astype(jnp.int32)
    plan = pl.pallas_call(
        plan_kernel,
        out_shape=(
            jax.ShapeDtypeStruct((shards * tiles + 2 * STEP,), jnp.int32),
            jax.ShapeDtypeStruct((2,), jnp.int32),
        ),
        in_specs=[SMEM],
        out_specs=(SMEM, SMEM),
        name="plan",
    )((shown + (TILE - 1)) // TILE)
    other_side = lax.ppermute(side, "doc", [(at, at ^ 1) for at in range(shards)])
    core = lax.axis_index("doc") % 2
    partial = hist_of(core.reshape(1), plan, data, side)
    hist = hist_of((1 - core).reshape(1), plan, data, other_side, partial)
    return (t_plus[0], t_minus[0], gradients, hist)


def solution(mesh):
    placed = (P("doc", None), P("doc", None), P("doc"), P(), P(), P("doc"), P("feat", "doc"))
    return jax.shard_map(
        body,
        mesh=mesh,
        in_specs=placed,
        out_specs=(P(), P(), P(None, "doc"), P(("feat", "doc"), None, None)),
        check_vma=False,
    )
```

```python
import jax
import jax.numpy as jnp
import numpy as np
from jax import lax
from jax.experimental import pallas as pl
from jax.experimental.pallas import tpu as pltpu
from jax.sharding import PartitionSpec as P


BINS = 256
LEAVES = 32
POS = 128
HALF = BINS // 2
TILE = 256
STEP = 8


def query_rows(scores, clicks, lengths_ref, queries, discount_row):
    lane = lax.broadcasted_iota(jnp.int32, (queries, POS), 1)
    row = lax.broadcasted_iota(jnp.int32, (queries, POS), 0)
    length = jnp.zeros((queries, POS), jnp.int32)
    for query in range(queries):
        length = jnp.where(row == query, lengths_ref[query], length)
    shown = lane < length
    clicked = shown & (clicks == 1)
    skipped = shown & (clicks == 0)
    count = jnp.sum(jnp.where(clicked, 1.0, 0.0), axis=1, keepdims=True)
    ideal = jnp.sum(
        jnp.where(lane.astype(jnp.float32) < count, discount_row, 0.0), axis=1, keepdims=True
    )
    ideal = jnp.maximum(ideal, 1.0)
    side = jnp.where(clicked, 1.0, jnp.where(skipped, -1.0, 0.0))
    return clicked, skipped, side, side * scores, ideal


def turned(rows):
    queries = rows[0].shape[0]
    pad = jnp.zeros((POS - queries * len(rows), POS), jnp.float32)
    return jnp.transpose(jnp.concatenate(list(rows) + [pad], axis=0))


def pair_kernel(gap_ref, discount_ref, scores_ref, clicks_ref, lengths_ref, plus_ref, minus_ref, bins_ref,
                sent_ref, packed):
    queries = scores_ref.shape[0]
    discount_row = discount_ref[...]
    clicked, skipped, side, signed, ideal = query_rows(
        scores_ref[...], clicks_ref[...], lengths_ref, queries, discount_row
    )
    weight = jnp.where(clicked, 1.0 / plus_ref[...], jnp.where(skipped, -1.0 / minus_ref[...], 0.0))
    columns = turned([signed, weight])
    scale = 1.0 / ideal
    plus = jnp.zeros((1, POS), jnp.float32)
    minus = jnp.zeros((1, POS), jnp.float32)
    for query in range(queries):
        other = columns[:, query : query + 1]
        strength = columns[:, queries + query : queries + query + 1]
        spread = other + signed[query : query + 1]
        cross = jnp.maximum(strength * -side[query : query + 1], 0.0)
        loss = jnp.maximum(-spread, 0.0) + jnp.log1p(jnp.exp(-jnp.abs(spread)))
        total = jnp.sum(cross * gap_ref[...] * loss, axis=0, keepdims=True)
        total = total * scale[query : query + 1]
        plus += jnp.where(side[query : query + 1] > 0.0, total, 0.0)
        minus += jnp.where(side[query : query + 1] < 0.0, total, 0.0)
    features, slots = bins_ref.shape
    for at, part in enumerate((plus, minus)):
        high = part.astype(jnp.bfloat16).astype(jnp.float32)
        pieces = jnp.concatenate([high, part - high], axis=0).astype(jnp.bfloat16)
        sent_ref[:, :, slots + at * POS : slots + (at + 1) * POS] = jnp.broadcast_to(
            pieces[None], (features // 2, 2, POS)
        )
    packed[...] = jnp.full(packed.shape, -1.0, jnp.float32)
    lane = lax.broadcasted_iota(jnp.int32, (1, POS), 1)
    start = jnp.int32(0)
    for query in range(queries):
        group = start // POS
        shift = start - group * POS
        length = lengths_ref[query]
        moved = pltpu.roll(
            bins_ref[:, query * POS : (query + 1) * POS].astype(jnp.float32), shift, 1
        )
        here = (lane >= shift) & (lane < shift + length)
        there = lane < shift + length - POS
        packed[group] = jnp.where(here, moved, packed[group])
        packed[group + 1] = jnp.where(there, moved, packed[group + 1])
        start += length
    for group in range(slots // POS):
        for owner in range(features // 2):
            sent_ref[owner, :, group * POS : (group + 1) * POS] = packed[
                group, 2 * owner : 2 * owner + 2
            ].astype(jnp.bfloat16)


def lambda_kernel(gap_ref, discount_ref, scores_ref, clicks_ref, lengths_ref, leaf_ref, sums_ref, plus_ref, minus_ref,
                  grad_ref, side_ref, packed, flat):
    queries = scores_ref.shape[0]
    discount_row = discount_ref[...]
    plus_sum = sums_ref[:, :POS]
    minus_sum = sums_ref[:, POS:]
    plus = jnp.sqrt(plus_sum / plus_sum[:, 0:1])
    minus = jnp.sqrt(minus_sum / minus_sum[:, 0:1])
    plus_ref[...] = plus
    minus_ref[...] = minus
    clicked, skipped, side, signed, ideal = query_rows(
        scores_ref[...], clicks_ref[...], lengths_ref, queries, discount_row
    )
    weight = jnp.where(clicked, 1.0 / plus, jnp.where(skipped, -1.0 / minus, 0.0))
    columns = turned([signed, weight])
    outer = jnp.abs(weight) / ideal
    packed[...] = jnp.zeros_like(packed)
    lane = lax.broadcasted_iota(jnp.int32, (1, POS), 1)
    start = jnp.int32(0)
    for query in range(queries):
        other = columns[:, query : query + 1]
        strength = columns[:, queries + query : queries + query + 1]
        spread = other + signed[query : query + 1]
        cross = jnp.maximum(strength * -side[query : query + 1], 0.0)
        grown = jnp.exp(spread)
        chance = 1.0 / (1.0 + grown)
        first = cross * gap_ref[...] * chance
        second = first * (grown * chance)
        slope = jnp.sum(first, axis=0, keepdims=True) * outer[query : query + 1]
        slope = slope * -side[query : query + 1]
        curve = jnp.sum(second, axis=0, keepdims=True) * outer[query : query + 1]
        grad_ref[0:1, query * POS : (query + 1) * POS] = slope
        grad_ref[1:2, query * POS : (query + 1) * POS] = curve
        group = start // POS
        shift = start - group * POS
        length = lengths_ref[query]
        rows = jnp.concatenate(
            [slope, curve, leaf_ref[query : query + 1].astype(jnp.float32),
             jnp.zeros((5, POS), jnp.float32)], axis=0
        )
        moved = pltpu.roll(rows, shift, 1)
        here = (lane >= shift) & (lane < shift + length)
        there = lane < shift + length - POS
        packed[group] = jnp.where(here, moved, packed[group])
        packed[group + 1] = jnp.where(there, moved, packed[group + 1])
        start += length
    for tile in range(queries * POS // TILE):
        at = 3 * POS * tile
        for half in range(2):
            rows = packed[2 * tile + half]
            flat[:, at + half * POS : at + (half + 1) * POS] = rows[0:2]
            flat[half : half + 1, at + 2 * POS : at + 3 * POS] = rows[2:3]
    side_ref[...] = jnp.broadcast_to(flat[...].astype(jnp.bfloat16)[None], side_ref.shape)


def plan_kernel(filled_ref, list_ref, total_ref):
    chips = filled_ref.shape[0] // 2
    tiles = (list_ref.shape[0] // 2 - STEP) // chips
    for core in range(2):
        base = core * (chips * tiles + STEP)

        def one_block(chip, carry):
            at, spare = carry
            used = filled_ref[2 * chip + core]
            for tile in range(tiles):
                list_ref[base + at] = chip * 8 + tile
                at = at + jnp.where(tile < used, 1, 0)
            return at, jnp.where(used < tiles, chip * 8 + tiles - 1, spare)

        at, spare = lax.fori_loop(0, chips, one_block, (jnp.int32(0), jnp.int32(0)))
        for extra in range(STEP):
            list_ref[base + at + extra] = spare
        total_ref[core] = (at + STEP - 1) // STEP


def accumulate(core, list_ref, total_ref, data_ref, side_ref, accs):
    base = core * (list_ref.shape[0] // 2)
    rows_a = lax.broadcasted_iota(jnp.int32, (2 * LEAVES, TILE), 0).astype(jnp.bfloat16)
    rows_b = lax.broadcasted_iota(jnp.int32, (HALF, TILE), 0).astype(jnp.bfloat16)
    zero = jnp.zeros((), jnp.bfloat16)
    one = jnp.ones((), jnp.bfloat16)

    def some_tiles(step, carry):
        for at in range(STEP):
            entry = list_ref[base + step * STEP + at]
            chip = lax.shift_right_logical(entry, 3)
            tile = lax.bitwise_and(entry, 7)
            bins = data_ref[2 * chip + core, :, pl.ds(pl.multiple_of(tile * TILE, TILE), TILE)]
            side = side_ref[chip, :, pl.ds(pl.multiple_of(tile * 3 * POS, POS), 3 * POS)]
            leaf = jnp.concatenate([side[0:1, TILE:], side[1:2, TILE:]], axis=1)
            left = []
            right = []
            for feature in range(2):
                row = bins[feature : feature + 1]
                high = row >= jnp.asarray(HALF, jnp.bfloat16)
                hit = jnp.where(high, leaf + jnp.asarray(LEAVES, jnp.bfloat16), leaf) == rows_a
                low = jnp.where(high, row - jnp.asarray(HALF, jnp.bfloat16), row)
                left.append(jnp.where(hit, side[0:1, :TILE], zero))
                left.append(jnp.where(hit, side[1:2, :TILE], zero))
                right.append(jnp.where(low == rows_b, one, zero))
            unit = at % 2
            register = (at // 2) % 2
            pltpu.matmul_push_rhs(jnp.concatenate(right, axis=0), register, unit, transpose=True)
            pltpu.matmul_acc_lhs(accs[unit], jnp.concatenate(left, axis=0), register)
        return carry

    lax.fori_loop(0, total_ref[core], some_tiles, 0)


def summed(core, list_ref, total_ref, data_ref, side_ref, finish):
    def run(acc_a, acc_b):
        accumulate(core, list_ref, total_ref, data_ref, side_ref, (acc_a, acc_b))
        finish(pltpu.matmul_pop(acc_a) + pltpu.matmul_pop(acc_b))

    shape = (8 * LEAVES, BINS)
    pl.run_scoped(run, pltpu.ACC(0)(shape, jnp.float32), pltpu.ACC(1)(shape, jnp.float32))


def first_kernel(core_ref, list_ref, total_ref, data_ref, side_ref, out_ref):
    rows = 4 * LEAVES

    def finish(total):
        for feature in range(2):
            out_ref[feature] = total[
                feature * rows : (feature + 1) * rows, feature * HALF : (feature + 1) * HALF
            ]

    summed(core_ref[0], list_ref, total_ref, data_ref, side_ref, finish)


def second_kernel(core_ref, list_ref, total_ref, data_ref, side_ref, before_ref, out_ref):
    rows = 4 * LEAVES

    def finish(total):
        for feature in range(2):
            mine = total[
                feature * rows : (feature + 1) * rows, feature * HALF : (feature + 1) * HALF
            ] + before_ref[feature]
            for which in range(2):
                for high in range(2):
                    at = (2 * which + high) * LEAVES
                    out_ref[
                        feature,
                        which * LEAVES : (which + 1) * LEAVES,
                        high * HALF : (high + 1) * HALF,
                    ] = mine[at : at + LEAVES]

    summed(core_ref[0], list_ref, total_ref, data_ref, side_ref, finish)


VMEM = pl.BlockSpec(memory_space=pltpu.VMEM)
SMEM = pl.BlockSpec(memory_space=pltpu.SMEM)


def hist_of(core, plan, data, side, before=None):
    part = (2, 4 * LEAVES, HALF)
    if before is None:
        return pl.pallas_call(
            first_kernel,
            out_shape=jax.ShapeDtypeStruct(part, jnp.float32),
            in_specs=[SMEM, SMEM, SMEM, VMEM, VMEM],
            out_specs=VMEM,
            name="first_half",
        )(core, *plan, data, side)
    return pl.pallas_call(
        second_kernel,
        out_shape=jax.ShapeDtypeStruct((2, 2 * LEAVES, BINS), jnp.float32),
        in_specs=[SMEM, SMEM, SMEM, VMEM, VMEM, VMEM],
        out_specs=VMEM,
        name="second_half",
    )(core, *plan, data, side, before)


def body(scores, clicks, lengths, t_plus_old, t_minus_old, leaf, bins):
    shards = lax.axis_size("doc")
    queries = scores.shape[0]
    slots = leaf.shape[0]
    tiles = slots // TILE
    places = np.arange(POS, dtype=np.float32)
    discount = (1.0 / np.log2(2.0 + places)).astype(np.float32)
    gap = jnp.asarray(np.abs(discount[:, None] - discount[None, :]))
    discount = jnp.asarray(discount[None])
    f32 = jnp.float32
    sent = pl.pallas_call(
        pair_kernel,
        out_shape=jax.ShapeDtypeStruct((shards, 2, slots + 2 * POS), jnp.bfloat16),
        in_specs=[VMEM, VMEM, VMEM, VMEM, SMEM, VMEM, VMEM, VMEM],
        out_specs=VMEM,
        scratch_shapes=[pltpu.VMEM((slots // POS + 1, bins.shape[0], POS), f32)],
        name="pair_terms",
    )(gap, discount, scores, clicks, lengths, t_plus_old[None], t_minus_old[None], bins)
    data = lax.all_to_all(sent, "doc", 0, 0, tiled=True)
    sums = jnp.sum(data[:, :, slots:].astype(f32), axis=(0, 1))
    t_plus, t_minus, gradients, side = pl.pallas_call(
        lambda_kernel,
        out_shape=(
            jax.ShapeDtypeStruct((1, POS), f32),
            jax.ShapeDtypeStruct((1, POS), f32),
            jax.ShapeDtypeStruct((2, slots), f32),
            jax.ShapeDtypeStruct((shards // 2, 2, 3 * slots // 2), jnp.bfloat16),
        ),
        in_specs=[VMEM, VMEM, VMEM, VMEM, SMEM, VMEM, VMEM],
        out_specs=(VMEM,) * 4,
        scratch_shapes=[
            pltpu.VMEM((queries + 1, 8, POS), f32),
            pltpu.VMEM((2, 3 * slots // 2), f32),
        ],
        name="lambdas",
    )(gap, discount, scores, clicks, lengths, leaf.reshape(queries, POS), sums[None])
    same_core = [[2 * chip + core for chip in range(shards // 2)] for core in range(2)]
    side = lax.all_to_all(side, "doc", 0, 0, axis_index_groups=same_core, tiled=True)
    shown = jnp.sum((data[:, 0, :slots] >= 0).astype(f32), axis=1).astype(jnp.int32)
    plan = pl.pallas_call(
        plan_kernel,
        out_shape=(
            jax.ShapeDtypeStruct((shards * tiles + 2 * STEP,), jnp.int32),
            jax.ShapeDtypeStruct((2,), jnp.int32),
        ),
        in_specs=[SMEM],
        out_specs=(SMEM, SMEM),
        name="plan",
    )((shown + (TILE - 1)) // TILE)
    other_side = lax.ppermute(side, "doc", [(at, at ^ 1) for at in range(shards)])
    core = lax.axis_index("doc") % 2
    data, side, other_side = (
        pltpu.with_memory_space_constraint(array, pltpu.VMEM) for array in (data, side, other_side)
    )
    partial = hist_of(core.reshape(1), plan, data, side)
    hist = hist_of((1 - core).reshape(1), plan, data, other_side, partial)
    return (t_plus[0], t_minus[0], gradients, hist)


def solution(mesh):
    placed = (P("doc", None), P("doc", None), P("doc"), P(), P(), P("doc"), P("feat", "doc"))
    return jax.shard_map(
        body,
        mesh=mesh,
        in_specs=placed,
        out_specs=(P(), P(), P(None, "doc"), P(("feat", "doc"), None, None)),
        check_vma=False,
    )
```

```python
import jax
import jax.numpy as jnp
import numpy as np
from jax import lax
from jax.experimental import pallas as pl
from jax.experimental.pallas import tpu as pltpu
from jax.sharding import PartitionSpec as P


BINS = 256
LEAVES = 32
POS = 128
HALF = BINS // 2
TILE = 256
STEP = 8


def query_rows(scores, clicks, lengths_ref, queries, discount_row):
    lane = lax.broadcasted_iota(jnp.int32, (queries, POS), 1)
    row = lax.broadcasted_iota(jnp.int32, (queries, POS), 0)
    length = jnp.zeros((queries, POS), jnp.int32)
    for query in range(queries):
        length = jnp.where(row == query, lengths_ref[query], length)
    shown = lane < length
    clicked = shown & (clicks == 1)
    skipped = shown & (clicks == 0)
    count = jnp.sum(jnp.where(clicked, 1.0, 0.0), axis=1, keepdims=True)
    ideal = jnp.sum(
        jnp.where(lane.astype(jnp.float32) < count, discount_row, 0.0), axis=1, keepdims=True
    )
    ideal = jnp.maximum(ideal, 1.0)
    side = jnp.where(clicked, 1.0, jnp.where(skipped, -1.0, 0.0))
    return clicked, skipped, side, side * scores, ideal


def turned(rows):
    queries = rows[0].shape[0]
    pad = jnp.zeros((POS - queries * len(rows), POS), jnp.float32)
    return jnp.transpose(jnp.concatenate(list(rows) + [pad], axis=0))


def pair_kernel(gap_ref, discount_ref, scores_ref, clicks_ref, lengths_ref, plus_ref, minus_ref, bins_ref,
                sent_ref, packed):
    queries = scores_ref.shape[0]
    discount_row = discount_ref[...]
    clicked, skipped, side, signed, ideal = query_rows(
        scores_ref[...], clicks_ref[...], lengths_ref, queries, discount_row
    )
    weight = jnp.where(clicked, 1.0 / plus_ref[...], jnp.where(skipped, -1.0 / minus_ref[...], 0.0))
    columns = turned([signed, weight])
    scale = 1.0 / ideal
    plus = jnp.zeros((1, POS), jnp.float32)
    minus = jnp.zeros((1, POS), jnp.float32)
    for query in range(queries):
        other = columns[:, query : query + 1]
        strength = columns[:, queries + query : queries + query + 1]
        spread = other + signed[query : query + 1]
        cross = jnp.maximum(strength * -side[query : query + 1], 0.0)
        loss = jnp.maximum(-spread, 0.0) + jnp.log1p(jnp.exp(-jnp.abs(spread)))
        total = jnp.sum(cross * gap_ref[...] * loss, axis=0, keepdims=True)
        total = total * scale[query : query + 1]
        plus += jnp.where(side[query : query + 1] > 0.0, total, 0.0)
        minus += jnp.where(side[query : query + 1] < 0.0, total, 0.0)
    features, slots = bins_ref.shape
    for at, part in enumerate((plus, minus)):
        high = part.astype(jnp.bfloat16).astype(jnp.float32)
        pieces = jnp.concatenate([high, part - high], axis=0).astype(jnp.bfloat16)
        sent_ref[:, :, slots + at * POS : slots + (at + 1) * POS] = jnp.broadcast_to(
            pieces[None], (features // 2, 2, POS)
        )
    packed[...] = jnp.full(packed.shape, -1.0, jnp.float32)
    lane = lax.broadcasted_iota(jnp.int32, (1, POS), 1)
    start = jnp.int32(0)
    for query in range(queries):
        group = start // POS
        shift = start - group * POS
        length = lengths_ref[query]
        moved = pltpu.roll(
            bins_ref[:, query * POS : (query + 1) * POS].astype(jnp.float32), shift, 1
        )
        here = (lane >= shift) & (lane < shift + length)
        there = lane < shift + length - POS
        packed[group] = jnp.where(here, moved, packed[group])
        packed[group + 1] = jnp.where(there, moved, packed[group + 1])
        start += length
    for group in range(slots // POS):
        for owner in range(features // 2):
            sent_ref[owner, :, group * POS : (group + 1) * POS] = packed[
                group, 2 * owner : 2 * owner + 2
            ].astype(jnp.bfloat16)


def lambda_kernel(gap_ref, discount_ref, scores_ref, clicks_ref, lengths_ref, leaf_ref, data_ref, plus_ref, minus_ref,
                  grad_ref, side_ref, packed, flat):
    queries = scores_ref.shape[0]
    discount_row = discount_ref[...]
    slots = grad_ref.shape[1]
    sums = jnp.sum(data_ref[:, :, slots:].astype(jnp.float32), axis=0)
    sums = sums[0:1] + sums[1:2]
    plus_sum = sums[:, :POS]
    minus_sum = sums[:, POS:]
    plus = jnp.sqrt(plus_sum / plus_sum[:, 0:1])
    minus = jnp.sqrt(minus_sum / minus_sum[:, 0:1])
    plus_ref[...] = plus
    minus_ref[...] = minus
    clicked, skipped, side, signed, ideal = query_rows(
        scores_ref[...], clicks_ref[...], lengths_ref, queries, discount_row
    )
    weight = jnp.where(clicked, 1.0 / plus, jnp.where(skipped, -1.0 / minus, 0.0))
    columns = turned([signed, weight])
    outer = jnp.abs(weight) / ideal
    packed[...] = jnp.zeros_like(packed)
    lane = lax.broadcasted_iota(jnp.int32, (1, POS), 1)
    start = jnp.int32(0)
    for query in range(queries):
        other = columns[:, query : query + 1]
        strength = columns[:, queries + query : queries + query + 1]
        spread = other + signed[query : query + 1]
        cross = jnp.maximum(strength * -side[query : query + 1], 0.0)
        grown = jnp.exp(spread)
        chance = 1.0 / (1.0 + grown)
        first = cross * gap_ref[...] * chance
        second = first * (grown * chance)
        slope = jnp.sum(first, axis=0, keepdims=True) * outer[query : query + 1]
        slope = slope * -side[query : query + 1]
        curve = jnp.sum(second, axis=0, keepdims=True) * outer[query : query + 1]
        grad_ref[0:1, query * POS : (query + 1) * POS] = slope
        grad_ref[1:2, query * POS : (query + 1) * POS] = curve
        group = start // POS
        shift = start - group * POS
        length = lengths_ref[query]
        rows = jnp.concatenate(
            [slope, curve, leaf_ref[query : query + 1].astype(jnp.float32),
             jnp.zeros((5, POS), jnp.float32)], axis=0
        )
        moved = pltpu.roll(rows, shift, 1)
        here = (lane >= shift) & (lane < shift + length)
        there = lane < shift + length - POS
        packed[group] = jnp.where(here, moved, packed[group])
        packed[group + 1] = jnp.where(there, moved, packed[group + 1])
        start += length
    for tile in range(queries * POS // TILE):
        at = 3 * POS * tile
        for half in range(2):
            rows = packed[2 * tile + half]
            flat[:, at + half * POS : at + (half + 1) * POS] = rows[0:2]
            flat[half : half + 1, at + 2 * POS : at + 3 * POS] = rows[2:3]
    side_ref[...] = jnp.broadcast_to(flat[...].astype(jnp.bfloat16)[None], side_ref.shape)


def plan_kernel(filled_ref, list_ref, total_ref):
    chips = filled_ref.shape[0] // 2
    tiles = (list_ref.shape[0] // 2 - STEP) // chips
    for core in range(2):
        base = core * (chips * tiles + STEP)

        def one_block(chip, carry):
            at, spare = carry
            used = filled_ref[2 * chip + core]
            for tile in range(tiles):
                list_ref[base + at] = chip * 8 + tile
                at = at + jnp.where(tile < used, 1, 0)
            return at, jnp.where(used < tiles, chip * 8 + tiles - 1, spare)

        at, spare = lax.fori_loop(0, chips, one_block, (jnp.int32(0), jnp.int32(0)))
        for extra in range(STEP):
            list_ref[base + at + extra] = spare
        total_ref[core] = (at + STEP - 1) // STEP


def accumulate(core, list_ref, total_ref, data_ref, side_ref, accs):
    base = core * (list_ref.shape[0] // 2)
    rows_a = lax.broadcasted_iota(jnp.int32, (2 * LEAVES, TILE), 0).astype(jnp.bfloat16)
    rows_b = lax.broadcasted_iota(jnp.int32, (HALF, TILE), 0).astype(jnp.bfloat16)
    zero = jnp.zeros((), jnp.bfloat16)
    one = jnp.ones((), jnp.bfloat16)

    def some_tiles(step, carry):
        for at in range(STEP):
            entry = list_ref[base + step * STEP + at]
            chip = lax.shift_right_logical(entry, 3)
            tile = lax.bitwise_and(entry, 7)
            bins = data_ref[2 * chip + core, :, pl.ds(pl.multiple_of(tile * TILE, TILE), TILE)]
            side = side_ref[chip, :, pl.ds(pl.multiple_of(tile * 3 * POS, POS), 3 * POS)]
            leaf = jnp.concatenate([side[0:1, TILE:], side[1:2, TILE:]], axis=1)
            left = []
            right = []
            for feature in range(2):
                row = bins[feature : feature + 1]
                high = row >= jnp.asarray(HALF, jnp.bfloat16)
                hit = jnp.where(high, leaf + jnp.asarray(LEAVES, jnp.bfloat16), leaf) == rows_a
                low = jnp.where(high, row - jnp.asarray(HALF, jnp.bfloat16), row)
                left.append(jnp.where(hit, side[0:1, :TILE], zero))
                left.append(jnp.where(hit, side[1:2, :TILE], zero))
                right.append(jnp.where(low == rows_b, one, zero))
            unit = at % 2
            register = (at // 2) % 2
            pltpu.matmul_push_rhs(jnp.concatenate(right, axis=0), register, unit, transpose=True)
            pltpu.matmul_acc_lhs(accs[unit], jnp.concatenate(left, axis=0), register)
        return carry

    lax.fori_loop(0, total_ref[core], some_tiles, 0)


def summed(core, list_ref, total_ref, data_ref, side_ref, finish):
    def run(acc_a, acc_b):
        accumulate(core, list_ref, total_ref, data_ref, side_ref, (acc_a, acc_b))
        finish(pltpu.matmul_pop(acc_a) + pltpu.matmul_pop(acc_b))

    shape = (8 * LEAVES, BINS)
    pl.run_scoped(run, pltpu.ACC(0)(shape, jnp.float32), pltpu.ACC(1)(shape, jnp.float32))


def first_kernel(core_ref, list_ref, total_ref, data_ref, side_ref, out_ref):
    rows = 4 * LEAVES

    def finish(total):
        for feature in range(2):
            out_ref[feature] = total[
                feature * rows : (feature + 1) * rows, feature * HALF : (feature + 1) * HALF
            ]

    summed(core_ref[0], list_ref, total_ref, data_ref, side_ref, finish)


def second_kernel(core_ref, list_ref, total_ref, data_ref, side_ref, before_ref, out_ref):
    rows = 4 * LEAVES

    def finish(total):
        for feature in range(2):
            mine = total[
                feature * rows : (feature + 1) * rows, feature * HALF : (feature + 1) * HALF
            ] + before_ref[feature]
            for which in range(2):
                for high in range(2):
                    at = (2 * which + high) * LEAVES
                    out_ref[
                        feature,
                        which * LEAVES : (which + 1) * LEAVES,
                        high * HALF : (high + 1) * HALF,
                    ] = mine[at : at + LEAVES]

    summed(core_ref[0], list_ref, total_ref, data_ref, side_ref, finish)


VMEM = pl.BlockSpec(memory_space=pltpu.VMEM)
SMEM = pl.BlockSpec(memory_space=pltpu.SMEM)


def in_vmem(array):
    return pltpu.with_memory_space_constraint(array, pltpu.VMEM)


def hist_of(core, plan, data, side, before=None):
    part = (2, 4 * LEAVES, HALF)
    if before is None:
        return pl.pallas_call(
            first_kernel,
            out_shape=pltpu.VMEM(part, jnp.float32),
            in_specs=[SMEM, SMEM, SMEM, VMEM, VMEM],
            out_specs=VMEM,
            name="first_half",
        )(core, *plan, data, side)
    return pl.pallas_call(
        second_kernel,
        out_shape=jax.ShapeDtypeStruct((2, 2 * LEAVES, BINS), jnp.float32),
        in_specs=[SMEM, SMEM, SMEM, VMEM, VMEM, VMEM],
        out_specs=VMEM,
        name="second_half",
    )(core, *plan, data, side, before)


def body(scores, clicks, lengths, t_plus_old, t_minus_old, leaf, bins):
    shards = lax.axis_size("doc")
    queries = scores.shape[0]
    slots = leaf.shape[0]
    tiles = slots // TILE
    places = np.arange(POS, dtype=np.float32)
    discount = (1.0 / np.log2(2.0 + places)).astype(np.float32)
    gap = jnp.asarray(np.abs(discount[:, None] - discount[None, :]))
    discount = jnp.asarray(discount[None])
    f32 = jnp.float32
    sent = pl.pallas_call(
        pair_kernel,
        out_shape=pltpu.VMEM((shards, 2, slots + 2 * POS), jnp.bfloat16),
        in_specs=[VMEM, VMEM, VMEM, VMEM, SMEM, VMEM, VMEM, VMEM],
        out_specs=VMEM,
        scratch_shapes=[pltpu.VMEM((slots // POS + 1, bins.shape[0], POS), f32)],
        name="pair_terms",
    )(gap, discount, scores, clicks, lengths, t_plus_old[None], t_minus_old[None], bins)
    data = lax.all_to_all(sent, "doc", 0, 0, tiled=True)
    t_plus, t_minus, gradients, side = pl.pallas_call(
        lambda_kernel,
        out_shape=(
            pltpu.VMEM((1, POS), f32),
            pltpu.VMEM((1, POS), f32),
            pltpu.VMEM((2, slots), f32),
            pltpu.VMEM((shards // 2, 2, 3 * slots // 2), jnp.bfloat16),
        ),
        in_specs=[VMEM, VMEM, VMEM, VMEM, SMEM, VMEM, VMEM],
        out_specs=(VMEM,) * 4,
        scratch_shapes=[
            pltpu.VMEM((queries + 1, 8, POS), f32),
            pltpu.VMEM((2, 3 * slots // 2), f32),
        ],
        name="lambdas",
    )(
        in_vmem(gap),
        in_vmem(discount),
        in_vmem(scores),
        in_vmem(clicks),
        lengths,
        in_vmem(leaf.reshape(queries, POS)),
        in_vmem(data),
    )
    same_core = [[2 * chip + core for chip in range(shards // 2)] for core in range(2)]
    side = lax.all_to_all(side, "doc", 0, 0, axis_index_groups=same_core, tiled=True)
    shown = jnp.sum((data[:, 0, :slots] >= 0).astype(f32), axis=1).astype(jnp.int32)
    plan = pl.pallas_call(
        plan_kernel,
        out_shape=(
            jax.ShapeDtypeStruct((shards * tiles + 2 * STEP,), jnp.int32),
            jax.ShapeDtypeStruct((2,), jnp.int32),
        ),
        in_specs=[SMEM],
        out_specs=(SMEM, SMEM),
        name="plan",
    )((shown + (TILE - 1)) // TILE)
    other_side = lax.ppermute(side, "doc", [(at, at ^ 1) for at in range(shards)])
    core = lax.axis_index("doc") % 2
    partial = hist_of(core.reshape(1), plan, in_vmem(data), in_vmem(side))
    hist = hist_of((1 - core).reshape(1), plan, in_vmem(data), in_vmem(other_side), partial)
    return (t_plus[0], t_minus[0], gradients, hist)


def solution(mesh):
    placed = (P("doc", None), P("doc", None), P("doc"), P(), P(), P("doc"), P("feat", "doc"))
    return jax.shard_map(
        body,
        mesh=mesh,
        in_specs=placed,
        out_specs=(P(), P(), P(None, "doc"), P(("feat", "doc"), None, None)),
        check_vma=False,
    )
```

```python
import jax
import jax.numpy as jnp
import numpy as np
from jax import lax
from jax.experimental import pallas as pl
from jax.experimental.pallas import tpu as pltpu
from jax.sharding import PartitionSpec as P


BINS = 256
LEAVES = 32
POS = 128
HALF = BINS // 2
TILE = 256
STEP = 8


def query_rows(scores, clicks, lengths_ref, queries, discount_row):
    lane = lax.broadcasted_iota(jnp.int32, (queries, POS), 1)
    row = lax.broadcasted_iota(jnp.int32, (queries, POS), 0)
    length = jnp.zeros((queries, POS), jnp.int32)
    for query in range(queries):
        length = jnp.where(row == query, lengths_ref[query], length)
    shown = lane < length
    clicked = shown & (clicks == 1)
    skipped = shown & (clicks == 0)
    count = jnp.sum(jnp.where(clicked, 1.0, 0.0), axis=1, keepdims=True)
    ideal = jnp.sum(
        jnp.where(lane.astype(jnp.float32) < count, discount_row, 0.0), axis=1, keepdims=True
    )
    ideal = jnp.maximum(ideal, 1.0)
    side = jnp.where(clicked, 1.0, jnp.where(skipped, -1.0, 0.0))
    return clicked, skipped, side, side * scores, ideal


def turned(rows):
    queries = rows[0].shape[0]
    pad = jnp.zeros((POS - queries * len(rows), POS), jnp.float32)
    return jnp.transpose(jnp.concatenate(list(rows) + [pad], axis=0))


def pair_kernel(gap_ref, scores_ref, clicks_ref, lengths_ref, plus_ref, minus_ref, bins_ref,
                sent_ref, packed):
    queries = scores_ref.shape[0]
    discount_row = gap_ref[POS : POS + 1]
    clicked, skipped, side, signed, ideal = query_rows(
        scores_ref[...], clicks_ref[...], lengths_ref, queries, discount_row
    )
    weight = jnp.where(clicked, 1.0 / plus_ref[...], jnp.where(skipped, -1.0 / minus_ref[...], 0.0))
    columns = turned([signed, weight])
    scale = 1.0 / ideal
    plus = jnp.zeros((1, POS), jnp.float32)
    minus = jnp.zeros((1, POS), jnp.float32)
    for query in range(queries):
        other = columns[:, query : query + 1]
        strength = columns[:, queries + query : queries + query + 1]
        spread = other + signed[query : query + 1]
        cross = jnp.maximum(strength * -side[query : query + 1], 0.0)
        loss = jnp.maximum(-spread, 0.0) + jnp.log1p(jnp.exp(-jnp.abs(spread)))
        total = jnp.sum(cross * gap_ref[:POS] * loss, axis=0, keepdims=True)
        total = total * scale[query : query + 1]
        plus += jnp.where(side[query : query + 1] > 0.0, total, 0.0)
        minus += jnp.where(side[query : query + 1] < 0.0, total, 0.0)
    features, slots = bins_ref.shape
    for at, part in enumerate((plus, minus)):
        high = part.astype(jnp.bfloat16).astype(jnp.float32)
        pieces = jnp.concatenate([high, part - high], axis=0).astype(jnp.bfloat16)
        sent_ref[:, :, slots + at * POS : slots + (at + 1) * POS] = jnp.broadcast_to(
            pieces[None], (features // 2, 2, POS)
        )
    packed[...] = jnp.full(packed.shape, -1.0, jnp.float32)
    lane = lax.broadcasted_iota(jnp.int32, (1, POS), 1)
    start = jnp.int32(0)
    for query in range(queries):
        group = start // POS
        shift = start - group * POS
        length = lengths_ref[query]
        moved = pltpu.roll(
            bins_ref[:, query * POS : (query + 1) * POS].astype(jnp.float32), shift, 1
        )
        here = (lane >= shift) & (lane < shift + length)
        there = lane < shift + length - POS
        packed[group] = jnp.where(here, moved, packed[group])
        packed[group + 1] = jnp.where(there, moved, packed[group + 1])
        start += length
    for group in range(slots // POS):
        for owner in range(features // 2):
            sent_ref[owner, :, group * POS : (group + 1) * POS] = packed[
                group, 2 * owner : 2 * owner + 2
            ].astype(jnp.bfloat16)


def lambda_kernel(gap_ref, scores_ref, clicks_ref, lengths_ref, leaf_ref, data_ref, plus_ref, minus_ref,
                  grad_ref, side_ref, packed, flat):
    queries = scores_ref.shape[0]
    discount_row = gap_ref[POS : POS + 1]
    slots = grad_ref.shape[1]
    sums = jnp.sum(data_ref[:, :, slots:].astype(jnp.float32), axis=0)
    sums = sums[0:1] + sums[1:2]
    plus_sum = sums[:, :POS]
    minus_sum = sums[:, POS:]
    plus = jnp.sqrt(plus_sum / plus_sum[:, 0:1])
    minus = jnp.sqrt(minus_sum / minus_sum[:, 0:1])
    plus_ref[...] = plus
    minus_ref[...] = minus
    clicked, skipped, side, signed, ideal = query_rows(
        scores_ref[...], clicks_ref[...], lengths_ref, queries, discount_row
    )
    weight = jnp.where(clicked, 1.0 / plus, jnp.where(skipped, -1.0 / minus, 0.0))
    columns = turned([signed, weight])
    outer = jnp.abs(weight) / ideal
    packed[...] = jnp.zeros_like(packed)
    lane = lax.broadcasted_iota(jnp.int32, (1, POS), 1)
    start = jnp.int32(0)
    for query in range(queries):
        other = columns[:, query : query + 1]
        strength = columns[:, queries + query : queries + query + 1]
        spread = other + signed[query : query + 1]
        cross = jnp.maximum(strength * -side[query : query + 1], 0.0)
        grown = jnp.exp(spread)
        chance = 1.0 / (1.0 + grown)
        first = cross * gap_ref[:POS] * chance
        second = first * (grown * chance)
        slope = jnp.sum(first, axis=0, keepdims=True) * outer[query : query + 1]
        slope = slope * -side[query : query + 1]
        curve = jnp.sum(second, axis=0, keepdims=True) * outer[query : query + 1]
        grad_ref[0:1, query * POS : (query + 1) * POS] = slope
        grad_ref[1:2, query * POS : (query + 1) * POS] = curve
        group = start // POS
        shift = start - group * POS
        length = lengths_ref[query]
        rows = jnp.concatenate(
            [slope, curve, leaf_ref[query : query + 1].astype(jnp.float32),
             jnp.zeros((5, POS), jnp.float32)], axis=0
        )
        moved = pltpu.roll(rows, shift, 1)
        here = (lane >= shift) & (lane < shift + length)
        there = lane < shift + length - POS
        packed[group] = jnp.where(here, moved, packed[group])
        packed[group + 1] = jnp.where(there, moved, packed[group + 1])
        start += length
    for tile in range(queries * POS // TILE):
        at = 3 * POS * tile
        for half in range(2):
            rows = packed[2 * tile + half]
            flat[:, at + half * POS : at + (half + 1) * POS] = rows[0:2]
            flat[half : half + 1, at + 2 * POS : at + 3 * POS] = rows[2:3]
    side_ref[...] = jnp.broadcast_to(flat[...].astype(jnp.bfloat16)[None], side_ref.shape)


def plan_kernel(
    filled_ref, plus_in, minus_in, grad_in, list_ref, total_ref, plus_ref, minus_ref, grad_ref
):
    plus_ref[...] = plus_in[...]
    minus_ref[...] = minus_in[...]
    grad_ref[...] = grad_in[...]
    chips = filled_ref.shape[0] // 2
    tiles = (list_ref.shape[0] // 2 - STEP) // chips
    for core in range(2):
        base = core * (chips * tiles + STEP)

        def one_block(chip, carry):
            at, spare = carry
            used = filled_ref[2 * chip + core]
            for tile in range(tiles):
                list_ref[base + at] = chip * 8 + tile
                at = at + jnp.where(tile < used, 1, 0)
            return at, jnp.where(used < tiles, chip * 8 + tiles - 1, spare)

        at, spare = lax.fori_loop(0, chips, one_block, (jnp.int32(0), jnp.int32(0)))
        for extra in range(STEP):
            list_ref[base + at + extra] = spare
        total_ref[core] = (at + STEP - 1) // STEP


def accumulate(core, list_ref, total_ref, data_ref, side_ref, accs):
    base = core * (list_ref.shape[0] // 2)
    rows_a = lax.broadcasted_iota(jnp.int32, (2 * LEAVES, TILE), 0).astype(jnp.bfloat16)
    rows_b = lax.broadcasted_iota(jnp.int32, (HALF, TILE), 0).astype(jnp.bfloat16)
    zero = jnp.zeros((), jnp.bfloat16)
    one = jnp.ones((), jnp.bfloat16)

    def some_tiles(step, carry):
        for at in range(STEP):
            entry = list_ref[base + step * STEP + at]
            chip = lax.shift_right_logical(entry, 3)
            tile = lax.bitwise_and(entry, 7)
            bins = data_ref[2 * chip + core, :, pl.ds(pl.multiple_of(tile * TILE, TILE), TILE)]
            side = side_ref[chip, :, pl.ds(pl.multiple_of(tile * 3 * POS, POS), 3 * POS)]
            leaf = jnp.concatenate([side[0:1, TILE:], side[1:2, TILE:]], axis=1)
            left = []
            right = []
            for feature in range(2):
                row = bins[feature : feature + 1]
                high = row >= jnp.asarray(HALF, jnp.bfloat16)
                hit = jnp.where(high, leaf + jnp.asarray(LEAVES, jnp.bfloat16), leaf) == rows_a
                low = jnp.where(high, row - jnp.asarray(HALF, jnp.bfloat16), row)
                left.append(jnp.where(hit, side[0:1, :TILE], zero))
                left.append(jnp.where(hit, side[1:2, :TILE], zero))
                right.append(jnp.where(low == rows_b, one, zero))
            unit = at % 2
            register = (at // 2) % 2
            pltpu.matmul_push_rhs(jnp.concatenate(right, axis=0), register, unit, transpose=True)
            pltpu.matmul_acc_lhs(accs[unit], jnp.concatenate(left, axis=0), register)
        return carry

    lax.fori_loop(0, total_ref[core], some_tiles, 0)


def summed(core, list_ref, total_ref, data_ref, side_ref, finish):
    def run(acc_a, acc_b):
        accumulate(core, list_ref, total_ref, data_ref, side_ref, (acc_a, acc_b))
        finish(pltpu.matmul_pop(acc_a) + pltpu.matmul_pop(acc_b))

    shape = (8 * LEAVES, BINS)
    pl.run_scoped(run, pltpu.ACC(0)(shape, jnp.float32), pltpu.ACC(1)(shape, jnp.float32))


def first_kernel(core_ref, list_ref, total_ref, data_ref, side_ref, out_ref):
    rows = 4 * LEAVES

    def finish(total):
        for feature in range(2):
            out_ref[feature] = total[
                feature * rows : (feature + 1) * rows, feature * HALF : (feature + 1) * HALF
            ]

    summed(core_ref[0], list_ref, total_ref, data_ref, side_ref, finish)


def second_kernel(core_ref, list_ref, total_ref, data_ref, side_ref, before_ref, out_ref):
    rows = 4 * LEAVES

    def finish(total):
        for feature in range(2):
            mine = total[
                feature * rows : (feature + 1) * rows, feature * HALF : (feature + 1) * HALF
            ] + before_ref[feature]
            for which in range(2):
                for high in range(2):
                    at = (2 * which + high) * LEAVES
                    out_ref[
                        feature,
                        which * LEAVES : (which + 1) * LEAVES,
                        high * HALF : (high + 1) * HALF,
                    ] = mine[at : at + LEAVES]

    summed(core_ref[0], list_ref, total_ref, data_ref, side_ref, finish)


VMEM = pl.BlockSpec(memory_space=pltpu.VMEM)
SMEM = pl.BlockSpec(memory_space=pltpu.SMEM)


def in_vmem(array):
    return pltpu.with_memory_space_constraint(array, pltpu.VMEM)


def in_smem(array):
    return pltpu.with_memory_space_constraint(array, pltpu.SMEM)


def hist_of(core, plan, data, side, before=None):
    part = (2, 4 * LEAVES, HALF)
    if before is None:
        return pl.pallas_call(
            first_kernel,
            out_shape=pltpu.VMEM(part, jnp.float32),
            in_specs=[SMEM, SMEM, SMEM, VMEM, VMEM],
            out_specs=VMEM,
            name="first_half",
        )(core, *plan, data, side)
    return pl.pallas_call(
        second_kernel,
        out_shape=jax.ShapeDtypeStruct((2, 2 * LEAVES, BINS), jnp.float32),
        in_specs=[SMEM, SMEM, SMEM, VMEM, VMEM, VMEM],
        out_specs=VMEM,
        name="second_half",
    )(core, *plan, data, side, before)


def body(scores, clicks, lengths, t_plus_old, t_minus_old, leaf, bins):
    shards = lax.axis_size("doc")
    queries = scores.shape[0]
    slots = leaf.shape[0]
    tiles = slots // TILE
    places = np.arange(POS, dtype=np.float32)
    discount = (1.0 / np.log2(2.0 + places)).astype(np.float32)
    gap = np.abs(discount[:, None] - discount[None, :])
    gap = jnp.asarray(np.concatenate([gap, np.tile(discount[None], (8, 1))]))
    f32 = jnp.float32
    sent = pl.pallas_call(
        pair_kernel,
        out_shape=pltpu.VMEM((shards, 2, slots + 2 * POS), jnp.bfloat16),
        in_specs=[VMEM, VMEM, VMEM, SMEM, VMEM, VMEM, VMEM],
        out_specs=VMEM,
        scratch_shapes=[pltpu.VMEM((slots // POS + 1, bins.shape[0], POS), f32)],
        name="pair_terms",
    )(gap, scores, clicks, lengths, t_plus_old[None], t_minus_old[None], bins)
    data = lax.all_to_all(sent, "doc", 0, 0, tiled=True)
    t_plus, t_minus, gradients, side = pl.pallas_call(
        lambda_kernel,
        out_shape=(
            pltpu.VMEM((1, POS), f32),
            pltpu.VMEM((1, POS), f32),
            pltpu.VMEM((2, slots), f32),
            pltpu.VMEM((shards // 2, 2, 3 * slots // 2), jnp.bfloat16),
        ),
        in_specs=[VMEM, VMEM, VMEM, SMEM, VMEM, VMEM],
        out_specs=(VMEM,) * 4,
        scratch_shapes=[
            pltpu.VMEM((queries + 1, 8, POS), f32),
            pltpu.VMEM((2, 3 * slots // 2), f32),
        ],
        name="lambdas",
    )(
        in_vmem(gap),
        in_vmem(scores),
        in_vmem(clicks),
        in_smem(lengths),
        in_vmem(leaf.reshape(queries, POS)),
        in_vmem(data),
    )
    same_core = [[2 * chip + core for chip in range(shards // 2)] for core in range(2)]
    side = lax.all_to_all(side, "doc", 0, 0, axis_index_groups=same_core, tiled=True)
    shown = jnp.sum((data[:, 0, :slots] >= 0).astype(f32), axis=1).astype(jnp.int32)
    *plan, t_plus, t_minus, gradients = pl.pallas_call(
        plan_kernel,
        out_shape=(
            pltpu.SMEM((shards * tiles + 2 * STEP,), jnp.int32),
            pltpu.SMEM((2,), jnp.int32),
            jax.ShapeDtypeStruct((1, POS), f32),
            jax.ShapeDtypeStruct((1, POS), f32),
            jax.ShapeDtypeStruct((2, slots), f32),
        ),
        in_specs=[SMEM, VMEM, VMEM, VMEM],
        out_specs=(SMEM, SMEM, VMEM, VMEM, VMEM),
        name="plan",
    )((shown + (TILE - 1)) // TILE, in_vmem(t_plus), in_vmem(t_minus), in_vmem(gradients))
    other_side = lax.ppermute(side, "doc", [(at, at ^ 1) for at in range(shards)])
    core = lax.axis_index("doc") % 2
    partial = hist_of(core.reshape(1), plan, in_vmem(data), in_vmem(side))
    hist = hist_of((1 - core).reshape(1), plan, in_vmem(data), in_vmem(other_side), in_vmem(partial))
    return (t_plus[0], t_minus[0], gradients, hist)


def solution(mesh):
    placed = (P("doc", None), P("doc", None), P("doc"), P(), P(), P("doc"), P("feat", "doc"))
    return jax.shard_map(
        body,
        mesh=mesh,
        in_specs=placed,
        out_specs=(P(), P(), P(None, "doc"), P(("feat", "doc"), None, None)),
        check_vma=False,
    )
```

```python
import jax
import jax.numpy as jnp
import numpy as np
from jax import lax
from jax.experimental import pallas as pl
from jax.experimental.pallas import tpu as pltpu
from jax.sharding import PartitionSpec as P


BINS = 256
LEAVES = 32
POS = 128
HALF = BINS // 2
TILE = 256
STEP = 8


def query_rows(scores, clicks, lengths_ref, queries, discount_row):
    lane = lax.broadcasted_iota(jnp.int32, (queries, POS), 1)
    row = lax.broadcasted_iota(jnp.int32, (queries, POS), 0)
    length = jnp.zeros((queries, POS), jnp.int32)
    for query in range(queries):
        length = jnp.where(row == query, lengths_ref[query], length)
    shown = lane < length
    clicked = shown & (clicks == 1)
    skipped = shown & (clicks == 0)
    count = jnp.sum(jnp.where(clicked, 1.0, 0.0), axis=1, keepdims=True)
    ideal = jnp.sum(
        jnp.where(lane.astype(jnp.float32) < count, discount_row, 0.0), axis=1, keepdims=True
    )
    ideal = jnp.maximum(ideal, 1.0)
    side = jnp.where(clicked, 1.0, jnp.where(skipped, -1.0, 0.0))
    return clicked, skipped, side, side * scores, ideal


def turned(rows):
    queries = rows[0].shape[0]
    pad = jnp.zeros((POS - queries * len(rows), POS), jnp.float32)
    return jnp.transpose(jnp.concatenate(list(rows) + [pad], axis=0))


def pair_kernel(gap_ref, scores_ref, clicks_ref, lengths_ref, plus_ref, minus_ref, bins_ref,
                sent_ref, packed):
    queries = scores_ref.shape[0]
    discount_row = gap_ref[POS : POS + 1]
    clicked, skipped, side, signed, ideal = query_rows(
        scores_ref[...], clicks_ref[...], lengths_ref, queries, discount_row
    )
    weight = jnp.where(clicked, 1.0 / plus_ref[...], jnp.where(skipped, -1.0 / minus_ref[...], 0.0))
    columns = turned([signed, weight])
    scale = 1.0 / ideal
    plus = jnp.zeros((1, POS), jnp.float32)
    minus = jnp.zeros((1, POS), jnp.float32)
    for query in range(queries):
        other = columns[:, query : query + 1]
        strength = columns[:, queries + query : queries + query + 1]
        spread = other + signed[query : query + 1]
        cross = jnp.maximum(strength * -side[query : query + 1], 0.0)
        loss = jnp.maximum(-spread, 0.0) + jnp.log1p(jnp.exp(-jnp.abs(spread)))
        total = jnp.sum(cross * gap_ref[:POS] * loss, axis=0, keepdims=True)
        total = total * scale[query : query + 1]
        plus += jnp.where(side[query : query + 1] > 0.0, total, 0.0)
        minus += jnp.where(side[query : query + 1] < 0.0, total, 0.0)
    features, slots = bins_ref.shape
    for at, part in enumerate((plus, minus)):
        high = part.astype(jnp.bfloat16).astype(jnp.float32)
        pieces = jnp.concatenate([high, part - high], axis=0).astype(jnp.bfloat16)
        sent_ref[:, :, slots + at * POS : slots + (at + 1) * POS] = jnp.broadcast_to(
            pieces[None], (features // 2, 2, POS)
        )
    packed[...] = jnp.full(packed.shape, -1.0, jnp.float32)
    lane = lax.broadcasted_iota(jnp.int32, (1, POS), 1)
    start = jnp.int32(0)
    for query in range(queries):
        group = start // POS
        shift = start - group * POS
        length = lengths_ref[query]
        moved = pltpu.roll(
            bins_ref[:, query * POS : (query + 1) * POS].astype(jnp.float32), shift, 1
        )
        here = (lane >= shift) & (lane < shift + length)
        there = lane < shift + length - POS
        packed[group] = jnp.where(here, moved, packed[group])
        packed[group + 1] = jnp.where(there, moved, packed[group + 1])
        start += length
    for group in range(slots // POS):
        for owner in range(features // 2):
            sent_ref[owner, :, group * POS : (group + 1) * POS] = packed[
                group, 2 * owner : 2 * owner + 2
            ].astype(jnp.bfloat16)


def ready_kernel(gap_ref, scores_ref, clicks_ref, lengths_ref, first_ref, second_ref, side_ref,
                 scale_ref, held_ref):
    queries = scores_ref.shape[0]
    _, _, side, signed, ideal = query_rows(
        scores_ref[...], clicks_ref[...], lengths_ref, queries, gap_ref[POS : POS + 1]
    )
    side_ref[...] = side
    scale_ref[...] = jnp.broadcast_to(1.0 / ideal, scale_ref.shape)
    columns = turned([signed, side])
    for query in range(queries):
        held_ref[query] = lengths_ref[query]
        spread = columns[:, query : query + 1] + signed[query : query + 1]
        cross = columns[:, queries + query : queries + query + 1] * side[query : query + 1]
        grown = jnp.exp(spread)
        chance = 1.0 / (1.0 + grown)
        first = jnp.where(cross < 0.0, gap_ref[:POS] * chance, 0.0)
        first_ref[query] = first
        second_ref[query] = first * (grown * chance)


def lambda_kernel(first_ref, second_ref, own_ref, scale_ref, held_ref, leaf_ref, data_ref,
                  plus_ref, minus_ref, grad_ref, side_ref, packed, flat):
    queries = own_ref.shape[0]
    slots = grad_ref.shape[1]
    sums = jnp.sum(data_ref[:, :, slots:].astype(jnp.float32), axis=0)
    sums = sums[0:1] + sums[1:2]
    plus_sum = sums[:, :POS]
    minus_sum = sums[:, POS:]
    plus = jnp.sqrt(plus_sum / plus_sum[:, 0:1])
    minus = jnp.sqrt(minus_sum / minus_sum[:, 0:1])
    plus_ref[...] = plus
    minus_ref[...] = minus
    side = own_ref[...]
    weight = jnp.where(side > 0.0, 1.0 / plus, jnp.where(side < 0.0, 1.0 / minus, 0.0))
    columns = turned([weight])
    outer = weight * scale_ref[...]
    packed[...] = jnp.zeros_like(packed)
    lane = lax.broadcasted_iota(jnp.int32, (1, POS), 1)
    start = jnp.int32(0)
    for query in range(queries):
        strength = columns[:, query : query + 1]
        slope = jnp.sum(strength * first_ref[query], axis=0, keepdims=True)
        curve = jnp.sum(strength * second_ref[query], axis=0, keepdims=True)
        slope = slope * outer[query : query + 1] * -side[query : query + 1]
        curve = curve * outer[query : query + 1]
        grad_ref[0:1, query * POS : (query + 1) * POS] = slope
        grad_ref[1:2, query * POS : (query + 1) * POS] = curve
        group = start // POS
        shift = start - group * POS
        length = held_ref[query]
        rows = jnp.concatenate(
            [slope, curve, leaf_ref[query : query + 1].astype(jnp.float32),
             jnp.zeros((5, POS), jnp.float32)], axis=0
        )
        moved = pltpu.roll(rows, shift, 1)
        here = (lane >= shift) & (lane < shift + length)
        there = lane < shift + length - POS
        packed[group] = jnp.where(here, moved, packed[group])
        packed[group + 1] = jnp.where(there, moved, packed[group + 1])
        start += length
    for group in range(queries):
        rows = packed[group]
        row = group // (queries // 2)
        at = (queries + group % (queries // 2)) * POS
        flat[:, group * POS : (group + 1) * POS] = rows[0:2]
        flat[row : row + 1, at : at + POS] = rows[2:3]
    side_ref[...] = jnp.broadcast_to(flat[...].astype(jnp.bfloat16)[None], side_ref.shape)


def plan_kernel(
    filled_ref, plus_in, minus_in, grad_in, list_ref, total_ref, plus_ref, minus_ref, grad_ref
):
    plus_ref[...] = plus_in[...]
    minus_ref[...] = minus_in[...]
    grad_ref[...] = grad_in[...]
    chips = filled_ref.shape[0] // 2
    groups = (list_ref.shape[0] // 2 - 2 * STEP) // chips
    for core in range(2):
        base = core * (chips * groups + 2 * STEP)

        def one_block(chip, carry):
            at, spare = carry
            used = filled_ref[2 * chip + core]
            for group in range(groups):
                list_ref[base + at] = chip * 16 + group
                at = at + jnp.where(group < used, 1, 0)
            return at, jnp.where(used < groups, chip * 16 + groups - 1, spare)

        at, spare = lax.fori_loop(0, chips, one_block, (jnp.int32(0), jnp.int32(0)))
        for extra in range(2 * STEP):
            list_ref[base + at + extra] = spare
        total_ref[core] = (at + 2 * STEP - 1) // (2 * STEP)


def accumulate(core, list_ref, total_ref, data_ref, side_ref, accs):
    base = core * (list_ref.shape[0] // 2)
    groups = side_ref.shape[2] * 2 // (3 * POS)
    rows_a = lax.broadcasted_iota(jnp.int32, (2 * LEAVES, TILE), 0).astype(jnp.bfloat16)
    rows_b = lax.broadcasted_iota(jnp.int32, (HALF, TILE), 0).astype(jnp.bfloat16)
    zero = jnp.zeros((), jnp.bfloat16)
    one = jnp.ones((), jnp.bfloat16)

    def some_tiles(step, carry):
        for at in range(STEP):
            bins = []
            sides = []
            leaves = []
            for half in range(2):
                entry = list_ref[base + (step * STEP + at) * 2 + half]
                chip = lax.shift_right_logical(entry, 4)
                group = lax.bitwise_and(entry, 15)
                late = group >= groups // 2
                place = groups + group - jnp.where(late, groups // 2, 0)
                here = pl.ds(pl.multiple_of(group * POS, POS), POS)
                bins.append(data_ref[2 * chip + core, :, here])
                sides.append(side_ref[chip, :, here])
                pair = side_ref[chip, :, pl.ds(pl.multiple_of(place * POS, POS), POS)]
                leaves.append(jnp.where(late, pair[1:2], pair[0:1]))
            bins = jnp.concatenate(bins, axis=1)
            side = jnp.concatenate(sides, axis=1)
            leaf = jnp.concatenate(leaves, axis=1)
            left = []
            right = []
            for feature in range(2):
                row = bins[feature : feature + 1]
                high = row >= jnp.asarray(HALF, jnp.bfloat16)
                hit = jnp.where(high, leaf + jnp.asarray(LEAVES, jnp.bfloat16), leaf) == rows_a
                low = jnp.where(high, row - jnp.asarray(HALF, jnp.bfloat16), row)
                left.append(jnp.where(hit, side[0:1], zero))
                left.append(jnp.where(hit, side[1:2], zero))
                right.append(jnp.where(low == rows_b, one, zero))
            unit = at % 2
            register = (at // 2) % 2
            pltpu.matmul_push_rhs(jnp.concatenate(right, axis=0), register, unit, transpose=True)
            pltpu.matmul_acc_lhs(accs[unit], jnp.concatenate(left, axis=0), register)
        return carry

    lax.fori_loop(0, total_ref[core], some_tiles, 0)


def summed(core, list_ref, total_ref, data_ref, side_ref, finish):
    def run(acc_a, acc_b):
        accumulate(core, list_ref, total_ref, data_ref, side_ref, (acc_a, acc_b))
        finish(pltpu.matmul_pop(acc_a) + pltpu.matmul_pop(acc_b))

    shape = (8 * LEAVES, BINS)
    pl.run_scoped(run, pltpu.ACC(0)(shape, jnp.float32), pltpu.ACC(1)(shape, jnp.float32))


def first_kernel(core_ref, list_ref, total_ref, data_ref, side_ref, out_ref):
    rows = 4 * LEAVES

    def finish(total):
        for feature in range(2):
            out_ref[feature] = total[
                feature * rows : (feature + 1) * rows, feature * HALF : (feature + 1) * HALF
            ]

    summed(core_ref[0], list_ref, total_ref, data_ref, side_ref, finish)


def second_kernel(core_ref, list_ref, total_ref, data_ref, side_ref, before_ref, out_ref):
    rows = 4 * LEAVES

    def finish(total):
        for feature in range(2):
            mine = total[
                feature * rows : (feature + 1) * rows, feature * HALF : (feature + 1) * HALF
            ] + before_ref[feature]
            for which in range(2):
                for high in range(2):
                    at = (2 * which + high) * LEAVES
                    out_ref[
                        feature,
                        which * LEAVES : (which + 1) * LEAVES,
                        high * HALF : (high + 1) * HALF,
                    ] = mine[at : at + LEAVES]

    summed(core_ref[0], list_ref, total_ref, data_ref, side_ref, finish)


VMEM = pl.BlockSpec(memory_space=pltpu.VMEM)
SMEM = pl.BlockSpec(memory_space=pltpu.SMEM)


def in_vmem(array):
    return pltpu.with_memory_space_constraint(array, pltpu.VMEM)


def in_smem(array):
    return pltpu.with_memory_space_constraint(array, pltpu.SMEM)


def hist_of(core, plan, data, side, before=None):
    part = (2, 4 * LEAVES, HALF)
    if before is None:
        return pl.pallas_call(
            first_kernel,
            out_shape=pltpu.VMEM(part, jnp.float32),
            in_specs=[SMEM, SMEM, SMEM, VMEM, VMEM],
            out_specs=VMEM,
            name="first_half",
        )(core, *plan, data, side)
    return pl.pallas_call(
        second_kernel,
        out_shape=jax.ShapeDtypeStruct((2, 2 * LEAVES, BINS), jnp.float32),
        in_specs=[SMEM, SMEM, SMEM, VMEM, VMEM, VMEM],
        out_specs=VMEM,
        name="second_half",
    )(core, *plan, data, side, before)


def body(scores, clicks, lengths, t_plus_old, t_minus_old, leaf, bins):
    shards = lax.axis_size("doc")
    queries = scores.shape[0]
    slots = leaf.shape[0]
    groups = slots // POS
    places = np.arange(POS, dtype=np.float32)
    discount = (1.0 / np.log2(2.0 + places)).astype(np.float32)
    gap = np.abs(discount[:, None] - discount[None, :])
    gap = jnp.asarray(np.concatenate([gap, np.tile(discount[None], (8, 1))]))
    f32 = jnp.float32
    sent = pl.pallas_call(
        pair_kernel,
        out_shape=pltpu.VMEM((shards, 2, slots + 2 * POS), jnp.bfloat16),
        in_specs=[VMEM, VMEM, VMEM, SMEM, VMEM, VMEM, VMEM],
        out_specs=VMEM,
        scratch_shapes=[pltpu.VMEM((slots // POS + 1, bins.shape[0], POS), f32)],
        name="pair_terms",
    )(gap, scores, clicks, lengths, t_plus_old[None], t_minus_old[None], bins)
    data = lax.all_to_all(sent, "doc", 0, 0, tiled=True)
    first, second, own, scale, held = pl.pallas_call(
        ready_kernel,
        out_shape=(
            pltpu.VMEM((queries, POS, POS), f32),
            pltpu.VMEM((queries, POS, POS), f32),
            pltpu.VMEM((queries, POS), f32),
            pltpu.VMEM((queries, POS), f32),
            pltpu.SMEM((queries,), jnp.int32),
        ),
        in_specs=[VMEM, VMEM, VMEM, SMEM],
        out_specs=(VMEM, VMEM, VMEM, VMEM, SMEM),
        name="ready_pairs",
    )(gap, scores, clicks, lengths)
    t_plus, t_minus, gradients, side = pl.pallas_call(
        lambda_kernel,
        out_shape=(
            pltpu.VMEM((1, POS), f32),
            pltpu.VMEM((1, POS), f32),
            pltpu.VMEM((2, slots), f32),
            pltpu.VMEM((shards // 2, 2, 3 * slots // 2), jnp.bfloat16),
        ),
        in_specs=[VMEM, VMEM, VMEM, VMEM, SMEM, VMEM, VMEM],
        out_specs=(VMEM,) * 4,
        scratch_shapes=[
            pltpu.VMEM((queries + 1, 8, POS), f32),
            pltpu.VMEM((2, 3 * slots // 2), f32),
        ],
        name="lambdas",
    )(
        in_vmem(first),
        in_vmem(second),
        in_vmem(own),
        in_vmem(scale),
        in_smem(held),
        in_vmem(leaf.reshape(queries, POS)),
        in_vmem(data),
    )
    same_core = [[2 * chip + core for chip in range(shards // 2)] for core in range(2)]
    side = lax.all_to_all(side, "doc", 0, 0, axis_index_groups=same_core, tiled=True)
    shown = jnp.sum((data[:, 0, :slots] >= 0).astype(f32), axis=1).astype(jnp.int32)
    *plan, t_plus, t_minus, gradients = pl.pallas_call(
        plan_kernel,
        out_shape=(
            pltpu.SMEM((shards * groups + 4 * STEP,), jnp.int32),
            pltpu.SMEM((2,), jnp.int32),
            jax.ShapeDtypeStruct((1, POS), f32),
            jax.ShapeDtypeStruct((1, POS), f32),
            jax.ShapeDtypeStruct((2, slots), f32),
        ),
        in_specs=[SMEM, VMEM, VMEM, VMEM],
        out_specs=(SMEM, SMEM, VMEM, VMEM, VMEM),
        name="plan",
    )((shown + (POS - 1)) // POS, in_vmem(t_plus), in_vmem(t_minus), in_vmem(gradients))
    other_side = lax.ppermute(side, "doc", [(at, at ^ 1) for at in range(shards)])
    core = lax.axis_index("doc") % 2
    partial = hist_of(core.reshape(1), plan, in_vmem(data), in_vmem(side))
    hist = hist_of((1 - core).reshape(1), plan, in_vmem(data), in_vmem(other_side), in_vmem(partial))
    return (t_plus[0], t_minus[0], gradients, hist)


def solution(mesh):
    placed = (P("doc", None), P("doc", None), P("doc"), P(), P(), P("doc"), P("feat", "doc"))
    return jax.shard_map(
        body,
        mesh=mesh,
        in_specs=placed,
        out_specs=(P(), P(), P(None, "doc"), P(("feat", "doc"), None, None)),
        check_vma=False,
    )
```

```python
import jax
import jax.numpy as jnp
import numpy as np
from jax import lax
from jax.experimental import pallas as pl
from jax.experimental.pallas import tpu as pltpu
from jax.sharding import PartitionSpec as P


BINS = 256
LEAVES = 32
POS = 128
HALF = BINS // 2
TILE = 256
STEP = 4
WIDE = 4


def query_rows(scores, clicks, lengths_ref, queries, discount_row):
    lane = lax.broadcasted_iota(jnp.int32, (queries, POS), 1)
    row = lax.broadcasted_iota(jnp.int32, (queries, POS), 0)
    length = jnp.zeros((queries, POS), jnp.int32)
    for query in range(queries):
        length = jnp.where(row == query, lengths_ref[query], length)
    shown = lane < length
    clicked = shown & (clicks == 1)
    skipped = shown & (clicks == 0)
    count = jnp.sum(jnp.where(clicked, 1.0, 0.0), axis=1, keepdims=True)
    ideal = jnp.sum(
        jnp.where(lane.astype(jnp.float32) < count, discount_row, 0.0), axis=1, keepdims=True
    )
    ideal = jnp.maximum(ideal, 1.0)
    side = jnp.where(clicked, 1.0, jnp.where(skipped, -1.0, 0.0))
    return clicked, skipped, side, side * scores, ideal


def turned(rows):
    queries = rows[0].shape[0]
    pad = jnp.zeros((POS - queries * len(rows), POS), jnp.float32)
    return jnp.transpose(jnp.concatenate(list(rows) + [pad], axis=0))


def pair_kernel(gap_ref, scores_ref, clicks_ref, lengths_ref, plus_ref, minus_ref, bins_from,
                sent_to, bins_ref, sent_ref, packed, took, gave):
    take = pltpu.make_async_copy(bins_from, bins_ref, took)
    take.start()
    queries = scores_ref.shape[0]
    clicked, skipped, side, signed, ideal = query_rows(
        scores_ref[...], clicks_ref[...], lengths_ref, queries, gap_ref[POS : POS + 1]
    )
    weight = jnp.where(clicked, 1.0 / plus_ref[...], jnp.where(skipped, -1.0 / minus_ref[...], 0.0))
    columns = turned([signed, weight])
    scale = 1.0 / ideal
    sums = [jnp.zeros((1, POS), jnp.float32), jnp.zeros((1, POS), jnp.float32)]

    def add_query(query):
        other = columns[:, query : query + 1]
        strength = columns[:, queries + query : queries + query + 1]
        spread = other + signed[query : query + 1]
        cross = jnp.maximum(strength * -side[query : query + 1], 0.0)
        loss = jnp.maximum(-spread, 0.0) + jnp.log1p(jnp.exp(-jnp.abs(spread)))
        total = jnp.sum(cross * gap_ref[:POS] * loss, axis=0, keepdims=True)
        total = total * scale[query : query + 1]
        sums[0] += jnp.where(side[query : query + 1] > 0.0, total, 0.0)
        sums[1] += jnp.where(side[query : query + 1] < 0.0, total, 0.0)

    for query in range(queries // 2):
        add_query(query)

    features, slots = bins_ref.shape
    packed[...] = jnp.full(packed.shape, -1.0, jnp.float32)
    take.wait()
    lane = lax.broadcasted_iota(jnp.int32, (1, POS), 1)
    start = jnp.int32(0)
    for query in range(queries):
        group = start // POS
        shift = start - group * POS
        length = lengths_ref[query]
        moved = pltpu.roll(
            bins_ref[:, query * POS : (query + 1) * POS].astype(jnp.float32), shift, 1
        )
        here = (lane >= shift) & (lane < shift + length)
        there = lane < shift + length - POS
        packed[group] = jnp.where(here, moved, packed[group])
        packed[group + 1] = jnp.where(there, moved, packed[group + 1])
        start += length
    for group in range(slots // POS):
        for owner in range(features // 2):
            sent_ref[owner, :, group * POS : (group + 1) * POS] = packed[
                group, 2 * owner : 2 * owner + 2
            ].astype(jnp.bfloat16)
    bulk = pl.ds(0, slots)
    give = pltpu.make_async_copy(sent_ref.at[:, :, bulk], sent_to.at[:, :, bulk], gave.at[0])
    give.start()
    for query in range(queries // 2, queries):
        add_query(query)
    for at, part in enumerate(sums):
        high = part.astype(jnp.bfloat16).astype(jnp.float32)
        pieces = jnp.concatenate([high, part - high], axis=0).astype(jnp.bfloat16)
        sent_ref[:, :, slots + at * POS : slots + (at + 1) * POS] = jnp.broadcast_to(
            pieces[None], (features // 2, 2, POS)
        )
    small = pl.ds(slots, 2 * POS)
    give_sums = pltpu.make_async_copy(
        sent_ref.at[:, :, small], sent_to.at[:, :, small], gave.at[1]
    )
    give_sums.start()
    give.wait()
    give_sums.wait()


def ready_kernel(gap_ref, scores_ref, clicks_ref, lengths_ref, first_ref, second_ref, side_ref,
                 scale_ref, held_ref):
    queries = scores_ref.shape[0]
    _, _, side, signed, ideal = query_rows(
        scores_ref[...], clicks_ref[...], lengths_ref, queries, gap_ref[POS : POS + 1]
    )
    side_ref[...] = side
    scale_ref[...] = jnp.broadcast_to(1.0 / ideal, scale_ref.shape)
    columns = turned([signed, side])
    for query in range(queries):
        held_ref[query] = lengths_ref[query]
        spread = columns[:, query : query + 1] + signed[query : query + 1]
        cross = columns[:, queries + query : queries + query + 1] * side[query : query + 1]
        grown = jnp.exp(spread)
        chance = 1.0 / (1.0 + grown)
        first = jnp.where(cross < 0.0, gap_ref[:POS] * chance, 0.0)
        first_ref[query] = first
        second_ref[query] = first * (grown * chance)


def lambda_kernel(first_ref, second_ref, own_ref, scale_ref, held_ref, leaf_ref, data_ref,
                  plus_ref, minus_ref, grad_ref, side_ref, packed, flat):
    queries = own_ref.shape[0]
    slots = grad_ref.shape[1]
    sums = jnp.sum(data_ref[:, :, slots:].astype(jnp.float32), axis=0)
    sums = sums[0:1] + sums[1:2]
    plus_sum = sums[:, :POS]
    minus_sum = sums[:, POS:]
    plus = jnp.sqrt(plus_sum / plus_sum[:, 0:1])
    minus = jnp.sqrt(minus_sum / minus_sum[:, 0:1])
    plus_ref[...] = plus
    minus_ref[...] = minus
    side = own_ref[...]
    weight = jnp.where(side > 0.0, 1.0 / plus, jnp.where(side < 0.0, 1.0 / minus, 0.0))
    columns = turned([weight])
    outer = weight * scale_ref[...]
    packed[...] = jnp.zeros_like(packed)
    lane = lax.broadcasted_iota(jnp.int32, (1, POS), 1)
    start = jnp.int32(0)
    for query in range(queries):
        strength = columns[:, query : query + 1]
        slope = jnp.sum(strength * first_ref[query], axis=0, keepdims=True)
        curve = jnp.sum(strength * second_ref[query], axis=0, keepdims=True)
        slope = slope * outer[query : query + 1] * -side[query : query + 1]
        curve = curve * outer[query : query + 1]
        grad_ref[0:1, query * POS : (query + 1) * POS] = slope
        grad_ref[1:2, query * POS : (query + 1) * POS] = curve
        group = start // POS
        shift = start - group * POS
        length = held_ref[query]
        rows = jnp.concatenate(
            [slope, curve, leaf_ref[query : query + 1].astype(jnp.float32),
             jnp.zeros((5, POS), jnp.float32)], axis=0
        )
        moved = pltpu.roll(rows, shift, 1)
        here = (lane >= shift) & (lane < shift + length)
        there = lane < shift + length - POS
        packed[group] = jnp.where(here, moved, packed[group])
        packed[group + 1] = jnp.where(there, moved, packed[group + 1])
        start += length
    for group in range(queries):
        rows = packed[group]
        row = group // (queries // 2)
        at = (queries + group % (queries // 2)) * POS
        flat[:, group * POS : (group + 1) * POS] = rows[0:2]
        flat[row : row + 1, at : at + POS] = rows[2:3]
    side_ref[...] = jnp.broadcast_to(flat[...].astype(jnp.bfloat16)[None], side_ref.shape)


def plan_kernel(
    filled_ref, plus_in, minus_in, grad_in, list_ref, total_ref, plus_ref, minus_ref, grad_ref
):
    plus_ref[...] = plus_in[...]
    minus_ref[...] = minus_in[...]
    grad_ref[...] = grad_in[...]
    chips = filled_ref.shape[0] // 2
    groups = (list_ref.shape[0] // 2 - 2 * STEP) // chips
    for core in range(2):
        base = core * (chips * groups + 2 * STEP)

        def one_block(chip, carry):
            at, spare = carry
            used = filled_ref[2 * chip + core]
            for group in range(groups):
                list_ref[base + at] = chip * 16 + group
                at = at + jnp.where(group < used, 1, 0)
            return at, jnp.where(used < groups, chip * 16 + groups - 1, spare)

        at, spare = lax.fori_loop(0, chips, one_block, (jnp.int32(0), jnp.int32(0)))
        for extra in range(2 * STEP):
            list_ref[base + at + extra] = spare
        total_ref[core] = (at + 2 * STEP - 1) // (2 * STEP)


def accumulate(core, list_ref, total_ref, data_ref, side_ref, accs):
    base = core * (list_ref.shape[0] // 2)
    groups = side_ref.shape[2] * 2 // (3 * POS)
    rows_a = lax.broadcasted_iota(jnp.int32, (2 * LEAVES, TILE), 0).astype(jnp.bfloat16)
    rows_b = lax.broadcasted_iota(jnp.int32, (HALF, TILE), 0).astype(jnp.bfloat16)
    zero = jnp.zeros((), jnp.bfloat16)
    one = jnp.ones((), jnp.bfloat16)

    def tiles_at(first, count):
        for at in range(count):
            bins = []
            sides = []
            leaves = []
            for half in range(2):
                entry = list_ref[base + (first + at) * 2 + half]
                chip = lax.shift_right_logical(entry, 4)
                group = lax.bitwise_and(entry, 15)
                late = group >= groups // 2
                place = groups + group - jnp.where(late, groups // 2, 0)
                here = pl.ds(pl.multiple_of(group * POS, POS), POS)
                bins.append(data_ref[2 * chip + core, :, here])
                sides.append(side_ref[chip, :, here])
                pair = side_ref[chip, :, pl.ds(pl.multiple_of(place * POS, POS), POS)]
                leaves.append(jnp.where(late, pair[1:2], pair[0:1]))
            bins = jnp.concatenate(bins, axis=1)
            side = jnp.concatenate(sides, axis=1)
            leaf = jnp.concatenate(leaves, axis=1)
            left = []
            right = []
            for feature in range(2):
                row = bins[feature : feature + 1]
                high = row >= jnp.asarray(HALF, jnp.bfloat16)
                hit = jnp.where(high, leaf + jnp.asarray(LEAVES, jnp.bfloat16), leaf) == rows_a
                low = jnp.where(high, row - jnp.asarray(HALF, jnp.bfloat16), row)
                left.append(jnp.where(hit, side[0:1], zero))
                left.append(jnp.where(hit, side[1:2], zero))
                right.append(jnp.where(low == rows_b, one, zero))
            unit = at % 2
            register = (at // 2) % 2
            pltpu.matmul_push_rhs(jnp.concatenate(right, axis=0), register, unit, transpose=True)
            pltpu.matmul_acc_lhs(accs[unit], jnp.concatenate(left, axis=0), register)

    def wide_step(step, carry):
        tiles_at(step * (STEP * WIDE), STEP * WIDE)
        return carry

    def step(step, carry):
        tiles_at(step * STEP, STEP)
        return carry

    total = total_ref[core]
    wide = total // WIDE
    lax.fori_loop(0, wide, wide_step, 0)
    lax.fori_loop(wide * WIDE, total, step, 0)


def summed(core, list_ref, total_ref, data_ref, side_ref, finish):
    def run(acc_a, acc_b):
        accumulate(core, list_ref, total_ref, data_ref, side_ref, (acc_a, acc_b))
        finish(pltpu.matmul_pop(acc_a) + pltpu.matmul_pop(acc_b))

    shape = (8 * LEAVES, BINS)
    pl.run_scoped(run, pltpu.ACC(0)(shape, jnp.float32), pltpu.ACC(1)(shape, jnp.float32))


def first_kernel(core_ref, list_ref, total_ref, data_ref, side_ref, out_ref):
    rows = 4 * LEAVES

    def finish(total):
        for feature in range(2):
            out_ref[feature] = total[
                feature * rows : (feature + 1) * rows, feature * HALF : (feature + 1) * HALF
            ]

    summed(core_ref[0], list_ref, total_ref, data_ref, side_ref, finish)


def second_kernel(core_ref, list_ref, total_ref, data_ref, side_ref, before_ref, out_ref):
    rows = 4 * LEAVES

    def finish(total):
        for feature in range(2):
            mine = total[
                feature * rows : (feature + 1) * rows, feature * HALF : (feature + 1) * HALF
            ] + before_ref[feature]
            for which in range(2):
                for high in range(2):
                    at = (2 * which + high) * LEAVES
                    out_ref[
                        feature,
                        which * LEAVES : (which + 1) * LEAVES,
                        high * HALF : (high + 1) * HALF,
                    ] = mine[at : at + LEAVES]

    summed(core_ref[0], list_ref, total_ref, data_ref, side_ref, finish)


VMEM = pl.BlockSpec(memory_space=pltpu.VMEM)
SMEM = pl.BlockSpec(memory_space=pltpu.SMEM)


def in_vmem(array):
    return pltpu.with_memory_space_constraint(array, pltpu.VMEM)


def in_smem(array):
    return pltpu.with_memory_space_constraint(array, pltpu.SMEM)


def hist_of(core, plan, data, side, before=None):
    part = (2, 4 * LEAVES, HALF)
    if before is None:
        return pl.pallas_call(
            first_kernel,
            out_shape=pltpu.VMEM(part, jnp.float32),
            in_specs=[SMEM, SMEM, SMEM, VMEM, VMEM],
            out_specs=VMEM,
            name="first_half",
        )(core, *plan, data, side)
    return pl.pallas_call(
        second_kernel,
        out_shape=jax.ShapeDtypeStruct((2, 2 * LEAVES, BINS), jnp.float32),
        in_specs=[SMEM, SMEM, SMEM, VMEM, VMEM, VMEM],
        out_specs=VMEM,
        name="second_half",
    )(core, *plan, data, side, before)


def body(scores, clicks, lengths, t_plus_old, t_minus_old, leaf, bins):
    shards = lax.axis_size("doc")
    queries = scores.shape[0]
    slots = leaf.shape[0]
    groups = slots // POS
    places = np.arange(POS, dtype=np.float32)
    discount = (1.0 / np.log2(2.0 + places)).astype(np.float32)
    gap = np.abs(discount[:, None] - discount[None, :])
    gap = jnp.asarray(np.concatenate([gap, np.tile(discount[None], (8, 1))]))
    f32 = jnp.float32
    sent_shape = (shards, 2, slots + 2 * POS)
    sent = pl.pallas_call(
        pair_kernel,
        out_shape=jax.ShapeDtypeStruct(sent_shape, jnp.bfloat16),
        in_specs=[VMEM, VMEM, VMEM, SMEM, VMEM, VMEM, pl.BlockSpec(memory_space=pl.ANY)],
        out_specs=pl.BlockSpec(memory_space=pl.ANY),
        scratch_shapes=[
            pltpu.VMEM(bins.shape, jnp.int32),
            pltpu.VMEM(sent_shape, jnp.bfloat16),
            pltpu.VMEM((slots // POS + 1, bins.shape[0], POS), f32),
            pltpu.SemaphoreType.DMA,
            pltpu.SemaphoreType.DMA((2,)),
        ],
        name="pair_terms",
    )(gap, scores, clicks, lengths, t_plus_old[None], t_minus_old[None], bins)
    data = lax.all_to_all(sent, "doc", 0, 0, tiled=True)
    first, second, own, scale, held = pl.pallas_call(
        ready_kernel,
        out_shape=(
            pltpu.VMEM((queries, POS, POS), f32),
            pltpu.VMEM((queries, POS, POS), f32),
            pltpu.VMEM((queries, POS), f32),
            pltpu.VMEM((queries, POS), f32),
            pltpu.SMEM((queries,), jnp.int32),
        ),
        in_specs=[VMEM, VMEM, VMEM, SMEM],
        out_specs=(VMEM, VMEM, VMEM, VMEM, SMEM),
        name="ready_pairs",
    )(gap, scores, clicks, lengths)
    t_plus, t_minus, gradients, side = pl.pallas_call(
        lambda_kernel,
        out_shape=(
            pltpu.VMEM((1, POS), f32),
            pltpu.VMEM((1, POS), f32),
            pltpu.VMEM((2, slots), f32),
            pltpu.VMEM((shards // 2, 2, 3 * slots // 2), jnp.bfloat16),
        ),
        in_specs=[VMEM, VMEM, VMEM, VMEM, SMEM, VMEM, VMEM],
        out_specs=(VMEM,) * 4,
        scratch_shapes=[
            pltpu.VMEM((queries + 1, 8, POS), f32),
            pltpu.VMEM((2, 3 * slots // 2), f32),
        ],
        name="lambdas",
    )(
        in_vmem(first),
        in_vmem(second),
        in_vmem(own),
        in_vmem(scale),
        in_smem(held),
        in_vmem(leaf.reshape(queries, POS)),
        in_vmem(data),
    )
    same_core = [[2 * chip + core for chip in range(shards // 2)] for core in range(2)]
    side = lax.all_to_all(side, "doc", 0, 0, axis_index_groups=same_core, tiled=True)
    shown = jnp.sum((data[:, 0, :slots] >= 0).astype(f32), axis=1).astype(jnp.int32)
    *plan, t_plus, t_minus, gradients = pl.pallas_call(
        plan_kernel,
        out_shape=(
            pltpu.SMEM((shards * groups + 4 * STEP,), jnp.int32),
            pltpu.SMEM((2,), jnp.int32),
            jax.ShapeDtypeStruct((1, POS), f32),
            jax.ShapeDtypeStruct((1, POS), f32),
            jax.ShapeDtypeStruct((2, slots), f32),
        ),
        in_specs=[SMEM, VMEM, VMEM, VMEM],
        out_specs=(SMEM, SMEM, VMEM, VMEM, VMEM),
        name="plan",
    )((shown + (POS - 1)) // POS, in_vmem(t_plus), in_vmem(t_minus), in_vmem(gradients))
    other_side = lax.ppermute(side, "doc", [(at, at ^ 1) for at in range(shards)])
    core = lax.axis_index("doc") % 2
    partial = hist_of(core.reshape(1), plan, in_vmem(data), in_vmem(side))
    hist = hist_of((1 - core).reshape(1), plan, in_vmem(data), in_vmem(other_side), in_vmem(partial))
    return (t_plus[0], t_minus[0], gradients, hist)


def solution(mesh):
    placed = (P("doc", None), P("doc", None), P("doc"), P(), P(), P("doc"), P("feat", "doc"))
    return jax.shard_map(
        body,
        mesh=mesh,
        in_specs=placed,
        out_specs=(P(), P(), P(None, "doc"), P(("feat", "doc"), None, None)),
        check_vma=False,
    )
```

```python
import jax
import jax.numpy as jnp
import numpy as np
from jax import lax
from jax.experimental import pallas as pl
from jax.experimental.pallas import tpu as pltpu
from jax.sharding import PartitionSpec as P


BINS = 256
LEAVES = 32
POS = 128
HALF = BINS // 2
TILE = 256
STEP = 4
WIDE = 4


def query_rows(scores, clicks, lengths_ref, queries, discount_row):
    lane = lax.broadcasted_iota(jnp.int32, (queries, POS), 1)
    row = lax.broadcasted_iota(jnp.int32, (queries, POS), 0)
    length = jnp.zeros((queries, POS), jnp.int32)
    for query in range(queries):
        length = jnp.where(row == query, lengths_ref[query], length)
    shown = lane < length
    clicked = shown & (clicks == 1)
    skipped = shown & (clicks == 0)
    count = jnp.sum(jnp.where(clicked, 1.0, 0.0), axis=1, keepdims=True)
    ideal = jnp.sum(
        jnp.where(lane.astype(jnp.float32) < count, discount_row, 0.0), axis=1, keepdims=True
    )
    ideal = jnp.maximum(ideal, 1.0)
    side = jnp.where(clicked, 1.0, jnp.where(skipped, -1.0, 0.0))
    return clicked, skipped, side, side * scores, ideal


def turned(rows):
    queries = rows[0].shape[0]
    pad = jnp.zeros((POS - queries * len(rows), POS), jnp.float32)
    return jnp.transpose(jnp.concatenate(list(rows) + [pad], axis=0))


def pair_kernel(gap_ref, scores_ref, clicks_ref, lengths_ref, plus_ref, minus_ref, bins_from,
                sent_to, bins_ref, sent_ref, packed, took, gave):
    take = pltpu.make_async_copy(bins_from, bins_ref, took)
    take.start()
    queries = scores_ref.shape[0]
    clicked, skipped, side, signed, ideal = query_rows(
        scores_ref[...], clicks_ref[...], lengths_ref, queries, gap_ref[POS : POS + 1]
    )
    weight = jnp.where(clicked, 1.0 / plus_ref[...], jnp.where(skipped, -1.0 / minus_ref[...], 0.0))
    columns = turned([signed, weight])
    scale = 1.0 / ideal
    sums = [jnp.zeros((1, POS), jnp.float32), jnp.zeros((1, POS), jnp.float32)]

    def add_query(query):
        other = columns[:, query : query + 1]
        strength = columns[:, queries + query : queries + query + 1]
        spread = other + signed[query : query + 1]
        cross = jnp.maximum(strength * -side[query : query + 1], 0.0)
        loss = jnp.maximum(-spread, 0.0) + jnp.log1p(jnp.exp(-jnp.abs(spread)))
        total = jnp.sum(cross * gap_ref[:POS] * loss, axis=0, keepdims=True)
        total = total * scale[query : query + 1]
        sums[0] += jnp.where(side[query : query + 1] > 0.0, total, 0.0)
        sums[1] += jnp.where(side[query : query + 1] < 0.0, total, 0.0)

    for query in range(queries):
        add_query(query)

    features, slots = bins_ref.shape
    owners = features // 2
    for at, part in enumerate(sums):
        high = part.astype(jnp.bfloat16).astype(jnp.float32)
        pieces = jnp.concatenate([high, part - high], axis=0).astype(jnp.bfloat16)
        sent_ref[:, :, slots + at * POS : slots + (at + 1) * POS] = jnp.broadcast_to(
            pieces[None], (owners, 2, POS)
        )
    packed[...] = jnp.full(packed.shape, -1.0, jnp.float32)
    take.wait()
    lane = lax.broadcasted_iota(jnp.int32, (1, POS), 1)
    start = jnp.int32(0)
    for query in range(queries):
        group = start // POS
        shift = start - group * POS
        length = lengths_ref[query]
        moved = pltpu.roll(
            bins_ref[:, query * POS : (query + 1) * POS].astype(jnp.float32), shift, 1
        )
        here = (lane >= shift) & (lane < shift + length)
        there = lane < shift + length - POS
        packed[group] = jnp.where(here, moved, packed[group])
        packed[group + 1] = jnp.where(there, moved, packed[group + 1])
        start += length
    chunks = gave.shape[0]
    gives = []
    for chunk in range(chunks):
        first = chunk * owners // chunks
        for owner in range(first, first + owners // chunks):
            for group in range(slots // POS):
                sent_ref[owner, :, group * POS : (group + 1) * POS] = packed[
                    group, 2 * owner : 2 * owner + 2
                ].astype(jnp.bfloat16)
        some = pl.ds(first, owners // chunks)
        gives.append(pltpu.make_async_copy(sent_ref.at[some], sent_to.at[some], gave.at[chunk]))
        gives[-1].start()
    for give in gives:
        give.wait()


def ready_kernel(gap_ref, scores_ref, clicks_ref, lengths_ref, first_ref, second_ref, side_ref,
                 scale_ref, held_ref):
    queries = scores_ref.shape[0]
    _, _, side, signed, ideal = query_rows(
        scores_ref[...], clicks_ref[...], lengths_ref, queries, gap_ref[POS : POS + 1]
    )
    side_ref[...] = side
    scale_ref[...] = jnp.broadcast_to(1.0 / ideal, scale_ref.shape)
    columns = turned([signed, side])
    for query in range(queries):
        held_ref[query] = lengths_ref[query]
        spread = columns[:, query : query + 1] + signed[query : query + 1]
        cross = columns[:, queries + query : queries + query + 1] * side[query : query + 1]
        grown = jnp.exp(spread)
        chance = 1.0 / (1.0 + grown)
        first = jnp.where(cross < 0.0, gap_ref[:POS] * chance, 0.0)
        first_ref[query] = first
        second_ref[query] = first * (grown * chance)


def lambda_kernel(first_ref, second_ref, own_ref, scale_ref, held_ref, leaf_ref, data_ref,
                  plus_ref, minus_ref, grad_ref, side_ref, packed, flat):
    queries = own_ref.shape[0]
    slots = grad_ref.shape[1]
    sums = jnp.sum(data_ref[:, :, slots:].astype(jnp.float32), axis=0)
    sums = sums[0:1] + sums[1:2]
    plus_sum = sums[:, :POS]
    minus_sum = sums[:, POS:]
    plus = jnp.sqrt(plus_sum / plus_sum[:, 0:1])
    minus = jnp.sqrt(minus_sum / minus_sum[:, 0:1])
    plus_ref[...] = plus
    minus_ref[...] = minus
    side = own_ref[...]
    weight = jnp.where(side > 0.0, 1.0 / plus, jnp.where(side < 0.0, 1.0 / minus, 0.0))
    columns = turned([weight])
    outer = weight * scale_ref[...]
    packed[...] = jnp.zeros_like(packed)
    lane = lax.broadcasted_iota(jnp.int32, (1, POS), 1)
    start = jnp.int32(0)
    for query in range(queries):
        strength = columns[:, query : query + 1]
        slope = jnp.sum(strength * first_ref[query], axis=0, keepdims=True)
        curve = jnp.sum(strength * second_ref[query], axis=0, keepdims=True)
        slope = slope * outer[query : query + 1] * -side[query : query + 1]
        curve = curve * outer[query : query + 1]
        grad_ref[0:1, query * POS : (query + 1) * POS] = slope
        grad_ref[1:2, query * POS : (query + 1) * POS] = curve
        group = start // POS
        shift = start - group * POS
        length = held_ref[query]
        rows = jnp.concatenate(
            [slope, curve, leaf_ref[query : query + 1].astype(jnp.float32),
             jnp.zeros((5, POS), jnp.float32)], axis=0
        )
        moved = pltpu.roll(rows, shift, 1)
        here = (lane >= shift) & (lane < shift + length)
        there = lane < shift + length - POS
        packed[group] = jnp.where(here, moved, packed[group])
        packed[group + 1] = jnp.where(there, moved, packed[group + 1])
        start += length
    for group in range(queries):
        rows = packed[group]
        row = group // (queries // 2)
        at = (queries + group % (queries // 2)) * POS
        flat[:, group * POS : (group + 1) * POS] = rows[0:2]
        flat[row : row + 1, at : at + POS] = rows[2:3]
    side_ref[...] = jnp.broadcast_to(flat[...].astype(jnp.bfloat16)[None], side_ref.shape)


def plan_kernel(
    filled_ref, plus_in, minus_in, grad_in, list_ref, total_ref, plus_ref, minus_ref, grad_ref
):
    plus_ref[...] = plus_in[...]
    minus_ref[...] = minus_in[...]
    grad_ref[...] = grad_in[...]
    chips = filled_ref.shape[0] // 2
    groups = (list_ref.shape[0] // 2 - 2 * STEP) // chips
    for core in range(2):
        base = core * (chips * groups + 2 * STEP)

        def one_block(chip, carry):
            at, spare = carry
            used = filled_ref[2 * chip + core]
            for group in range(groups):
                list_ref[base + at] = chip * 16 + group
                at = at + jnp.where(group < used, 1, 0)
            return at, jnp.where(used < groups, chip * 16 + groups - 1, spare)

        at, spare = lax.fori_loop(0, chips, one_block, (jnp.int32(0), jnp.int32(0)))
        for extra in range(2 * STEP):
            list_ref[base + at + extra] = spare
        total_ref[core] = (at + 2 * STEP - 1) // (2 * STEP)


def accumulate(core, list_ref, total_ref, data_ref, side_ref, accs):
    base = core * (list_ref.shape[0] // 2)
    groups = side_ref.shape[2] * 2 // (3 * POS)
    rows_a = lax.broadcasted_iota(jnp.int32, (2 * LEAVES, TILE), 0).astype(jnp.bfloat16)
    rows_b = lax.broadcasted_iota(jnp.int32, (HALF, TILE), 0).astype(jnp.bfloat16)
    zero = jnp.zeros((), jnp.bfloat16)
    one = jnp.ones((), jnp.bfloat16)

    def tiles_at(first, count):
        for at in range(count):
            bins = []
            sides = []
            leaves = []
            for half in range(2):
                entry = list_ref[base + (first + at) * 2 + half]
                chip = lax.shift_right_logical(entry, 4)
                group = lax.bitwise_and(entry, 15)
                late = group >= groups // 2
                place = groups + group - jnp.where(late, groups // 2, 0)
                here = pl.ds(pl.multiple_of(group * POS, POS), POS)
                bins.append(data_ref[2 * chip + core, :, here])
                sides.append(side_ref[chip, :, here])
                pair = side_ref[chip, :, pl.ds(pl.multiple_of(place * POS, POS), POS)]
                leaves.append(jnp.where(late, pair[1:2], pair[0:1]))
            bins = jnp.concatenate(bins, axis=1)
            side = jnp.concatenate(sides, axis=1)
            leaf = jnp.concatenate(leaves, axis=1)
            left = []
            right = []
            for feature in range(2):
                row = bins[feature : feature + 1]
                high = row >= jnp.asarray(HALF, jnp.bfloat16)
                hit = jnp.where(high, leaf + jnp.asarray(LEAVES, jnp.bfloat16), leaf) == rows_a
                low = jnp.where(high, row - jnp.asarray(HALF, jnp.bfloat16), row)
                left.append(jnp.where(hit, side[0:1], zero))
                left.append(jnp.where(hit, side[1:2], zero))
                right.append(jnp.where(low == rows_b, one, zero))
            unit = at % 2
            register = (at // 2) % 2
            pltpu.matmul_push_rhs(jnp.concatenate(right, axis=0), register, unit, transpose=True)
            pltpu.matmul_acc_lhs(accs[unit], jnp.concatenate(left, axis=0), register)

    def wide_step(step, carry):
        tiles_at(step * (STEP * WIDE), STEP * WIDE)
        return carry

    def step(step, carry):
        tiles_at(step * STEP, STEP)
        return carry

    total = total_ref[core]
    wide = total // WIDE
    lax.fori_loop(0, wide, wide_step, 0)
    lax.fori_loop(wide * WIDE, total, step, 0)


def summed(core, list_ref, total_ref, data_ref, side_ref, finish):
    def run(acc_a, acc_b):
        accumulate(core, list_ref, total_ref, data_ref, side_ref, (acc_a, acc_b))
        finish(pltpu.matmul_pop(acc_a) + pltpu.matmul_pop(acc_b))

    shape = (8 * LEAVES, BINS)
    pl.run_scoped(run, pltpu.ACC(0)(shape, jnp.float32), pltpu.ACC(1)(shape, jnp.float32))


def first_kernel(core_ref, list_ref, total_ref, data_ref, side_ref, out_ref):
    rows = 4 * LEAVES

    def finish(total):
        for feature in range(2):
            out_ref[feature] = total[
                feature * rows : (feature + 1) * rows, feature * HALF : (feature + 1) * HALF
            ]

    summed(core_ref[0], list_ref, total_ref, data_ref, side_ref, finish)


def second_kernel(core_ref, list_ref, total_ref, data_ref, side_ref, before_ref, out_ref):
    rows = 4 * LEAVES

    def finish(total):
        for feature in range(2):
            mine = total[
                feature * rows : (feature + 1) * rows, feature * HALF : (feature + 1) * HALF
            ] + before_ref[feature]
            for which in range(2):
                for high in range(2):
                    at = (2 * which + high) * LEAVES
                    out_ref[
                        feature,
                        which * LEAVES : (which + 1) * LEAVES,
                        high * HALF : (high + 1) * HALF,
                    ] = mine[at : at + LEAVES]

    summed(core_ref[0], list_ref, total_ref, data_ref, side_ref, finish)


VMEM = pl.BlockSpec(memory_space=pltpu.VMEM)
SMEM = pl.BlockSpec(memory_space=pltpu.SMEM)


def in_vmem(array):
    return pltpu.with_memory_space_constraint(array, pltpu.VMEM)


def in_smem(array):
    return pltpu.with_memory_space_constraint(array, pltpu.SMEM)


def hist_of(core, plan, data, side, before=None):
    part = (2, 4 * LEAVES, HALF)
    if before is None:
        return pl.pallas_call(
            first_kernel,
            out_shape=pltpu.VMEM(part, jnp.float32),
            in_specs=[SMEM, SMEM, SMEM, VMEM, VMEM],
            out_specs=VMEM,
            name="first_half",
        )(core, *plan, data, side)
    return pl.pallas_call(
        second_kernel,
        out_shape=jax.ShapeDtypeStruct((2, 2 * LEAVES, BINS), jnp.float32),
        in_specs=[SMEM, SMEM, SMEM, VMEM, VMEM, VMEM],
        out_specs=VMEM,
        name="second_half",
    )(core, *plan, data, side, before)


def body(scores, clicks, lengths, t_plus_old, t_minus_old, leaf, bins):
    shards = lax.axis_size("doc")
    queries = scores.shape[0]
    slots = leaf.shape[0]
    groups = slots // POS
    places = np.arange(POS, dtype=np.float32)
    discount = (1.0 / np.log2(2.0 + places)).astype(np.float32)
    gap = np.abs(discount[:, None] - discount[None, :])
    gap = jnp.asarray(np.concatenate([gap, np.tile(discount[None], (8, 1))]))
    f32 = jnp.float32
    sent_shape = (shards, 2, slots + 2 * POS)
    sent = pl.pallas_call(
        pair_kernel,
        out_shape=jax.ShapeDtypeStruct(sent_shape, jnp.bfloat16),
        in_specs=[VMEM, VMEM, VMEM, SMEM, VMEM, VMEM, pl.BlockSpec(memory_space=pl.ANY)],
        out_specs=pl.BlockSpec(memory_space=pl.ANY),
        scratch_shapes=[
            pltpu.VMEM(bins.shape, jnp.int32),
            pltpu.VMEM(sent_shape, jnp.bfloat16),
            pltpu.VMEM((slots // POS + 1, bins.shape[0], POS), f32),
            pltpu.SemaphoreType.DMA,
            pltpu.SemaphoreType.DMA((4,)),
        ],
        name="pair_terms",
    )(gap, scores, clicks, lengths, t_plus_old[None], t_minus_old[None], bins)
    data = lax.all_to_all(sent, "doc", 0, 0, tiled=True)
    first, second, own, scale, held = pl.pallas_call(
        ready_kernel,
        out_shape=(
            pltpu.VMEM((queries, POS, POS), f32),
            pltpu.VMEM((queries, POS, POS), f32),
            pltpu.VMEM((queries, POS), f32),
            pltpu.VMEM((queries, POS), f32),
            pltpu.SMEM((queries,), jnp.int32),
        ),
        in_specs=[VMEM, VMEM, VMEM, SMEM],
        out_specs=(VMEM, VMEM, VMEM, VMEM, SMEM),
        name="ready_pairs",
    )(gap, scores, clicks, lengths)
    t_plus, t_minus, gradients, side = pl.pallas_call(
        lambda_kernel,
        out_shape=(
            pltpu.VMEM((1, POS), f32),
            pltpu.VMEM((1, POS), f32),
            pltpu.VMEM((2, slots), f32),
            pltpu.VMEM((shards // 2, 2, 3 * slots // 2), jnp.bfloat16),
        ),
        in_specs=[VMEM, VMEM, VMEM, VMEM, SMEM, VMEM, VMEM],
        out_specs=(VMEM,) * 4,
        scratch_shapes=[
            pltpu.VMEM((queries + 1, 8, POS), f32),
            pltpu.VMEM((2, 3 * slots // 2), f32),
        ],
        name="lambdas",
    )(
        in_vmem(first),
        in_vmem(second),
        in_vmem(own),
        in_vmem(scale),
        in_smem(held),
        in_vmem(leaf.reshape(queries, POS)),
        in_vmem(data),
    )
    same_core = [[2 * chip + core for chip in range(shards // 2)] for core in range(2)]
    side = lax.all_to_all(side, "doc", 0, 0, axis_index_groups=same_core, tiled=True)
    shown = jnp.sum((data[:, 0, :slots] >= 0).astype(f32), axis=1).astype(jnp.int32)
    *plan, t_plus, t_minus, gradients = pl.pallas_call(
        plan_kernel,
        out_shape=(
            pltpu.SMEM((shards * groups + 4 * STEP,), jnp.int32),
            pltpu.SMEM((2,), jnp.int32),
            jax.ShapeDtypeStruct((1, POS), f32),
            jax.ShapeDtypeStruct((1, POS), f32),
            jax.ShapeDtypeStruct((2, slots), f32),
        ),
        in_specs=[SMEM, VMEM, VMEM, VMEM],
        out_specs=(SMEM, SMEM, VMEM, VMEM, VMEM),
        name="plan",
    )((shown + (POS - 1)) // POS, in_vmem(t_plus), in_vmem(t_minus), in_vmem(gradients))
    other_side = lax.ppermute(side, "doc", [(at, at ^ 1) for at in range(shards)])
    core = lax.axis_index("doc") % 2
    partial = hist_of(core.reshape(1), plan, in_vmem(data), in_vmem(side))
    hist = hist_of((1 - core).reshape(1), plan, in_vmem(data), in_vmem(other_side), in_vmem(partial))
    return (t_plus[0], t_minus[0], gradients, hist)


def solution(mesh):
    placed = (P("doc", None), P("doc", None), P("doc"), P(), P(), P("doc"), P("feat", "doc"))
    return jax.shard_map(
        body,
        mesh=mesh,
        in_specs=placed,
        out_specs=(P(), P(), P(None, "doc"), P(("feat", "doc"), None, None)),
        check_vma=False,
    )
```

```python
import jax
import jax.numpy as jnp
import numpy as np
from jax import lax
from jax.experimental import pallas as pl
from jax.experimental.pallas import tpu as pltpu
from jax.sharding import PartitionSpec as P


BINS = 256
LEAVES = 32
POS = 128
HALF = BINS // 2
TILE = 256
STEP = 4
WIDE = 4
PARTS = 4


def query_rows(scores, clicks, lengths_ref, queries, discount_row):
    lane = lax.broadcasted_iota(jnp.int32, (queries, POS), 1)
    row = lax.broadcasted_iota(jnp.int32, (queries, POS), 0)
    length = jnp.zeros((queries, POS), jnp.int32)
    for query in range(queries):
        length = jnp.where(row == query, lengths_ref[query], length)
    shown = lane < length
    clicked = shown & (clicks == 1)
    skipped = shown & (clicks == 0)
    count = jnp.sum(jnp.where(clicked, 1.0, 0.0), axis=1, keepdims=True)
    ideal = jnp.sum(
        jnp.where(lane.astype(jnp.float32) < count, discount_row, 0.0), axis=1, keepdims=True
    )
    ideal = jnp.maximum(ideal, 1.0)
    side = jnp.where(clicked, 1.0, jnp.where(skipped, -1.0, 0.0))
    return clicked, skipped, side, side * scores, ideal


def turned(rows):
    queries = rows[0].shape[0]
    pad = jnp.zeros((POS - queries * len(rows), POS), jnp.float32)
    return jnp.transpose(jnp.concatenate(list(rows) + [pad], axis=0))


def pair_kernel(gap_ref, scores_ref, clicks_ref, lengths_ref, plus_ref, minus_ref, bins_from,
                sent_to, bins_ref, sent_ref, packed, took, gave):
    take = pltpu.make_async_copy(bins_from, bins_ref, took)
    take.start()
    queries = scores_ref.shape[0]
    clicked, skipped, side, signed, ideal = query_rows(
        scores_ref[...], clicks_ref[...], lengths_ref, queries, gap_ref[POS : POS + 1]
    )
    weight = jnp.where(clicked, 1.0 / plus_ref[...], jnp.where(skipped, -1.0 / minus_ref[...], 0.0))
    columns = turned([signed, weight])
    scale = 1.0 / ideal
    sums = [jnp.zeros((1, POS), jnp.float32), jnp.zeros((1, POS), jnp.float32)]

    def add_query(query):
        other = columns[:, query : query + 1]
        strength = columns[:, queries + query : queries + query + 1]
        spread = other + signed[query : query + 1]
        cross = jnp.maximum(strength * -side[query : query + 1], 0.0)
        loss = jnp.maximum(-spread, 0.0) + jnp.log1p(jnp.exp(-jnp.abs(spread)))
        total = jnp.sum(cross * gap_ref[:POS] * loss, axis=0, keepdims=True)
        total = total * scale[query : query + 1]
        sums[0] += jnp.where(side[query : query + 1] > 0.0, total, 0.0)
        sums[1] += jnp.where(side[query : query + 1] < 0.0, total, 0.0)

    for query in range(queries):
        add_query(query)

    features, slots = bins_ref.shape
    owners = features // 2
    for at, part in enumerate(sums):
        high = part.astype(jnp.bfloat16).astype(jnp.float32)
        pieces = jnp.concatenate([high, part - high], axis=0).astype(jnp.bfloat16)
        sent_ref[:, :, slots + at * POS : slots + (at + 1) * POS] = jnp.broadcast_to(
            pieces[None], (owners, 2, POS)
        )
    packed[...] = jnp.full(packed.shape, -1.0, jnp.float32)
    take.wait()
    lane = lax.broadcasted_iota(jnp.int32, (1, POS), 1)
    start = jnp.int32(0)
    for query in range(queries):
        group = start // POS
        shift = start - group * POS
        length = lengths_ref[query]
        moved = pltpu.roll(
            bins_ref[:, query * POS : (query + 1) * POS].astype(jnp.float32), shift, 1
        )
        here = (lane >= shift) & (lane < shift + length)
        there = lane < shift + length - POS
        packed[group] = jnp.where(here, moved, packed[group])
        packed[group + 1] = jnp.where(there, moved, packed[group + 1])
        start += length
    chunks = gave.shape[0]
    gives = []
    for chunk in range(chunks):
        first = chunk * owners // chunks
        for owner in range(first, first + owners // chunks):
            for group in range(slots // POS):
                sent_ref[owner, :, group * POS : (group + 1) * POS] = packed[
                    group, 2 * owner : 2 * owner + 2
                ].astype(jnp.bfloat16)
        some = pl.ds(first, owners // chunks)
        gives.append(pltpu.make_async_copy(sent_ref.at[some], sent_to.at[some], gave.at[chunk]))
        gives[-1].start()
    for give in gives:
        give.wait()


def ready_kernel(gap_ref, scores_ref, clicks_ref, lengths_ref, first_ref, second_ref, side_ref,
                 scale_ref, held_ref):
    queries = scores_ref.shape[0]
    _, _, side, signed, ideal = query_rows(
        scores_ref[...], clicks_ref[...], lengths_ref, queries, gap_ref[POS : POS + 1]
    )
    side_ref[...] = side
    scale_ref[...] = jnp.broadcast_to(1.0 / ideal, scale_ref.shape)
    columns = turned([signed, side])
    for query in range(queries):
        held_ref[query] = lengths_ref[query]
        spread = columns[:, query : query + 1] + signed[query : query + 1]
        cross = columns[:, queries + query : queries + query + 1] * side[query : query + 1]
        grown = jnp.exp(spread)
        chance = 1.0 / (1.0 + grown)
        first = jnp.where(cross < 0.0, gap_ref[:POS] * chance, 0.0)
        first_ref[query] = first
        second_ref[query] = first * (grown * chance)


def lambda_kernel(first_ref, second_ref, own_ref, scale_ref, held_ref, leaf_ref, data_ref,
                  plus_ref, minus_ref, grad_ref, side_ref, packed, flat):
    queries = own_ref.shape[0]
    slots = grad_ref.shape[1]
    sums = jnp.sum(data_ref[:, :, slots:].astype(jnp.float32), axis=0)
    sums = sums[0:1] + sums[1:2]
    plus_sum = sums[:, :POS]
    minus_sum = sums[:, POS:]
    plus = jnp.sqrt(plus_sum / plus_sum[:, 0:1])
    minus = jnp.sqrt(minus_sum / minus_sum[:, 0:1])
    plus_ref[...] = plus
    minus_ref[...] = minus
    side = own_ref[...]
    weight = jnp.where(side > 0.0, 1.0 / plus, jnp.where(side < 0.0, 1.0 / minus, 0.0))
    columns = turned([weight])
    outer = weight * scale_ref[...]
    packed[...] = jnp.zeros_like(packed)
    lane = lax.broadcasted_iota(jnp.int32, (1, POS), 1)
    start = jnp.int32(0)
    for query in range(queries):
        strength = columns[:, query : query + 1]
        slope = jnp.sum(strength * first_ref[query], axis=0, keepdims=True)
        curve = jnp.sum(strength * second_ref[query], axis=0, keepdims=True)
        slope = slope * outer[query : query + 1] * -side[query : query + 1]
        curve = curve * outer[query : query + 1]
        grad_ref[0:1, query * POS : (query + 1) * POS] = slope
        grad_ref[1:2, query * POS : (query + 1) * POS] = curve
        group = start // POS
        shift = start - group * POS
        length = held_ref[query]
        rows = jnp.concatenate(
            [slope, curve, leaf_ref[query : query + 1].astype(jnp.float32),
             jnp.zeros((5, POS), jnp.float32)], axis=0
        )
        moved = pltpu.roll(rows, shift, 1)
        here = (lane >= shift) & (lane < shift + length)
        there = lane < shift + length - POS
        packed[group] = jnp.where(here, moved, packed[group])
        packed[group + 1] = jnp.where(there, moved, packed[group + 1])
        start += length
    for group in range(queries):
        rows = packed[group]
        row = group // (queries // 2)
        at = (queries + group % (queries // 2)) * POS
        flat[:, group * POS : (group + 1) * POS] = rows[0:2]
        flat[row : row + 1, at : at + POS] = rows[2:3]
    side_ref[...] = jnp.broadcast_to(flat[...].astype(jnp.bfloat16)[None], side_ref.shape)


def plan_kernel(
    filled_ref, plus_in, minus_in, grad_in, list_ref, total_ref, plus_ref, minus_ref, grad_ref
):
    plus_ref[...] = plus_in[...]
    minus_ref[...] = minus_in[...]
    grad_ref[...] = grad_in[...]
    chips = filled_ref.shape[0] // PARTS
    groups = (list_ref.shape[0] // PARTS - 2 * STEP) // chips
    for core in range(PARTS):
        base = core * (chips * groups + 2 * STEP)

        def one_block(chip, carry):
            at, spare = carry
            used = filled_ref[PARTS * chip + core]
            for group in range(groups):
                list_ref[base + at] = chip * 16 + group
                at = at + jnp.where(group < used, 1, 0)
            return at, jnp.where(used < groups, chip * 16 + groups - 1, spare)

        at, spare = lax.fori_loop(0, chips, one_block, (jnp.int32(0), jnp.int32(0)))
        for extra in range(2 * STEP):
            list_ref[base + at + extra] = spare
        total_ref[core] = (at + 2 * STEP - 1) // (2 * STEP)


def accumulate(core, list_ref, total_ref, data_ref, side_ref, accs):
    base = core * (list_ref.shape[0] // PARTS)
    groups = side_ref.shape[2] * 2 // (3 * POS)
    rows_a = lax.broadcasted_iota(jnp.int32, (2 * LEAVES, TILE), 0).astype(jnp.bfloat16)
    rows_b = lax.broadcasted_iota(jnp.int32, (HALF, TILE), 0).astype(jnp.bfloat16)
    zero = jnp.zeros((), jnp.bfloat16)
    one = jnp.ones((), jnp.bfloat16)

    def tiles_at(first, count):
        for at in range(count):
            bins = []
            sides = []
            leaves = []
            for half in range(2):
                entry = list_ref[base + (first + at) * 2 + half]
                chip = lax.shift_right_logical(entry, 4)
                group = lax.bitwise_and(entry, 15)
                late = group >= groups // 2
                place = groups + group - jnp.where(late, groups // 2, 0)
                here = pl.ds(pl.multiple_of(group * POS, POS), POS)
                bins.append(data_ref[PARTS * chip + core, :, here])
                sides.append(side_ref[chip, :, here])
                pair = side_ref[chip, :, pl.ds(pl.multiple_of(place * POS, POS), POS)]
                leaves.append(jnp.where(late, pair[1:2], pair[0:1]))
            bins = jnp.concatenate(bins, axis=1)
            side = jnp.concatenate(sides, axis=1)
            leaf = jnp.concatenate(leaves, axis=1)
            left = []
            right = []
            for feature in range(2):
                row = bins[feature : feature + 1]
                high = row >= jnp.asarray(HALF, jnp.bfloat16)
                hit = jnp.where(high, leaf + jnp.asarray(LEAVES, jnp.bfloat16), leaf) == rows_a
                low = jnp.where(high, row - jnp.asarray(HALF, jnp.bfloat16), row)
                left.append(jnp.where(hit, side[0:1], zero))
                left.append(jnp.where(hit, side[1:2], zero))
                right.append(jnp.where(low == rows_b, one, zero))
            unit = at % 2
            register = (at // 2) % 2
            pltpu.matmul_push_rhs(jnp.concatenate(right, axis=0), register, unit, transpose=True)
            pltpu.matmul_acc_lhs(accs[unit], jnp.concatenate(left, axis=0), register)

    def wide_step(step, carry):
        tiles_at(step * (STEP * WIDE), STEP * WIDE)
        return carry

    def step(step, carry):
        tiles_at(step * STEP, STEP)
        return carry

    total = total_ref[core]
    wide = total // WIDE
    lax.fori_loop(0, wide, wide_step, 0)
    lax.fori_loop(wide * WIDE, total, step, 0)


def summed(core, list_ref, total_ref, data_ref, side_ref, finish):
    def run(acc_a, acc_b):
        accumulate(core, list_ref, total_ref, data_ref, side_ref, (acc_a, acc_b))
        finish(pltpu.matmul_pop(acc_a) + pltpu.matmul_pop(acc_b))

    shape = (8 * LEAVES, BINS)
    pl.run_scoped(run, pltpu.ACC(0)(shape, jnp.float32), pltpu.ACC(1)(shape, jnp.float32))


def part_kernel(core_ref, list_ref, total_ref, data_ref, side_ref, *refs):
    rows = 4 * LEAVES
    out_ref = refs[-1]

    def finish(total):
        for feature in range(2):
            mine = total[
                feature * rows : (feature + 1) * rows, feature * HALF : (feature + 1) * HALF
            ]
            out_ref[feature] = mine if len(refs) == 1 else mine + refs[0][feature]

    summed(core_ref[0], list_ref, total_ref, data_ref, side_ref, finish)


def last_kernel(core_ref, list_ref, total_ref, data_ref, side_ref, before_ref, out_ref):
    rows = 4 * LEAVES

    def finish(total):
        for feature in range(2):
            mine = total[
                feature * rows : (feature + 1) * rows, feature * HALF : (feature + 1) * HALF
            ] + before_ref[feature]
            for which in range(2):
                for high in range(2):
                    at = (2 * which + high) * LEAVES
                    out_ref[
                        feature,
                        which * LEAVES : (which + 1) * LEAVES,
                        high * HALF : (high + 1) * HALF,
                    ] = mine[at : at + LEAVES]

    summed(core_ref[0], list_ref, total_ref, data_ref, side_ref, finish)


VMEM = pl.BlockSpec(memory_space=pltpu.VMEM)
SMEM = pl.BlockSpec(memory_space=pltpu.SMEM)


def in_vmem(array):
    return pltpu.with_memory_space_constraint(array, pltpu.VMEM)


def in_smem(array):
    return pltpu.with_memory_space_constraint(array, pltpu.SMEM)


def hist_of(core, plan, data, side, before=None, last=False):
    given = [in_vmem(data), in_vmem(side)]
    if before is not None:
        given.append(in_vmem(before))
    if last:
        out_shape = jax.ShapeDtypeStruct((2, 2 * LEAVES, BINS), jnp.float32)
    else:
        out_shape = pltpu.VMEM((2, 4 * LEAVES, HALF), jnp.float32)
    return pl.pallas_call(
        last_kernel if last else part_kernel,
        out_shape=out_shape,
        in_specs=[SMEM, SMEM, SMEM] + [VMEM] * len(given),
        out_specs=VMEM,
        name="last_part" if last else "part",
    )(core.reshape(1), *plan, *given)


def body(scores, clicks, lengths, t_plus_old, t_minus_old, leaf, bins):
    shards = lax.axis_size("doc")
    queries = scores.shape[0]
    slots = leaf.shape[0]
    groups = slots // POS
    places = np.arange(POS, dtype=np.float32)
    discount = (1.0 / np.log2(2.0 + places)).astype(np.float32)
    gap = np.abs(discount[:, None] - discount[None, :])
    gap = jnp.asarray(np.concatenate([gap, np.tile(discount[None], (8, 1))]))
    f32 = jnp.float32
    sent_shape = (shards, 2, slots + 2 * POS)
    sent = pl.pallas_call(
        pair_kernel,
        out_shape=jax.ShapeDtypeStruct(sent_shape, jnp.bfloat16),
        in_specs=[VMEM, VMEM, VMEM, SMEM, VMEM, VMEM, pl.BlockSpec(memory_space=pl.ANY)],
        out_specs=pl.BlockSpec(memory_space=pl.ANY),
        scratch_shapes=[
            pltpu.VMEM(bins.shape, jnp.int32),
            pltpu.VMEM(sent_shape, jnp.bfloat16),
            pltpu.VMEM((slots // POS + 1, bins.shape[0], POS), f32),
            pltpu.SemaphoreType.DMA,
            pltpu.SemaphoreType.DMA((4,)),
        ],
        name="pair_terms",
    )(gap, scores, clicks, lengths, t_plus_old[None], t_minus_old[None], bins)
    data = lax.all_to_all(sent, "doc", 0, 0, tiled=True)
    first, second, own, scale, held = pl.pallas_call(
        ready_kernel,
        out_shape=(
            pltpu.VMEM((queries, POS, POS), f32),
            pltpu.VMEM((queries, POS, POS), f32),
            pltpu.VMEM((queries, POS), f32),
            pltpu.VMEM((queries, POS), f32),
            pltpu.SMEM((queries,), jnp.int32),
        ),
        in_specs=[VMEM, VMEM, VMEM, SMEM],
        out_specs=(VMEM, VMEM, VMEM, VMEM, SMEM),
        name="ready_pairs",
    )(gap, scores, clicks, lengths)
    t_plus, t_minus, gradients, side = pl.pallas_call(
        lambda_kernel,
        out_shape=(
            pltpu.VMEM((1, POS), f32),
            pltpu.VMEM((1, POS), f32),
            pltpu.VMEM((2, slots), f32),
            pltpu.VMEM((shards // PARTS, 2, 3 * slots // 2), jnp.bfloat16),
        ),
        in_specs=[VMEM, VMEM, VMEM, VMEM, SMEM, VMEM, VMEM],
        out_specs=(VMEM,) * 4,
        scratch_shapes=[
            pltpu.VMEM((queries + 1, 8, POS), f32),
            pltpu.VMEM((2, 3 * slots // 2), f32),
        ],
        name="lambdas",
    )(
        in_vmem(first),
        in_vmem(second),
        in_vmem(own),
        in_vmem(scale),
        in_smem(held),
        in_vmem(leaf.reshape(queries, POS)),
        in_vmem(data),
    )
    alike = [list(range(part, shards, PARTS)) for part in range(PARTS)]
    side = lax.all_to_all(side, "doc", 0, 0, axis_index_groups=alike, tiled=True)
    shown = jnp.sum((data[:, 0, :slots] >= 0).astype(f32), axis=1).astype(jnp.int32)
    *plan, t_plus, t_minus, gradients = pl.pallas_call(
        plan_kernel,
        out_shape=(
            pltpu.SMEM((shards * groups + 2 * PARTS * STEP,), jnp.int32),
            pltpu.SMEM((PARTS,), jnp.int32),
            jax.ShapeDtypeStruct((1, POS), f32),
            jax.ShapeDtypeStruct((1, POS), f32),
            jax.ShapeDtypeStruct((2, slots), f32),
        ),
        in_specs=[SMEM, VMEM, VMEM, VMEM],
        out_specs=(SMEM, SMEM, VMEM, VMEM, VMEM),
        name="plan",
    )((shown + (POS - 1)) // POS, in_vmem(t_plus), in_vmem(t_minus), in_vmem(gradients))
    swap = [[(at, at ^ bit) for at in range(shards)] for bit in (1, 2)]
    own = lax.rem(lax.axis_index("doc"), PARTS)
    side_far = lax.ppermute(side, "doc", swap[1])
    side_near = lax.ppermute(side, "doc", swap[0])
    side_last = lax.ppermute(side_far, "doc", swap[0])
    partial = hist_of(own, plan, data, side)
    partial = hist_of(lax.bitwise_xor(own, 1), plan, data, side_near, partial)
    partial = hist_of(lax.bitwise_xor(own, 2), plan, data, side_far, partial)
    hist = hist_of(lax.bitwise_xor(own, 3), plan, data, side_last, partial, True)
    return (t_plus[0], t_minus[0], gradients, hist)


def solution(mesh):
    placed = (P("doc", None), P("doc", None), P("doc"), P(), P(), P("doc"), P("feat", "doc"))
    return jax.shard_map(
        body,
        mesh=mesh,
        in_specs=placed,
        out_specs=(P(), P(), P(None, "doc"), P(("feat", "doc"), None, None)),
        check_vma=False,
    )
```

```python
import jax
import jax.numpy as jnp
import numpy as np
from jax import lax
from jax.experimental import pallas as pl
from jax.experimental.pallas import tpu as pltpu
from jax.sharding import PartitionSpec as P


BINS = 256
LEAVES = 32
POS = 128
HALF = BINS // 2
TILE = 256
STEP = 4
WIDE = 4
PARTS = 4


def query_rows(scores, clicks, lengths_ref, queries, discount_row):
    lane = lax.broadcasted_iota(jnp.int32, (queries, POS), 1)
    row = lax.broadcasted_iota(jnp.int32, (queries, POS), 0)
    length = jnp.zeros((queries, POS), jnp.int32)
    for query in range(queries):
        length = jnp.where(row == query, lengths_ref[query], length)
    shown = lane < length
    clicked = shown & (clicks == 1)
    skipped = shown & (clicks == 0)
    count = jnp.sum(jnp.where(clicked, 1.0, 0.0), axis=1, keepdims=True)
    ideal = jnp.sum(
        jnp.where(lane.astype(jnp.float32) < count, discount_row, 0.0), axis=1, keepdims=True
    )
    ideal = jnp.maximum(ideal, 1.0)
    side = jnp.where(clicked, 1.0, jnp.where(skipped, -1.0, 0.0))
    return clicked, skipped, side, side * scores, ideal


def turned(rows):
    queries = rows[0].shape[0]
    pad = jnp.zeros((POS - queries * len(rows), POS), jnp.float32)
    return jnp.transpose(jnp.concatenate(list(rows) + [pad], axis=0))


def pair_kernel(*refs):
    small_from, bins_from, sent_to = refs[:6], refs[6], refs[7]
    small, bins_ref, sent_ref, packed = refs[8:14], refs[14], refs[15], refs[16]
    took_small, took, gave = refs[17:]
    gap_ref, scores_ref, clicks_ref, lengths_ref, plus_ref, minus_ref = small
    blocks = took.shape[0]
    height = bins_ref.shape[0] // blocks
    small_takes = [
        pltpu.make_async_copy(there, here, took_small.at[at])
        for at, (there, here) in enumerate(zip(small_from, small))
    ]
    takes = []
    for block in range(blocks):
        rows = pl.ds(block * height, height)
        takes.append(
            pltpu.make_async_copy(bins_from.at[rows], bins_ref.at[rows], took.at[block])
        )
    for take in small_takes + takes:
        take.start()
    for take in small_takes:
        take.wait()
    queries = scores_ref.shape[0]
    clicked, skipped, side, signed, ideal = query_rows(
        scores_ref[...], clicks_ref[...], lengths_ref, queries, gap_ref[POS : POS + 1]
    )
    weight = jnp.where(clicked, 1.0 / plus_ref[...], jnp.where(skipped, -1.0 / minus_ref[...], 0.0))
    columns = turned([signed, weight])
    scale = 1.0 / ideal
    sums = [jnp.zeros((1, POS), jnp.float32), jnp.zeros((1, POS), jnp.float32)]

    def add_query(query):
        other = columns[:, query : query + 1]
        strength = columns[:, queries + query : queries + query + 1]
        spread = other + signed[query : query + 1]
        cross = jnp.maximum(strength * -side[query : query + 1], 0.0)
        loss = jnp.maximum(-spread, 0.0) + jnp.log1p(jnp.exp(-jnp.abs(spread)))
        total = jnp.sum(cross * gap_ref[:POS] * loss, axis=0, keepdims=True)
        total = total * scale[query : query + 1]
        sums[0] += jnp.where(side[query : query + 1] > 0.0, total, 0.0)
        sums[1] += jnp.where(side[query : query + 1] < 0.0, total, 0.0)

    for query in range(queries):
        add_query(query)

    features, slots = bins_ref.shape
    owners = features // 2
    for at, part in enumerate(sums):
        high = part.astype(jnp.bfloat16).astype(jnp.float32)
        pieces = jnp.concatenate([high, part - high], axis=0).astype(jnp.bfloat16)
        sent_ref[:, :, slots + at * POS : slots + (at + 1) * POS] = jnp.broadcast_to(
            pieces[None], (owners, 2, POS)
        )
    packed[...] = jnp.full(packed.shape, -1.0, jnp.float32)
    for take in takes:
        take.wait()
    lane = lax.broadcasted_iota(jnp.int32, (1, POS), 1)
    start = jnp.int32(0)
    for query in range(queries):
        group = start // POS
        shift = start - group * POS
        length = lengths_ref[query]
        moved = pltpu.roll(
            bins_ref[:, query * POS : (query + 1) * POS].astype(jnp.float32), shift, 1
        )
        here = (lane >= shift) & (lane < shift + length)
        there = lane < shift + length - POS
        packed[group] = jnp.where(here, moved, packed[group])
        packed[group + 1] = jnp.where(there, moved, packed[group + 1])
        start += length
    chunks = gave.shape[0]
    gives = []
    for chunk in range(chunks):
        first = chunk * owners // chunks
        for owner in range(first, first + owners // chunks):
            for group in range(slots // POS):
                sent_ref[owner, :, group * POS : (group + 1) * POS] = packed[
                    group, 2 * owner : 2 * owner + 2
                ].astype(jnp.bfloat16)
        some = pl.ds(first, owners // chunks)
        gives.append(pltpu.make_async_copy(sent_ref.at[some], sent_to.at[some], gave.at[chunk]))
        gives[-1].start()
    for give in gives:
        give.wait()


def ready_kernel(gap_ref, scores_ref, clicks_ref, lengths_ref, first_ref, second_ref, side_ref,
                 scale_ref, held_ref):
    queries = scores_ref.shape[0]
    _, _, side, signed, ideal = query_rows(
        scores_ref[...], clicks_ref[...], lengths_ref, queries, gap_ref[POS : POS + 1]
    )
    side_ref[...] = side
    scale_ref[...] = jnp.broadcast_to(1.0 / ideal, scale_ref.shape)
    columns = turned([signed, side])
    for query in range(queries):
        held_ref[query] = lengths_ref[query]
        spread = columns[:, query : query + 1] + signed[query : query + 1]
        cross = columns[:, queries + query : queries + query + 1] * side[query : query + 1]
        grown = jnp.exp(spread)
        chance = 1.0 / (1.0 + grown)
        first = jnp.where(cross < 0.0, gap_ref[:POS] * chance, 0.0)
        first_ref[query] = first
        second_ref[query] = first * (grown * chance)


def lambda_kernel(first_ref, second_ref, own_ref, scale_ref, held_ref, leaf_ref, data_ref,
                  plus_ref, minus_ref, grad_ref, side_ref, packed, flat):
    queries = own_ref.shape[0]
    slots = grad_ref.shape[1]
    sums = jnp.sum(data_ref[:, :, slots:].astype(jnp.float32), axis=0)
    sums = sums[0:1] + sums[1:2]
    plus_sum = sums[:, :POS]
    minus_sum = sums[:, POS:]
    plus = jnp.sqrt(plus_sum / plus_sum[:, 0:1])
    minus = jnp.sqrt(minus_sum / minus_sum[:, 0:1])
    plus_ref[...] = plus
    minus_ref[...] = minus
    side = own_ref[...]
    weight = jnp.where(side > 0.0, 1.0 / plus, jnp.where(side < 0.0, 1.0 / minus, 0.0))
    columns = turned([weight])
    outer = weight * scale_ref[...]
    packed[...] = jnp.zeros_like(packed)
    lane = lax.broadcasted_iota(jnp.int32, (1, POS), 1)
    start = jnp.int32(0)
    for query in range(queries):
        strength = columns[:, query : query + 1]
        slope = jnp.sum(strength * first_ref[query], axis=0, keepdims=True)
        curve = jnp.sum(strength * second_ref[query], axis=0, keepdims=True)
        slope = slope * outer[query : query + 1] * -side[query : query + 1]
        curve = curve * outer[query : query + 1]
        grad_ref[0:1, query * POS : (query + 1) * POS] = slope
        grad_ref[1:2, query * POS : (query + 1) * POS] = curve
        group = start // POS
        shift = start - group * POS
        length = held_ref[query]
        rows = jnp.concatenate(
            [slope, curve, leaf_ref[query : query + 1].astype(jnp.float32),
             jnp.zeros((5, POS), jnp.float32)], axis=0
        )
        moved = pltpu.roll(rows, shift, 1)
        here = (lane >= shift) & (lane < shift + length)
        there = lane < shift + length - POS
        packed[group] = jnp.where(here, moved, packed[group])
        packed[group + 1] = jnp.where(there, moved, packed[group + 1])
        start += length
    for group in range(queries):
        rows = packed[group]
        row = group // (queries // 2)
        at = (queries + group % (queries // 2)) * POS
        flat[:, group * POS : (group + 1) * POS] = rows[0:2]
        flat[row : row + 1, at : at + POS] = rows[2:3]
    side_ref[...] = jnp.broadcast_to(flat[...].astype(jnp.bfloat16)[None], side_ref.shape)


def plan_kernel(
    filled_ref, plus_in, minus_in, grad_in, list_ref, total_ref, plus_ref, minus_ref, grad_ref
):
    plus_ref[...] = plus_in[...]
    minus_ref[...] = minus_in[...]
    grad_ref[...] = grad_in[...]
    chips = filled_ref.shape[0] // PARTS
    groups = grad_in.shape[1] // POS
    for core in range(PARTS):
        base = core * (list_ref.shape[0] // PARTS)

        def one_block(chip, carry):
            at, spare = carry
            used = filled_ref[PARTS * chip + core]
            for group in range(groups):
                list_ref[base + at + group] = chip * 16 + group
            return at + used, jnp.where(used < groups, chip * 16 + groups - 1, spare)

        at, spare = lax.fori_loop(0, chips, one_block, (jnp.int32(0), jnp.int32(0)))
        for extra in range(2 * STEP):
            list_ref[base + at + extra] = spare
        total_ref[core] = (at + 2 * STEP - 1) // (2 * STEP)


def accumulate(core, list_ref, total_ref, data_ref, side_ref, accs):
    base = core * (list_ref.shape[0] // PARTS)
    groups = side_ref.shape[2] * 2 // (3 * POS)
    rows_a = lax.broadcasted_iota(jnp.int32, (2 * LEAVES, TILE), 0).astype(jnp.bfloat16)
    rows_b = lax.broadcasted_iota(jnp.int32, (HALF, TILE), 0).astype(jnp.bfloat16)
    zero = jnp.zeros((), jnp.bfloat16)
    one = jnp.ones((), jnp.bfloat16)

    def tiles_at(first, count):
        for at in range(count):
            bins = []
            sides = []
            leaves = []
            for half in range(2):
                entry = list_ref[base + (first + at) * 2 + half]
                chip = lax.shift_right_logical(entry, 4)
                group = lax.bitwise_and(entry, 15)
                late = group >= groups // 2
                place = groups + group - jnp.where(late, groups // 2, 0)
                here = pl.ds(pl.multiple_of(group * POS, POS), POS)
                bins.append(data_ref[PARTS * chip + core, :, here])
                sides.append(side_ref[chip, :, here])
                pair = side_ref[chip, :, pl.ds(pl.multiple_of(place * POS, POS), POS)]
                leaves.append(jnp.where(late, pair[1:2], pair[0:1]))
            bins = jnp.concatenate(bins, axis=1)
            side = jnp.concatenate(sides, axis=1)
            leaf = jnp.concatenate(leaves, axis=1)
            left = []
            right = []
            for feature in range(2):
                row = bins[feature : feature + 1]
                high = row >= jnp.asarray(HALF, jnp.bfloat16)
                hit = jnp.where(high, leaf + jnp.asarray(LEAVES, jnp.bfloat16), leaf) == rows_a
                low = jnp.where(high, row - jnp.asarray(HALF, jnp.bfloat16), row)
                left.append(jnp.where(hit, side[0:1], zero))
                left.append(jnp.where(hit, side[1:2], zero))
                right.append(jnp.where(low == rows_b, one, zero))
            unit = at % 2
            register = (at // 2) % 2
            pltpu.matmul_push_rhs(jnp.concatenate(right, axis=0), register, unit, transpose=True)
            pltpu.matmul_acc_lhs(accs[unit], jnp.concatenate(left, axis=0), register)

    def wide_step(step, carry):
        tiles_at(step * (STEP * WIDE), STEP * WIDE)
        return carry

    def step(step, carry):
        tiles_at(step * STEP, STEP)
        return carry

    total = total_ref[core]
    wide = total // WIDE
    lax.fori_loop(0, wide, wide_step, 0)
    lax.fori_loop(wide * WIDE, total, step, 0)


def summed(core, list_ref, total_ref, data_ref, side_ref, finish):
    def run(acc_a, acc_b):
        accumulate(core, list_ref, total_ref, data_ref, side_ref, (acc_a, acc_b))
        finish(pltpu.matmul_pop(acc_a) + pltpu.matmul_pop(acc_b))

    shape = (8 * LEAVES, BINS)
    pl.run_scoped(run, pltpu.ACC(0)(shape, jnp.float32), pltpu.ACC(1)(shape, jnp.float32))


def part_kernel(core_ref, list_ref, total_ref, data_ref, side_ref, *refs):
    rows = 4 * LEAVES
    out_ref = refs[-1]

    def finish(total):
        for feature in range(2):
            mine = total[
                feature * rows : (feature + 1) * rows, feature * HALF : (feature + 1) * HALF
            ]
            out_ref[feature] = mine if len(refs) == 1 else mine + refs[0][feature]

    summed(core_ref[0], list_ref, total_ref, data_ref, side_ref, finish)


def last_kernel(core_ref, list_ref, total_ref, data_ref, side_ref, before_ref, out_ref):
    rows = 4 * LEAVES

    def finish(total):
        for feature in range(2):
            mine = total[
                feature * rows : (feature + 1) * rows, feature * HALF : (feature + 1) * HALF
            ] + before_ref[feature]
            for which in range(2):
                for high in range(2):
                    at = (2 * which + high) * LEAVES
                    out_ref[
                        feature,
                        which * LEAVES : (which + 1) * LEAVES,
                        high * HALF : (high + 1) * HALF,
                    ] = mine[at : at + LEAVES]

    summed(core_ref[0], list_ref, total_ref, data_ref, side_ref, finish)


VMEM = pl.BlockSpec(memory_space=pltpu.VMEM)
SMEM = pl.BlockSpec(memory_space=pltpu.SMEM)


def in_vmem(array):
    return pltpu.with_memory_space_constraint(array, pltpu.VMEM)


def in_smem(array):
    return pltpu.with_memory_space_constraint(array, pltpu.SMEM)


def hist_of(core, plan, data, side, before=None, last=False):
    given = [in_vmem(data), in_vmem(side)]
    if before is not None:
        given.append(in_vmem(before))
    if last:
        out_shape = jax.ShapeDtypeStruct((2, 2 * LEAVES, BINS), jnp.float32)
    else:
        out_shape = pltpu.VMEM((2, 4 * LEAVES, HALF), jnp.float32)
    return pl.pallas_call(
        last_kernel if last else part_kernel,
        out_shape=out_shape,
        in_specs=[SMEM, SMEM, SMEM] + [VMEM] * len(given),
        out_specs=VMEM,
        name="last_part" if last else "part",
    )(core.reshape(1), *plan, *given)


def body(scores, clicks, lengths, t_plus_old, t_minus_old, leaf, bins):
    shards = lax.axis_size("doc")
    queries = scores.shape[0]
    slots = leaf.shape[0]
    groups = slots // POS
    places = np.arange(POS, dtype=np.float32)
    discount = (1.0 / np.log2(2.0 + places)).astype(np.float32)
    gap = np.abs(discount[:, None] - discount[None, :])
    gap = jnp.asarray(np.concatenate([gap, np.tile(discount[None], (8, 1))]))
    f32 = jnp.float32
    sent_shape = (shards, 2, slots + 2 * POS)
    given = (gap, scores, clicks, lengths, t_plus_old[None], t_minus_old[None])
    anywhere = pl.BlockSpec(memory_space=pl.ANY)
    sent = pl.pallas_call(
        pair_kernel,
        out_shape=jax.ShapeDtypeStruct(sent_shape, jnp.bfloat16),
        in_specs=[anywhere] * 7,
        out_specs=anywhere,
        scratch_shapes=[
            *(
                (pltpu.SMEM if array.ndim == 1 else pltpu.VMEM)(array.shape, array.dtype)
                for array in given
            ),
            pltpu.VMEM(bins.shape, jnp.int32),
            pltpu.VMEM(sent_shape, jnp.bfloat16),
            pltpu.VMEM((slots // POS + 1, bins.shape[0], POS), f32),
            pltpu.SemaphoreType.DMA((len(given),)),
            pltpu.SemaphoreType.DMA((1,)),
            pltpu.SemaphoreType.DMA((4,)),
        ],
        name="pair_terms",
    )(*given, bins)
    data = lax.all_to_all(sent, "doc", 0, 0, tiled=True)
    first, second, own, scale, held = pl.pallas_call(
        ready_kernel,
        out_shape=(
            pltpu.VMEM((queries, POS, POS), f32),
            pltpu.VMEM((queries, POS, POS), f32),
            pltpu.VMEM((queries, POS), f32),
            pltpu.VMEM((queries, POS), f32),
            pltpu.SMEM((queries,), jnp.int32),
        ),
        in_specs=[VMEM, VMEM, VMEM, SMEM],
        out_specs=(VMEM, VMEM, VMEM, VMEM, SMEM),
        name="ready_pairs",
    )(gap, scores, clicks, lengths)
    t_plus, t_minus, gradients, side = pl.pallas_call(
        lambda_kernel,
        out_shape=(
            pltpu.VMEM((1, POS), f32),
            pltpu.VMEM((1, POS), f32),
            pltpu.VMEM((2, slots), f32),
            pltpu.VMEM((shards // PARTS, 2, 3 * slots // 2), jnp.bfloat16),
        ),
        in_specs=[VMEM, VMEM, VMEM, VMEM, SMEM, VMEM, VMEM],
        out_specs=(VMEM,) * 4,
        scratch_shapes=[
            pltpu.VMEM((queries + 1, 8, POS), f32),
            pltpu.VMEM((2, 3 * slots // 2), f32),
        ],
        name="lambdas",
    )(
        in_vmem(first),
        in_vmem(second),
        in_vmem(own),
        in_vmem(scale),
        in_smem(held),
        in_vmem(leaf.reshape(queries, POS)),
        in_vmem(data),
    )
    alike = [list(range(part, shards, PARTS)) for part in range(PARTS)]
    side = lax.all_to_all(side, "doc", 0, 0, axis_index_groups=alike, tiled=True)
    shown = jnp.sum((data[:, 0, :slots] >= 0).astype(f32), axis=1).astype(jnp.int32)
    *plan, t_plus, t_minus, gradients = pl.pallas_call(
        plan_kernel,
        out_shape=(
            pltpu.SMEM((shards * groups + PARTS * 16,), jnp.int32),
            pltpu.SMEM((PARTS,), jnp.int32),
            jax.ShapeDtypeStruct((1, POS), f32),
            jax.ShapeDtypeStruct((1, POS), f32),
            jax.ShapeDtypeStruct((2, slots), f32),
        ),
        in_specs=[SMEM, VMEM, VMEM, VMEM],
        out_specs=(SMEM, SMEM, VMEM, VMEM, VMEM),
        name="plan",
    )((shown + (POS - 1)) // POS, in_vmem(t_plus), in_vmem(t_minus), in_vmem(gradients))
    swap = [[(at, at ^ bit) for at in range(shards)] for bit in (1, 2)]
    own = lax.rem(lax.axis_index("doc"), PARTS)
    side_far = lax.ppermute(side, "doc", swap[1])
    side_near = lax.ppermute(side, "doc", swap[0])
    side_last = lax.ppermute(side_far, "doc", swap[0])
    partial = hist_of(own, plan, data, side)
    partial = hist_of(lax.bitwise_xor(own, 1), plan, data, side_near, partial)
    partial = hist_of(lax.bitwise_xor(own, 2), plan, data, side_far, partial)
    hist = hist_of(lax.bitwise_xor(own, 3), plan, data, side_last, partial, True)
    return (t_plus[0], t_minus[0], gradients, hist)


def solution(mesh):
    placed = (P("doc", None), P("doc", None), P("doc"), P(), P(), P("doc"), P("feat", "doc"))
    return jax.shard_map(
        body,
        mesh=mesh,
        in_specs=placed,
        out_specs=(P(), P(), P(None, "doc"), P(("feat", "doc"), None, None)),
        check_vma=False,
    )
```

```python
import jax
import jax.numpy as jnp
import numpy as np
from jax import lax
from jax.experimental import pallas as pl
from jax.experimental.pallas import tpu as pltpu
from jax.sharding import PartitionSpec as P


BINS = 256
LEAVES = 32
POS = 128
HALF = BINS // 2
TILE = 256
STEP = 4
WIDE = 4
PARTS = 4


def query_rows(scores, clicks, lengths_ref, queries, discount_row):
    lane = lax.broadcasted_iota(jnp.int32, (queries, POS), 1)
    row = lax.broadcasted_iota(jnp.int32, (queries, POS), 0)
    length = jnp.zeros((queries, POS), jnp.int32)
    for query in range(queries):
        length = jnp.where(row == query, lengths_ref[query], length)
    shown = lane < length
    clicked = shown & (clicks == 1)
    skipped = shown & (clicks == 0)
    count = jnp.sum(jnp.where(clicked, 1.0, 0.0), axis=1, keepdims=True)
    ideal = jnp.sum(
        jnp.where(lane.astype(jnp.float32) < count, discount_row, 0.0), axis=1, keepdims=True
    )
    ideal = jnp.maximum(ideal, 1.0)
    side = jnp.where(clicked, 1.0, jnp.where(skipped, -1.0, 0.0))
    return clicked, skipped, side, side * scores, ideal


def turned(rows):
    queries = rows[0].shape[0]
    pad = jnp.zeros((POS - queries * len(rows), POS), jnp.float32)
    return jnp.transpose(jnp.concatenate(list(rows) + [pad], axis=0))


def pair_kernel(*refs):
    small_from, bins_from, sent_to = refs[:6], refs[6], refs[7]
    small, bins_ref, sent_ref, packed = refs[8:14], refs[14], refs[15], refs[16]
    took_small, took, gave = refs[17:]
    gap_ref, scores_ref, clicks_ref, lengths_ref, plus_ref, minus_ref = small
    blocks = took.shape[0]
    height = bins_ref.shape[0] // blocks
    small_takes = [
        pltpu.make_async_copy(there, here, took_small.at[at])
        for at, (there, here) in enumerate(zip(small_from, small))
    ]
    takes = []
    for block in range(blocks):
        rows = pl.ds(block * height, height)
        takes.append(
            pltpu.make_async_copy(bins_from.at[rows], bins_ref.at[rows], took.at[block])
        )
    for take in small_takes + takes:
        take.start()
    for take in small_takes:
        take.wait()
    queries = scores_ref.shape[0]
    clicked, skipped, side, signed, ideal = query_rows(
        scores_ref[...], clicks_ref[...], lengths_ref, queries, gap_ref[POS : POS + 1]
    )
    weight = jnp.where(clicked, 1.0 / plus_ref[...], jnp.where(skipped, -1.0 / minus_ref[...], 0.0))
    columns = turned([signed, weight])
    scale = 1.0 / ideal
    sums = [jnp.zeros((1, POS), jnp.float32), jnp.zeros((1, POS), jnp.float32)]

    def add_query(query):
        other = columns[:, query : query + 1]
        strength = columns[:, queries + query : queries + query + 1]
        spread = other + signed[query : query + 1]
        cross = jnp.maximum(strength * -side[query : query + 1], 0.0)
        loss = jnp.maximum(-spread, 0.0) + jnp.log1p(jnp.exp(-jnp.abs(spread)))
        total = jnp.sum(cross * gap_ref[:POS] * loss, axis=0, keepdims=True)
        total = total * scale[query : query + 1]
        sums[0] += jnp.where(side[query : query + 1] > 0.0, total, 0.0)
        sums[1] += jnp.where(side[query : query + 1] < 0.0, total, 0.0)

    for query in range(queries):
        add_query(query)

    features, slots = bins_ref.shape
    owners = features // 2
    for at, part in enumerate(sums):
        high = part.astype(jnp.bfloat16).astype(jnp.float32)
        pieces = jnp.concatenate([high, part - high], axis=0).astype(jnp.bfloat16)
        sent_ref[:, :, slots + at * POS : slots + (at + 1) * POS] = jnp.broadcast_to(
            pieces[None], (owners, 2, POS)
        )
    packed[...] = jnp.full(packed.shape, -1.0, jnp.float32)
    for take in takes:
        take.wait()
    lane = lax.broadcasted_iota(jnp.int32, (1, POS), 1)
    start = jnp.int32(0)
    for query in range(queries):
        group = start // POS
        shift = start - group * POS
        length = lengths_ref[query]
        moved = pltpu.roll(
            bins_ref[:, query * POS : (query + 1) * POS].astype(jnp.float32), shift, 1
        )
        here = (lane >= shift) & (lane < shift + length)
        there = lane < shift + length - POS
        packed[group] = jnp.where(here, moved, packed[group])
        packed[group + 1] = jnp.where(there, moved, packed[group + 1])
        start += length
    chunks = gave.shape[0]
    gives = []
    for chunk in range(chunks):
        first = chunk * owners // chunks
        for owner in range(first, first + owners // chunks):
            for group in range(slots // POS):
                sent_ref[owner, :, group * POS : (group + 1) * POS] = packed[
                    group, 2 * owner : 2 * owner + 2
                ].astype(jnp.bfloat16)
        some = pl.ds(first, owners // chunks)
        gives.append(pltpu.make_async_copy(sent_ref.at[some], sent_to.at[some], gave.at[chunk]))
        gives[-1].start()
    for give in gives:
        give.wait()


def ready_kernel(gap_ref, scores_ref, clicks_ref, lengths_ref, first_ref, second_ref, side_ref,
                 scale_ref, held_ref):
    queries = scores_ref.shape[0]
    _, _, side, signed, ideal = query_rows(
        scores_ref[...], clicks_ref[...], lengths_ref, queries, gap_ref[POS : POS + 1]
    )
    side_ref[...] = side
    scale_ref[...] = jnp.broadcast_to(1.0 / ideal, scale_ref.shape)
    columns = turned([signed, side])
    for query in range(queries):
        held_ref[query] = lengths_ref[query]
        spread = columns[:, query : query + 1] + signed[query : query + 1]
        cross = columns[:, queries + query : queries + query + 1] * side[query : query + 1]
        grown = jnp.exp(spread)
        chance = 1.0 / (1.0 + grown)
        first = jnp.where(cross < 0.0, gap_ref[:POS] * chance, 0.0)
        first_ref[query] = first
        second_ref[query] = first * (grown * chance)


def lambda_kernel(first_ref, second_ref, own_ref, scale_ref, held_ref, leaf_ref, data_ref,
                  plus_ref, minus_ref, grad_ref, side_ref, packed, flat):
    queries = own_ref.shape[0]
    slots = grad_ref.shape[1]
    sums = jnp.sum(data_ref[:, :, slots:].astype(jnp.float32), axis=0)
    sums = sums[0:1] + sums[1:2]
    plus_sum = sums[:, :POS]
    minus_sum = sums[:, POS:]
    plus = jnp.sqrt(plus_sum / plus_sum[:, 0:1])
    minus = jnp.sqrt(minus_sum / minus_sum[:, 0:1])
    plus_ref[...] = plus
    minus_ref[...] = minus
    side = own_ref[...]
    weight = jnp.where(side > 0.0, 1.0 / plus, jnp.where(side < 0.0, 1.0 / minus, 0.0))
    columns = turned([weight])
    outer = weight * scale_ref[...]
    packed[...] = jnp.zeros_like(packed)
    lane = lax.broadcasted_iota(jnp.int32, (1, POS), 1)
    start = jnp.int32(0)
    for query in range(queries):
        strength = columns[:, query : query + 1]
        slope = jnp.sum(strength * first_ref[query], axis=0, keepdims=True)
        curve = jnp.sum(strength * second_ref[query], axis=0, keepdims=True)
        slope = slope * outer[query : query + 1] * -side[query : query + 1]
        curve = curve * outer[query : query + 1]
        grad_ref[0:1, query * POS : (query + 1) * POS] = slope
        grad_ref[1:2, query * POS : (query + 1) * POS] = curve
        group = start // POS
        shift = start - group * POS
        length = held_ref[query]
        rows = jnp.concatenate(
            [slope, curve, leaf_ref[query : query + 1].astype(jnp.float32),
             jnp.zeros((5, POS), jnp.float32)], axis=0
        )
        moved = pltpu.roll(rows, shift, 1)
        here = (lane >= shift) & (lane < shift + length)
        there = lane < shift + length - POS
        packed[group] = jnp.where(here, moved, packed[group])
        packed[group + 1] = jnp.where(there, moved, packed[group + 1])
        start += length
    for group in range(queries):
        rows = packed[group]
        row = group // (queries // 2)
        at = (queries + group % (queries // 2)) * POS
        flat[:, group * POS : (group + 1) * POS] = rows[0:2]
        flat[row : row + 1, at : at + POS] = rows[2:3]
    side_ref[...] = jnp.broadcast_to(flat[...].astype(jnp.bfloat16)[None], side_ref.shape)


def owner_of(chip, part):
    high = lax.shift_right_logical(chip, 2)
    return 16 * high + 2 * (chip - 4 * high) + part


def plan_kernel(
    filled_ref, plus_in, minus_in, grad_in, list_ref, total_ref, plus_ref, minus_ref, grad_ref
):
    plus_ref[...] = plus_in[...]
    minus_ref[...] = minus_in[...]
    grad_ref[...] = grad_in[...]
    chips = filled_ref.shape[0] // PARTS
    groups = grad_in.shape[1] // POS
    for core in range(PARTS):
        base = core * (list_ref.shape[0] // PARTS)

        def one_block(chip, carry):
            at, spare = carry
            used = filled_ref[owner_of(chip, 8 * (core // 2) + core % 2)]
            for group in range(groups):
                list_ref[base + at + group] = chip * 16 + group
            return at + used, jnp.where(used < groups, chip * 16 + groups - 1, spare)

        at, spare = lax.fori_loop(0, chips, one_block, (jnp.int32(0), jnp.int32(0)))
        for extra in range(2 * STEP):
            list_ref[base + at + extra] = spare
        total_ref[core] = (at + 2 * STEP - 1) // (2 * STEP)


def accumulate(core, list_ref, total_ref, data_ref, side_ref, accs):
    base = core * (list_ref.shape[0] // PARTS)
    groups = side_ref.shape[2] * 2 // (3 * POS)
    part = 8 * lax.shift_right_logical(core, 1) + lax.bitwise_and(core, 1)
    rows_a = lax.broadcasted_iota(jnp.int32, (2 * LEAVES, TILE), 0).astype(jnp.bfloat16)
    rows_b = lax.broadcasted_iota(jnp.int32, (HALF, TILE), 0).astype(jnp.bfloat16)
    zero = jnp.zeros((), jnp.bfloat16)
    one = jnp.ones((), jnp.bfloat16)

    def tiles_at(first, count):
        for at in range(count):
            bins = []
            sides = []
            leaves = []
            for half in range(2):
                entry = list_ref[base + (first + at) * 2 + half]
                chip = lax.shift_right_logical(entry, 4)
                group = lax.bitwise_and(entry, 15)
                late = group >= groups // 2
                place = groups + group - jnp.where(late, groups // 2, 0)
                here = pl.ds(pl.multiple_of(group * POS, POS), POS)
                bins.append(data_ref[owner_of(chip, part), :, here])
                sides.append(side_ref[chip, :, here])
                pair = side_ref[chip, :, pl.ds(pl.multiple_of(place * POS, POS), POS)]
                leaves.append(jnp.where(late, pair[1:2], pair[0:1]))
            bins = jnp.concatenate(bins, axis=1)
            side = jnp.concatenate(sides, axis=1)
            leaf = jnp.concatenate(leaves, axis=1)
            left = []
            right = []
            for feature in range(2):
                row = bins[feature : feature + 1]
                high = row >= jnp.asarray(HALF, jnp.bfloat16)
                hit = jnp.where(high, leaf + jnp.asarray(LEAVES, jnp.bfloat16), leaf) == rows_a
                low = jnp.where(high, row - jnp.asarray(HALF, jnp.bfloat16), row)
                left.append(jnp.where(hit, side[0:1], zero))
                left.append(jnp.where(hit, side[1:2], zero))
                right.append(jnp.where(low == rows_b, one, zero))
            unit = at % 2
            register = (at // 2) % 2
            pltpu.matmul_push_rhs(jnp.concatenate(right, axis=0), register, unit, transpose=True)
            pltpu.matmul_acc_lhs(accs[unit], jnp.concatenate(left, axis=0), register)

    def wide_step(step, carry):
        tiles_at(step * (STEP * WIDE), STEP * WIDE)
        return carry

    def step(step, carry):
        tiles_at(step * STEP, STEP)
        return carry

    total = total_ref[core]
    wide = total // WIDE
    lax.fori_loop(0, wide, wide_step, 0)
    lax.fori_loop(wide * WIDE, total, step, 0)


def summed(core, list_ref, total_ref, data_ref, side_ref, finish):
    def run(acc_a, acc_b):
        accumulate(core, list_ref, total_ref, data_ref, side_ref, (acc_a, acc_b))
        finish(pltpu.matmul_pop(acc_a) + pltpu.matmul_pop(acc_b))

    shape = (8 * LEAVES, BINS)
    pl.run_scoped(run, pltpu.ACC(0)(shape, jnp.float32), pltpu.ACC(1)(shape, jnp.float32))


def part_kernel(core_ref, list_ref, total_ref, data_ref, side_ref, *refs):
    rows = 4 * LEAVES
    out_ref = refs[-1]

    def finish(total):
        for feature in range(2):
            mine = total[
                feature * rows : (feature + 1) * rows, feature * HALF : (feature + 1) * HALF
            ]
            out_ref[feature] = mine if len(refs) == 1 else mine + refs[0][feature]

    summed(core_ref[0], list_ref, total_ref, data_ref, side_ref, finish)


def last_kernel(core_ref, list_ref, total_ref, data_ref, side_ref, before_ref, out_ref):
    rows = 4 * LEAVES

    def finish(total):
        for feature in range(2):
            mine = total[
                feature * rows : (feature + 1) * rows, feature * HALF : (feature + 1) * HALF
            ] + before_ref[feature]
            for which in range(2):
                for high in range(2):
                    at = (2 * which + high) * LEAVES
                    out_ref[
                        feature,
                        which * LEAVES : (which + 1) * LEAVES,
                        high * HALF : (high + 1) * HALF,
                    ] = mine[at : at + LEAVES]

    summed(core_ref[0], list_ref, total_ref, data_ref, side_ref, finish)


VMEM = pl.BlockSpec(memory_space=pltpu.VMEM)
SMEM = pl.BlockSpec(memory_space=pltpu.SMEM)


def in_vmem(array):
    return pltpu.with_memory_space_constraint(array, pltpu.VMEM)


def in_smem(array):
    return pltpu.with_memory_space_constraint(array, pltpu.SMEM)


def hist_of(core, plan, data, side, before=None, last=False):
    given = [in_vmem(data), in_vmem(side)]
    if before is not None:
        given.append(in_vmem(before))
    if last:
        out_shape = jax.ShapeDtypeStruct((2, 2 * LEAVES, BINS), jnp.float32)
    else:
        out_shape = pltpu.VMEM((2, 4 * LEAVES, HALF), jnp.float32)
    return pl.pallas_call(
        last_kernel if last else part_kernel,
        out_shape=out_shape,
        in_specs=[SMEM, SMEM, SMEM] + [VMEM] * len(given),
        out_specs=VMEM,
        name="last_part" if last else "part",
    )(core.reshape(1), *plan, *given)


def body(scores, clicks, lengths, t_plus_old, t_minus_old, leaf, bins):
    shards = lax.axis_size("doc")
    queries = scores.shape[0]
    slots = leaf.shape[0]
    groups = slots // POS
    places = np.arange(POS, dtype=np.float32)
    discount = (1.0 / np.log2(2.0 + places)).astype(np.float32)
    gap = np.abs(discount[:, None] - discount[None, :])
    gap = jnp.asarray(np.concatenate([gap, np.tile(discount[None], (8, 1))]))
    f32 = jnp.float32
    sent_shape = (shards, 2, slots + 2 * POS)
    given = (gap, scores, clicks, lengths, t_plus_old[None], t_minus_old[None])
    anywhere = pl.BlockSpec(memory_space=pl.ANY)
    sent = pl.pallas_call(
        pair_kernel,
        out_shape=jax.ShapeDtypeStruct(sent_shape, jnp.bfloat16),
        in_specs=[anywhere] * 7,
        out_specs=anywhere,
        scratch_shapes=[
            *(
                (pltpu.SMEM if array.ndim == 1 else pltpu.VMEM)(array.shape, array.dtype)
                for array in given
            ),
            pltpu.VMEM(bins.shape, jnp.int32),
            pltpu.VMEM(sent_shape, jnp.bfloat16),
            pltpu.VMEM((slots // POS + 1, bins.shape[0], POS), f32),
            pltpu.SemaphoreType.DMA((len(given),)),
            pltpu.SemaphoreType.DMA((1,)),
            pltpu.SemaphoreType.DMA((4,)),
        ],
        name="pair_terms",
    )(*given, bins)
    data = lax.all_to_all(sent, "doc", 0, 0, tiled=True)
    first, second, own, scale, held = pl.pallas_call(
        ready_kernel,
        out_shape=(
            pltpu.VMEM((queries, POS, POS), f32),
            pltpu.VMEM((queries, POS, POS), f32),
            pltpu.VMEM((queries, POS), f32),
            pltpu.VMEM((queries, POS), f32),
            pltpu.SMEM((queries,), jnp.int32),
        ),
        in_specs=[VMEM, VMEM, VMEM, SMEM],
        out_specs=(VMEM, VMEM, VMEM, VMEM, SMEM),
        name="ready_pairs",
    )(gap, scores, clicks, lengths)
    t_plus, t_minus, gradients, side = pl.pallas_call(
        lambda_kernel,
        out_shape=(
            pltpu.VMEM((1, POS), f32),
            pltpu.VMEM((1, POS), f32),
            pltpu.VMEM((2, slots), f32),
            pltpu.VMEM((shards // PARTS, 2, 3 * slots // 2), jnp.bfloat16),
        ),
        in_specs=[VMEM, VMEM, VMEM, VMEM, SMEM, VMEM, VMEM],
        out_specs=(VMEM,) * 4,
        scratch_shapes=[
            pltpu.VMEM((queries + 1, 8, POS), f32),
            pltpu.VMEM((2, 3 * slots // 2), f32),
        ],
        name="lambdas",
    )(
        in_vmem(first),
        in_vmem(second),
        in_vmem(own),
        in_vmem(scale),
        in_smem(held),
        in_vmem(leaf.reshape(queries, POS)),
        in_vmem(data),
    )
    alike = [
        [16 * (chip // 4) + 2 * (chip % 4) + 8 * (part // 2) + part % 2 for chip in range(16)]
        for part in range(PARTS)
    ]
    side = lax.all_to_all(side, "doc", 0, 0, axis_index_groups=alike, tiled=True)
    shown = jnp.sum((data[:, 0, :slots] >= 0).astype(f32), axis=1).astype(jnp.int32)
    *plan, t_plus, t_minus, gradients = pl.pallas_call(
        plan_kernel,
        out_shape=(
            pltpu.SMEM((shards * groups + PARTS * 16,), jnp.int32),
            pltpu.SMEM((PARTS,), jnp.int32),
            jax.ShapeDtypeStruct((1, POS), f32),
            jax.ShapeDtypeStruct((1, POS), f32),
            jax.ShapeDtypeStruct((2, slots), f32),
        ),
        in_specs=[SMEM, VMEM, VMEM, VMEM],
        out_specs=(SMEM, SMEM, VMEM, VMEM, VMEM),
        name="plan",
    )((shown + (POS - 1)) // POS, in_vmem(t_plus), in_vmem(t_minus), in_vmem(gradients))
    swap = [[(at, at ^ bit) for at in range(shards)] for bit in (1, 8)]
    index = lax.axis_index("doc")
    own = 2 * lax.rem(index // 8, 2) + lax.rem(index, 2)
    side_far = lax.ppermute(side, "doc", swap[1])
    side_near = lax.ppermute(side, "doc", swap[0])
    side_last = lax.ppermute(side_far, "doc", swap[0])
    partial = hist_of(own, plan, data, side)
    partial = hist_of(lax.bitwise_xor(own, 1), plan, data, side_near, partial)
    partial = hist_of(lax.bitwise_xor(own, 2), plan, data, side_far, partial)
    hist = hist_of(lax.bitwise_xor(own, 3), plan, data, side_last, partial, True)
    return (t_plus[0], t_minus[0], gradients, hist)


def solution(mesh):
    placed = (P("doc", None), P("doc", None), P("doc"), P(), P(), P("doc"), P("feat", "doc"))
    return jax.shard_map(
        body,
        mesh=mesh,
        in_specs=placed,
        out_specs=(P(), P(), P(None, "doc"), P(("feat", "doc"), None, None)),
        check_vma=False,
    )
```

```python
import functools

import jax
import jax.numpy as jnp
import numpy as np
from jax import lax
from jax.experimental import pallas as pl
from jax.experimental.pallas import tpu as pltpu
from jax.sharding import PartitionSpec as P


BINS = 256
LEAVES = 32
POS = 128
HALF = BINS // 2
TILE = 256
STEP = 4
WIDE = 4
PARTS = 4


def query_rows(scores, clicks, lengths_ref, queries, discount_row):
    lane = lax.broadcasted_iota(jnp.int32, (queries, POS), 1)
    row = lax.broadcasted_iota(jnp.int32, (queries, POS), 0)
    length = jnp.zeros((queries, POS), jnp.int32)
    for query in range(queries):
        length = jnp.where(row == query, lengths_ref[query], length)
    shown = lane < length
    clicked = shown & (clicks == 1)
    skipped = shown & (clicks == 0)
    count = jnp.sum(jnp.where(clicked, 1.0, 0.0), axis=1, keepdims=True)
    ideal = jnp.sum(
        jnp.where(lane.astype(jnp.float32) < count, discount_row, 0.0), axis=1, keepdims=True
    )
    ideal = jnp.maximum(ideal, 1.0)
    side = jnp.where(clicked, 1.0, jnp.where(skipped, -1.0, 0.0))
    return clicked, skipped, side, side * scores, ideal


def turned(rows):
    queries = rows[0].shape[0]
    pad = jnp.zeros((POS - queries * len(rows), POS), jnp.float32)
    return jnp.transpose(jnp.concatenate(list(rows) + [pad], axis=0))


def pair_kernel(*refs):
    small_from, bins_from, sent_to = refs[:6], refs[6], refs[7]
    small, bins_ref, sent_ref, packed = refs[8:14], refs[14], refs[15], refs[16]
    took_small, took, gave = refs[17:]
    gap_ref, scores_ref, clicks_ref, lengths_ref, plus_ref, minus_ref = small
    blocks = took.shape[0]
    height = bins_ref.shape[0] // blocks
    small_takes = [
        pltpu.make_async_copy(there, here, took_small.at[at])
        for at, (there, here) in enumerate(zip(small_from, small))
    ]
    takes = []
    for block in range(blocks):
        rows = pl.ds(block * height, height)
        takes.append(
            pltpu.make_async_copy(bins_from.at[rows], bins_ref.at[rows], took.at[block])
        )
    for take in small_takes + takes:
        take.start()
    for take in small_takes:
        take.wait()
    queries = scores_ref.shape[0]
    clicked, skipped, side, signed, ideal = query_rows(
        scores_ref[...], clicks_ref[...], lengths_ref, queries, gap_ref[POS : POS + 1]
    )
    weight = jnp.where(clicked, 1.0 / plus_ref[...], jnp.where(skipped, -1.0 / minus_ref[...], 0.0))
    columns = turned([signed, weight])
    scale = 1.0 / ideal
    sums = [jnp.zeros((1, POS), jnp.float32), jnp.zeros((1, POS), jnp.float32)]

    def add_query(query):
        other = columns[:, query : query + 1]
        strength = columns[:, queries + query : queries + query + 1]
        spread = other + signed[query : query + 1]
        cross = jnp.maximum(strength * -side[query : query + 1], 0.0)
        loss = jnp.maximum(-spread, 0.0) + jnp.log1p(jnp.exp(-jnp.abs(spread)))
        total = jnp.sum(cross * gap_ref[:POS] * loss, axis=0, keepdims=True)
        total = total * scale[query : query + 1]
        sums[0] += jnp.where(side[query : query + 1] > 0.0, total, 0.0)
        sums[1] += jnp.where(side[query : query + 1] < 0.0, total, 0.0)

    for query in range(queries):
        add_query(query)

    features, slots = bins_ref.shape
    owners = features // 2
    for at, part in enumerate(sums):
        high = part.astype(jnp.bfloat16).astype(jnp.float32)
        pieces = jnp.concatenate([high, part - high], axis=0).astype(jnp.bfloat16)
        sent_ref[:, :, slots + at * POS : slots + (at + 1) * POS] = jnp.broadcast_to(
            pieces[None], (owners, 2, POS)
        )
    packed[...] = jnp.full(packed.shape, -1.0, jnp.float32)
    for take in takes:
        take.wait()
    lane = lax.broadcasted_iota(jnp.int32, (1, POS), 1)
    start = jnp.int32(0)
    for query in range(queries):
        group = start // POS
        shift = start - group * POS
        length = lengths_ref[query]
        moved = pltpu.roll(
            bins_ref[:, query * POS : (query + 1) * POS].astype(jnp.float32), shift, 1
        )
        here = (lane >= shift) & (lane < shift + length)
        there = lane < shift + length - POS
        packed[group] = jnp.where(here, moved, packed[group])
        packed[group + 1] = jnp.where(there, moved, packed[group + 1])
        start += length
    chunks = gave.shape[0]
    gives = []
    for chunk in range(chunks):
        first = chunk * owners // chunks
        for owner in range(first, first + owners // chunks):
            for group in range(slots // POS):
                sent_ref[owner, :, group * POS : (group + 1) * POS] = packed[
                    group, 2 * owner : 2 * owner + 2
                ].astype(jnp.bfloat16)
        some = pl.ds(first, owners // chunks)
        gives.append(pltpu.make_async_copy(sent_ref.at[some], sent_to.at[some], gave.at[chunk]))
        gives[-1].start()
    for give in gives:
        give.wait()


def ready_kernel(gap_ref, scores_ref, clicks_ref, lengths_ref, first_ref, second_ref, side_ref,
                 scale_ref, held_ref):
    queries = scores_ref.shape[0]
    _, _, side, signed, ideal = query_rows(
        scores_ref[...], clicks_ref[...], lengths_ref, queries, gap_ref[POS : POS + 1]
    )
    side_ref[...] = side
    scale_ref[...] = jnp.broadcast_to(1.0 / ideal, scale_ref.shape)
    columns = turned([signed, side])
    for query in range(queries):
        held_ref[query] = lengths_ref[query]
        spread = columns[:, query : query + 1] + signed[query : query + 1]
        cross = columns[:, queries + query : queries + query + 1] * side[query : query + 1]
        grown = jnp.exp(spread)
        chance = 1.0 / (1.0 + grown)
        first = jnp.where(cross < 0.0, gap_ref[:POS] * chance, 0.0)
        first_ref[query] = first
        second_ref[query] = first * (grown * chance)


def lambda_kernel(first_ref, second_ref, own_ref, scale_ref, held_ref, leaf_ref, data_ref,
                  plus_ref, minus_ref, grad_ref, side_ref, packed, flat):
    queries = own_ref.shape[0]
    slots = grad_ref.shape[1]
    sums = jnp.sum(data_ref[:, :, slots:].astype(jnp.float32), axis=0)
    sums = sums[0:1] + sums[1:2]
    plus_sum = sums[:, :POS]
    minus_sum = sums[:, POS:]
    plus = jnp.sqrt(plus_sum / plus_sum[:, 0:1])
    minus = jnp.sqrt(minus_sum / minus_sum[:, 0:1])
    plus_ref[...] = plus
    minus_ref[...] = minus
    side = own_ref[...]
    weight = jnp.where(side > 0.0, 1.0 / plus, jnp.where(side < 0.0, 1.0 / minus, 0.0))
    columns = turned([weight])
    outer = weight * scale_ref[...]
    packed[...] = jnp.zeros_like(packed)
    lane = lax.broadcasted_iota(jnp.int32, (1, POS), 1)
    start = jnp.int32(0)
    for query in range(queries):
        strength = columns[:, query : query + 1]
        slope = jnp.sum(strength * first_ref[query], axis=0, keepdims=True)
        curve = jnp.sum(strength * second_ref[query], axis=0, keepdims=True)
        slope = slope * outer[query : query + 1] * -side[query : query + 1]
        curve = curve * outer[query : query + 1]
        grad_ref[0:1, query * POS : (query + 1) * POS] = slope
        grad_ref[1:2, query * POS : (query + 1) * POS] = curve
        group = start // POS
        shift = start - group * POS
        length = held_ref[query]
        rows = jnp.concatenate(
            [slope, curve, leaf_ref[query : query + 1].astype(jnp.float32),
             jnp.zeros((5, POS), jnp.float32)], axis=0
        )
        moved = pltpu.roll(rows, shift, 1)
        here = (lane >= shift) & (lane < shift + length)
        there = lane < shift + length - POS
        packed[group] = jnp.where(here, moved, packed[group])
        packed[group + 1] = jnp.where(there, moved, packed[group + 1])
        start += length
    for group in range(queries):
        rows = packed[group]
        row = group // (queries // 2)
        at = (queries + group % (queries // 2)) * POS
        flat[:, group * POS : (group + 1) * POS] = rows[0:2]
        flat[row : row + 1, at : at + POS] = rows[2:3]
    side_ref[...] = jnp.broadcast_to(flat[...].astype(jnp.bfloat16)[None], side_ref.shape)


def owner_of(chip, part):
    high = lax.shift_right_logical(chip, 2)
    return 16 * high + 2 * (chip - 4 * high) + part


def plan_kernel(
    filled_ref, plus_in, minus_in, grad_in, list_ref, total_ref, plus_ref, minus_ref, grad_ref
):
    plus_ref[...] = plus_in[...]
    minus_ref[...] = minus_in[...]
    grad_ref[...] = grad_in[...]
    chips = filled_ref.shape[0] // PARTS
    groups = grad_in.shape[1] // POS
    for core in range(PARTS):
        base = core * (list_ref.shape[0] // PARTS)

        def one_block(chip, carry):
            at, spare = carry
            used = filled_ref[owner_of(chip, 8 * (core // 2) + core % 2)]
            for group in range(groups):
                list_ref[base + at + group] = chip * 16 + group
            return at + used, jnp.where(used < groups, chip * 16 + groups - 1, spare)

        at, spare = lax.fori_loop(0, chips, one_block, (jnp.int32(0), jnp.int32(0)))
        for extra in range(2 * STEP):
            list_ref[base + at + extra] = spare
        total_ref[core] = (at + 2 * STEP - 1) // (2 * STEP)


def accumulate(core, begin, end, list_ref, data_ref, side_ref, accs):
    base = core * (list_ref.shape[0] // PARTS)
    groups = side_ref.shape[2] * 2 // (3 * POS)
    part = 8 * lax.shift_right_logical(core, 1) + lax.bitwise_and(core, 1)
    rows_a = lax.broadcasted_iota(jnp.int32, (2 * LEAVES, TILE), 0).astype(jnp.bfloat16)
    rows_b = lax.broadcasted_iota(jnp.int32, (HALF, TILE), 0).astype(jnp.bfloat16)
    zero = jnp.zeros((), jnp.bfloat16)
    one = jnp.ones((), jnp.bfloat16)

    def tiles_at(first, count):
        for at in range(count):
            bins = []
            sides = []
            leaves = []
            for half in range(2):
                entry = list_ref[base + (first + at) * 2 + half]
                chip = lax.shift_right_logical(entry, 4)
                group = lax.bitwise_and(entry, 15)
                late = group >= groups // 2
                place = groups + group - jnp.where(late, groups // 2, 0)
                here = pl.ds(pl.multiple_of(group * POS, POS), POS)
                bins.append(data_ref[owner_of(chip, part), :, here])
                sides.append(side_ref[chip, :, here])
                pair = side_ref[chip, :, pl.ds(pl.multiple_of(place * POS, POS), POS)]
                leaves.append(jnp.where(late, pair[1:2], pair[0:1]))
            bins = jnp.concatenate(bins, axis=1)
            side = jnp.concatenate(sides, axis=1)
            leaf = jnp.concatenate(leaves, axis=1)
            left = []
            right = []
            for feature in range(2):
                row = bins[feature : feature + 1]
                high = row >= jnp.asarray(HALF, jnp.bfloat16)
                hit = jnp.where(high, leaf + jnp.asarray(LEAVES, jnp.bfloat16), leaf) == rows_a
                low = jnp.where(high, row - jnp.asarray(HALF, jnp.bfloat16), row)
                left.append(jnp.where(hit, side[0:1], zero))
                left.append(jnp.where(hit, side[1:2], zero))
                right.append(jnp.where(low == rows_b, one, zero))
            unit = at % 2
            register = (at // 2) % 2
            pltpu.matmul_push_rhs(jnp.concatenate(right, axis=0), register, unit, transpose=True)
            pltpu.matmul_acc_lhs(accs[unit], jnp.concatenate(left, axis=0), register)

    def wide_step(step, carry):
        tiles_at((begin + step * WIDE) * STEP, STEP * WIDE)
        return carry

    def step(step, carry):
        tiles_at(step * STEP, STEP)
        return carry

    wide = (end - begin) // WIDE
    lax.fori_loop(0, wide, wide_step, 0)
    lax.fori_loop(begin + wide * WIDE, end, step, 0)


def summed(share, core_ref, list_ref, total_ref, data_ref, side_ref, finish):
    core = core_ref[0]
    total = total_ref[core]
    early = lax.shift_right_logical(total * lax.bitwise_and(core, 1), 1)
    begin = early if share == "late" else 0
    end = early if share == "early" else total

    def run(acc_a, acc_b):
        accumulate(core, begin, end, list_ref, data_ref, side_ref, (acc_a, acc_b))
        total = pltpu.matmul_pop(acc_a) + pltpu.matmul_pop(acc_b)
        finish(jnp.where(end > begin, total, 0.0))

    shape = (8 * LEAVES, BINS)
    pl.run_scoped(run, pltpu.ACC(0)(shape, jnp.float32), pltpu.ACC(1)(shape, jnp.float32))


def part_kernel(share, core_ref, list_ref, total_ref, data_ref, side_ref, *refs):
    rows = 4 * LEAVES
    out_ref = refs[-1]

    def finish(total):
        for feature in range(2):
            mine = total[
                feature * rows : (feature + 1) * rows, feature * HALF : (feature + 1) * HALF
            ]
            out_ref[feature] = mine if len(refs) == 1 else mine + refs[0][feature]

    summed(share, core_ref, list_ref, total_ref, data_ref, side_ref, finish)


def last_kernel(share, core_ref, list_ref, total_ref, data_ref, side_ref, before_ref, out_ref):
    rows = 4 * LEAVES

    def finish(total):
        for feature in range(2):
            mine = total[
                feature * rows : (feature + 1) * rows, feature * HALF : (feature + 1) * HALF
            ] + before_ref[feature]
            for which in range(2):
                for high in range(2):
                    at = (2 * which + high) * LEAVES
                    out_ref[
                        feature,
                        which * LEAVES : (which + 1) * LEAVES,
                        high * HALF : (high + 1) * HALF,
                    ] = mine[at : at + LEAVES]

    summed(share, core_ref, list_ref, total_ref, data_ref, side_ref, finish)


VMEM = pl.BlockSpec(memory_space=pltpu.VMEM)
SMEM = pl.BlockSpec(memory_space=pltpu.SMEM)


def in_vmem(array):
    return pltpu.with_memory_space_constraint(array, pltpu.VMEM)


def in_smem(array):
    return pltpu.with_memory_space_constraint(array, pltpu.SMEM)


def hist_of(core, plan, data, side, before=None, last=False, share="all"):
    given = [in_vmem(data), in_vmem(side)]
    if before is not None:
        given.append(in_vmem(before))
    if last:
        out_shape = jax.ShapeDtypeStruct((2, 2 * LEAVES, BINS), jnp.float32)
    else:
        out_shape = pltpu.VMEM((2, 4 * LEAVES, HALF), jnp.float32)
    return pl.pallas_call(
        functools.partial(last_kernel if last else part_kernel, share),
        out_shape=out_shape,
        in_specs=[SMEM, SMEM, SMEM] + [VMEM] * len(given),
        out_specs=VMEM,
        name="last_part" if last else "part",
    )(core.reshape(1), *plan, *given)


def body(scores, clicks, lengths, t_plus_old, t_minus_old, leaf, bins):
    shards = lax.axis_size("doc")
    queries = scores.shape[0]
    slots = leaf.shape[0]
    groups = slots // POS
    places = np.arange(POS, dtype=np.float32)
    discount = (1.0 / np.log2(2.0 + places)).astype(np.float32)
    gap = np.abs(discount[:, None] - discount[None, :])
    gap = jnp.asarray(np.concatenate([gap, np.tile(discount[None], (8, 1))]))
    f32 = jnp.float32
    sent_shape = (shards, 2, slots + 2 * POS)
    given = (gap, scores, clicks, lengths, t_plus_old[None], t_minus_old[None])
    anywhere = pl.BlockSpec(memory_space=pl.ANY)
    sent = pl.pallas_call(
        pair_kernel,
        out_shape=jax.ShapeDtypeStruct(sent_shape, jnp.bfloat16),
        in_specs=[anywhere] * 7,
        out_specs=anywhere,
        scratch_shapes=[
            *(
                (pltpu.SMEM if array.ndim == 1 else pltpu.VMEM)(array.shape, array.dtype)
                for array in given
            ),
            pltpu.VMEM(bins.shape, jnp.int32),
            pltpu.VMEM(sent_shape, jnp.bfloat16),
            pltpu.VMEM((slots // POS + 1, bins.shape[0], POS), f32),
            pltpu.SemaphoreType.DMA((len(given),)),
            pltpu.SemaphoreType.DMA((1,)),
            pltpu.SemaphoreType.DMA((4,)),
        ],
        name="pair_terms",
    )(*given, bins)
    data = lax.all_to_all(sent, "doc", 0, 0, tiled=True)
    first, second, own, scale, held = pl.pallas_call(
        ready_kernel,
        out_shape=(
            pltpu.VMEM((queries, POS, POS), f32),
            pltpu.VMEM((queries, POS, POS), f32),
            pltpu.VMEM((queries, POS), f32),
            pltpu.VMEM((queries, POS), f32),
            pltpu.SMEM((queries,), jnp.int32),
        ),
        in_specs=[VMEM, VMEM, VMEM, SMEM],
        out_specs=(VMEM, VMEM, VMEM, VMEM, SMEM),
        name="ready_pairs",
    )(gap, scores, clicks, lengths)
    t_plus, t_minus, gradients, side = pl.pallas_call(
        lambda_kernel,
        out_shape=(
            pltpu.VMEM((1, POS), f32),
            pltpu.VMEM((1, POS), f32),
            pltpu.VMEM((2, slots), f32),
            pltpu.VMEM((shards // PARTS, 2, 3 * slots // 2), jnp.bfloat16),
        ),
        in_specs=[VMEM, VMEM, VMEM, VMEM, SMEM, VMEM, VMEM],
        out_specs=(VMEM,) * 4,
        scratch_shapes=[
            pltpu.VMEM((queries + 1, 8, POS), f32),
            pltpu.VMEM((2, 3 * slots // 2), f32),
        ],
        name="lambdas",
    )(
        in_vmem(first),
        in_vmem(second),
        in_vmem(own),
        in_vmem(scale),
        in_smem(held),
        in_vmem(leaf.reshape(queries, POS)),
        in_vmem(data),
    )
    alike = [
        [16 * (chip // 4) + 2 * (chip % 4) + 8 * (part // 2) + part % 2 for chip in range(16)]
        for part in range(PARTS)
    ]
    side = lax.all_to_all(side, "doc", 0, 0, axis_index_groups=alike, tiled=True)
    shown = jnp.sum((data[:, 0, :slots] >= 0).astype(f32), axis=1).astype(jnp.int32)
    *plan, t_plus, t_minus, gradients = pl.pallas_call(
        plan_kernel,
        out_shape=(
            pltpu.SMEM((shards * groups + PARTS * 16,), jnp.int32),
            pltpu.SMEM((PARTS,), jnp.int32),
            jax.ShapeDtypeStruct((1, POS), f32),
            jax.ShapeDtypeStruct((1, POS), f32),
            jax.ShapeDtypeStruct((2, slots), f32),
        ),
        in_specs=[SMEM, VMEM, VMEM, VMEM],
        out_specs=(SMEM, SMEM, VMEM, VMEM, VMEM),
        name="plan",
    )((shown + (POS - 1)) // POS, in_vmem(t_plus), in_vmem(t_minus), in_vmem(gradients))
    swap = [[(at, at ^ bit) for at in range(shards)] for bit in (1, 8)]
    index = lax.axis_index("doc")
    own = 2 * lax.rem(index // 8, 2) + lax.rem(index, 2)
    side_far = lax.ppermute(side, "doc", swap[1])
    side_near = lax.ppermute(side, "doc", swap[0])
    side_last = lax.ppermute(side_far, "doc", swap[0])
    partial = hist_of(own, plan, data, side, share="early")
    partial = hist_of(own, plan, data, side, partial, share="late")
    partial = hist_of(lax.bitwise_xor(own, 1), plan, data, side_near, partial)
    partial = hist_of(lax.bitwise_xor(own, 2), plan, data, side_far, partial)
    hist = hist_of(lax.bitwise_xor(own, 3), plan, data, side_last, partial, True)
    return (t_plus[0], t_minus[0], gradients, hist)


def solution(mesh):
    placed = (P("doc", None), P("doc", None), P("doc"), P(), P(), P("doc"), P("feat", "doc"))
    return jax.shard_map(
        body,
        mesh=mesh,
        in_specs=placed,
        out_specs=(P(), P(), P(None, "doc"), P(("feat", "doc"), None, None)),
        check_vma=False,
    )
```

```python
import functools

import jax
import jax.numpy as jnp
import numpy as np
from jax import lax
from jax.experimental import pallas as pl
from jax.experimental.pallas import tpu as pltpu
from jax.sharding import PartitionSpec as P


BINS = 256
LEAVES = 32
POS = 128
HALF = BINS // 2
TILE = 256
STEP = 4
WIDE = 4
PARTS = 4


def query_rows(scores, clicks, lengths_ref, queries, discount_row):
    lane = lax.broadcasted_iota(jnp.int32, (queries, POS), 1)
    row = lax.broadcasted_iota(jnp.int32, (queries, POS), 0)
    length = jnp.zeros((queries, POS), jnp.int32)
    for query in range(queries):
        length = jnp.where(row == query, lengths_ref[query], length)
    shown = lane < length
    clicked = shown & (clicks == 1)
    skipped = shown & (clicks == 0)
    count = jnp.sum(jnp.where(clicked, 1.0, 0.0), axis=1, keepdims=True)
    ideal = jnp.sum(
        jnp.where(lane.astype(jnp.float32) < count, discount_row, 0.0), axis=1, keepdims=True
    )
    ideal = jnp.maximum(ideal, 1.0)
    side = jnp.where(clicked, 1.0, jnp.where(skipped, -1.0, 0.0))
    return clicked, skipped, side, side * scores, ideal


def turned(rows):
    queries = rows[0].shape[0]
    pad = jnp.zeros((POS - queries * len(rows), POS), jnp.float32)
    return jnp.transpose(jnp.concatenate(list(rows) + [pad], axis=0))


def pair_kernel(*refs):
    small_from, bins_from, sent_to = refs[:6], refs[6], refs[7]
    small, bins_ref, sent_ref, packed = refs[8:14], refs[14], refs[15], refs[16]
    took_small, took, gave = refs[17:]
    gap_ref, scores_ref, clicks_ref, lengths_ref, plus_ref, minus_ref = small
    blocks = took.shape[0]
    height = bins_ref.shape[0] // blocks
    small_takes = [
        pltpu.make_async_copy(there, here, took_small.at[at])
        for at, (there, here) in enumerate(zip(small_from, small))
    ]
    takes = []
    for block in range(blocks):
        rows = pl.ds(block * height, height)
        takes.append(
            pltpu.make_async_copy(bins_from.at[rows], bins_ref.at[rows], took.at[block])
        )
    for take in small_takes + takes:
        take.start()
    for take in small_takes:
        take.wait()
    queries = scores_ref.shape[0]
    clicked, skipped, side, signed, ideal = query_rows(
        scores_ref[...], clicks_ref[...], lengths_ref, queries, gap_ref[POS : POS + 1]
    )
    weight = jnp.where(clicked, 1.0 / plus_ref[...], jnp.where(skipped, -1.0 / minus_ref[...], 0.0))
    columns = turned([signed, weight])
    scale = 1.0 / ideal
    sums = [jnp.zeros((1, POS), jnp.float32), jnp.zeros((1, POS), jnp.float32)]

    def add_query(query):
        other = columns[:, query : query + 1]
        strength = columns[:, queries + query : queries + query + 1]
        spread = other + signed[query : query + 1]
        cross = jnp.maximum(strength * -side[query : query + 1], 0.0)
        loss = jnp.maximum(-spread, 0.0) + jnp.log1p(jnp.exp(-jnp.abs(spread)))
        total = jnp.sum(cross * gap_ref[:POS] * loss, axis=0, keepdims=True)
        total = total * scale[query : query + 1]
        sums[0] += jnp.where(side[query : query + 1] > 0.0, total, 0.0)
        sums[1] += jnp.where(side[query : query + 1] < 0.0, total, 0.0)

    for query in range(queries):
        add_query(query)

    features, slots = bins_ref.shape
    owners = features // 2
    for at, part in enumerate(sums):
        high = part.astype(jnp.bfloat16).astype(jnp.float32)
        pieces = jnp.concatenate([high, part - high], axis=0).astype(jnp.bfloat16)
        sent_ref[:, :, slots + at * POS : slots + (at + 1) * POS] = jnp.broadcast_to(
            pieces[None], (owners, 2, POS)
        )
    packed[...] = jnp.full(packed.shape, -1.0, jnp.float32)
    for take in takes:
        take.wait()
    lane = lax.broadcasted_iota(jnp.int32, (1, POS), 1)
    start = jnp.int32(0)
    for query in range(queries):
        group = start // POS
        shift = start - group * POS
        length = lengths_ref[query]
        moved = pltpu.roll(
            bins_ref[:, query * POS : (query + 1) * POS].astype(jnp.float32), shift, 1
        )
        here = (lane >= shift) & (lane < shift + length)
        there = lane < shift + length - POS
        packed[group] = jnp.where(here, moved, packed[group])
        packed[group + 1] = jnp.where(there, moved, packed[group + 1])
        start += length
    chunks = gave.shape[0]
    gives = []
    for chunk in range(chunks):
        first = chunk * owners // chunks
        for owner in range(first, first + owners // chunks):
            for group in range(slots // POS):
                sent_ref[owner, :, group * POS : (group + 1) * POS] = packed[
                    group, 2 * owner : 2 * owner + 2
                ].astype(jnp.bfloat16)
        some = pl.ds(first, owners // chunks)
        gives.append(pltpu.make_async_copy(sent_ref.at[some], sent_to.at[some], gave.at[chunk]))
        gives[-1].start()
    for give in gives:
        give.wait()


def ready_kernel(gap_ref, scores_ref, clicks_ref, lengths_ref, first_ref, second_ref, side_ref,
                 scale_ref, held_ref):
    queries = scores_ref.shape[0]
    _, _, side, signed, ideal = query_rows(
        scores_ref[...], clicks_ref[...], lengths_ref, queries, gap_ref[POS : POS + 1]
    )
    side_ref[...] = side
    scale_ref[...] = jnp.broadcast_to(1.0 / ideal, scale_ref.shape)
    columns = turned([signed, side])
    for query in range(queries):
        held_ref[query] = lengths_ref[query]
        spread = columns[:, query : query + 1] + signed[query : query + 1]
        cross = columns[:, queries + query : queries + query + 1] * side[query : query + 1]
        grown = jnp.exp(spread)
        chance = 1.0 / (1.0 + grown)
        first = jnp.where(cross < 0.0, gap_ref[:POS] * chance, 0.0)
        first_ref[query] = first
        second_ref[query] = first * (grown * chance)


def lambda_kernel(first_ref, second_ref, own_ref, scale_ref, held_ref, leaf_ref, data_ref,
                  plus_ref, minus_ref, grad_ref, side_ref, packed, flat):
    queries = own_ref.shape[0]
    slots = grad_ref.shape[1]
    sums = jnp.sum(data_ref[:, :, slots:].astype(jnp.float32), axis=0)
    sums = sums[0:1] + sums[1:2]
    plus_sum = sums[:, :POS]
    minus_sum = sums[:, POS:]
    plus = jnp.sqrt(plus_sum / plus_sum[:, 0:1])
    minus = jnp.sqrt(minus_sum / minus_sum[:, 0:1])
    plus_ref[...] = plus
    minus_ref[...] = minus
    side = own_ref[...]
    weight = jnp.where(side > 0.0, 1.0 / plus, jnp.where(side < 0.0, 1.0 / minus, 0.0))
    columns = turned([weight])
    outer = weight * scale_ref[...]
    packed[...] = jnp.zeros_like(packed)
    lane = lax.broadcasted_iota(jnp.int32, (1, POS), 1)
    start = jnp.int32(0)
    for query in range(queries):
        strength = columns[:, query : query + 1]
        slope = jnp.sum(strength * first_ref[query], axis=0, keepdims=True)
        curve = jnp.sum(strength * second_ref[query], axis=0, keepdims=True)
        slope = slope * outer[query : query + 1] * -side[query : query + 1]
        curve = curve * outer[query : query + 1]
        grad_ref[0:1, query * POS : (query + 1) * POS] = slope
        grad_ref[1:2, query * POS : (query + 1) * POS] = curve
        group = start // POS
        shift = start - group * POS
        length = held_ref[query]
        rows = jnp.concatenate(
            [slope, curve, leaf_ref[query : query + 1].astype(jnp.float32),
             jnp.zeros((5, POS), jnp.float32)], axis=0
        )
        moved = pltpu.roll(rows, shift, 1)
        here = (lane >= shift) & (lane < shift + length)
        there = lane < shift + length - POS
        packed[group] = jnp.where(here, moved, packed[group])
        packed[group + 1] = jnp.where(there, moved, packed[group + 1])
        start += length
    for group in range(queries):
        rows = packed[group]
        row = group // (queries // 2)
        at = (queries + group % (queries // 2)) * POS
        flat[:, group * POS : (group + 1) * POS] = rows[0:2]
        flat[row : row + 1, at : at + POS] = rows[2:3]
    side_ref[...] = jnp.broadcast_to(flat[...].astype(jnp.bfloat16)[None], side_ref.shape)


def owner_of(chip, part):
    high = lax.shift_right_logical(chip, 2)
    return 16 * high + 2 * (chip - 4 * high) + part


def plan_kernel(
    filled_ref, plus_in, minus_in, grad_in, list_ref, total_ref, plus_ref, minus_ref, grad_ref
):
    plus_ref[...] = plus_in[...]
    minus_ref[...] = minus_in[...]
    grad_ref[...] = grad_in[...]
    chips = filled_ref.shape[0] // PARTS
    groups = grad_in.shape[1] // POS
    for core in range(PARTS):
        base = core * (list_ref.shape[0] // PARTS)

        def one_block(chip, carry):
            at, spare = carry
            used = filled_ref[owner_of(chip, 8 * (core // 2) + core % 2)]
            for group in range(groups):
                list_ref[base + at + group] = chip * 16 + group
            return at + used, jnp.where(used < groups, chip * 16 + groups - 1, spare)

        at, spare = lax.fori_loop(0, chips, one_block, (jnp.int32(0), jnp.int32(0)))
        for extra in range(2 * STEP):
            list_ref[base + at + extra] = spare
        total_ref[core] = (at + 2 * STEP - 1) // (2 * STEP)


def accumulate(core, begin, end, list_ref, data_ref, side_ref, accs):
    base = core * (list_ref.shape[0] // PARTS)
    groups = side_ref.shape[2] * 2 // (3 * POS)
    part = 8 * lax.shift_right_logical(core, 1) + lax.bitwise_and(core, 1)
    rows_a = lax.broadcasted_iota(jnp.int32, (2 * LEAVES, TILE), 0).astype(jnp.bfloat16)
    rows_b = lax.broadcasted_iota(jnp.int32, (HALF, TILE), 0).astype(jnp.bfloat16)
    zero = jnp.zeros((), jnp.bfloat16)
    one = jnp.ones((), jnp.bfloat16)

    def tiles_at(first, count):
        for at in range(count):
            bins = []
            sides = []
            leaves = []
            for half in range(2):
                entry = list_ref[base + (first + at) * 2 + half]
                chip = lax.shift_right_logical(entry, 4)
                group = lax.bitwise_and(entry, 15)
                late = group >= groups // 2
                place = groups + group - jnp.where(late, groups // 2, 0)
                here = pl.ds(pl.multiple_of(group * POS, POS), POS)
                bins.append(data_ref[owner_of(chip, part), :, here])
                sides.append(side_ref[chip, :, here])
                pair = side_ref[chip, :, pl.ds(pl.multiple_of(place * POS, POS), POS)]
                leaves.append(jnp.where(late, pair[1:2], pair[0:1]))
            bins = jnp.concatenate(bins, axis=1)
            side = jnp.concatenate(sides, axis=1)
            leaf = jnp.concatenate(leaves, axis=1)
            left = []
            right = []
            for feature in range(2):
                row = bins[feature : feature + 1]
                high = row >= jnp.asarray(HALF, jnp.bfloat16)
                hit = jnp.where(high, leaf + jnp.asarray(LEAVES, jnp.bfloat16), leaf) == rows_a
                low = jnp.where(high, row - jnp.asarray(HALF, jnp.bfloat16), row)
                left.append(jnp.where(hit, side[0:1], zero))
                left.append(jnp.where(hit, side[1:2], zero))
                right.append(jnp.where(low == rows_b, one, zero))
            unit = at % 2
            register = (at // 2) % 2
            pltpu.matmul_push_rhs(jnp.concatenate(right, axis=0), register, unit, transpose=True)
            pltpu.matmul_acc_lhs(accs[unit], jnp.concatenate(left, axis=0), register)

    def wide_step(step, carry):
        tiles_at((begin + step * WIDE) * STEP, STEP * WIDE)
        return carry

    def step(step, carry):
        tiles_at(step * STEP, STEP)
        return carry

    wide = (end - begin) // WIDE
    lax.fori_loop(0, wide, wide_step, 0)
    lax.fori_loop(begin + wide * WIDE, end, step, 0)


def summed(share, core_ref, list_ref, total_ref, data_ref, side_ref, finish):
    core = core_ref[0]
    total = total_ref[core]
    odd = lax.bitwise_and(lax.axis_index("doc"), 1)
    quarters, late = share
    early = lax.shift_right_logical(total * odd * quarters, 2)
    begin = early if late else 0
    end = total if late else early

    def run(acc_a, acc_b):
        accumulate(core, begin, end, list_ref, data_ref, side_ref, (acc_a, acc_b))
        total = pltpu.matmul_pop(acc_a) + pltpu.matmul_pop(acc_b)
        finish(jnp.where(end > begin, total, 0.0))

    shape = (8 * LEAVES, BINS)
    pl.run_scoped(run, pltpu.ACC(0)(shape, jnp.float32), pltpu.ACC(1)(shape, jnp.float32))


def part_kernel(share, core_ref, list_ref, total_ref, data_ref, side_ref, *refs):
    rows = 4 * LEAVES
    out_ref = refs[-1]

    def finish(total):
        for feature in range(2):
            mine = total[
                feature * rows : (feature + 1) * rows, feature * HALF : (feature + 1) * HALF
            ]
            out_ref[feature] = mine if len(refs) == 1 else mine + refs[0][feature]

    summed(share, core_ref, list_ref, total_ref, data_ref, side_ref, finish)


def last_kernel(share, core_ref, list_ref, total_ref, data_ref, side_ref, before_ref, out_ref):
    rows = 4 * LEAVES

    def finish(total):
        for feature in range(2):
            mine = total[
                feature * rows : (feature + 1) * rows, feature * HALF : (feature + 1) * HALF
            ] + before_ref[feature]
            for which in range(2):
                for high in range(2):
                    at = (2 * which + high) * LEAVES
                    out_ref[
                        feature,
                        which * LEAVES : (which + 1) * LEAVES,
                        high * HALF : (high + 1) * HALF,
                    ] = mine[at : at + LEAVES]

    summed(share, core_ref, list_ref, total_ref, data_ref, side_ref, finish)


VMEM = pl.BlockSpec(memory_space=pltpu.VMEM)
SMEM = pl.BlockSpec(memory_space=pltpu.SMEM)


def in_vmem(array):
    return pltpu.with_memory_space_constraint(array, pltpu.VMEM)


def in_smem(array):
    return pltpu.with_memory_space_constraint(array, pltpu.SMEM)


def hist_of(core, plan, data, side, before=None, last=False, share=(0, True)):
    given = [in_vmem(data), in_vmem(side)]
    if before is not None:
        given.append(in_vmem(before))
    if last:
        out_shape = jax.ShapeDtypeStruct((2, 2 * LEAVES, BINS), jnp.float32)
    else:
        out_shape = pltpu.VMEM((2, 4 * LEAVES, HALF), jnp.float32)
    return pl.pallas_call(
        functools.partial(last_kernel if last else part_kernel, share),
        out_shape=out_shape,
        in_specs=[SMEM, SMEM, SMEM] + [VMEM] * len(given),
        out_specs=VMEM,
        name="last_part" if last else "part",
    )(core.reshape(1), *plan, *given)


def body(scores, clicks, lengths, t_plus_old, t_minus_old, leaf, bins):
    shards = lax.axis_size("doc")
    queries = scores.shape[0]
    slots = leaf.shape[0]
    groups = slots // POS
    places = np.arange(POS, dtype=np.float32)
    discount = (1.0 / np.log2(2.0 + places)).astype(np.float32)
    gap = np.abs(discount[:, None] - discount[None, :])
    gap = jnp.asarray(np.concatenate([gap, np.tile(discount[None], (8, 1))]))
    f32 = jnp.float32
    sent_shape = (shards, 2, slots + 2 * POS)
    given = (gap, scores, clicks, lengths, t_plus_old[None], t_minus_old[None])
    anywhere = pl.BlockSpec(memory_space=pl.ANY)
    sent = pl.pallas_call(
        pair_kernel,
        out_shape=jax.ShapeDtypeStruct(sent_shape, jnp.bfloat16),
        in_specs=[anywhere] * 7,
        out_specs=anywhere,
        scratch_shapes=[
            *(
                (pltpu.SMEM if array.ndim == 1 else pltpu.VMEM)(array.shape, array.dtype)
                for array in given
            ),
            pltpu.VMEM(bins.shape, jnp.int32),
            pltpu.VMEM(sent_shape, jnp.bfloat16),
            pltpu.VMEM((slots // POS + 1, bins.shape[0], POS), f32),
            pltpu.SemaphoreType.DMA((len(given),)),
            pltpu.SemaphoreType.DMA((1,)),
            pltpu.SemaphoreType.DMA((4,)),
        ],
        name="pair_terms",
    )(*given, bins)
    data = lax.all_to_all(sent, "doc", 0, 0, tiled=True)
    first, second, own, scale, held = pl.pallas_call(
        ready_kernel,
        out_shape=(
            pltpu.VMEM((queries, POS, POS), f32),
            pltpu.VMEM((queries, POS, POS), f32),
            pltpu.VMEM((queries, POS), f32),
            pltpu.VMEM((queries, POS), f32),
            pltpu.SMEM((queries,), jnp.int32),
        ),
        in_specs=[VMEM, VMEM, VMEM, SMEM],
        out_specs=(VMEM, VMEM, VMEM, VMEM, SMEM),
        name="ready_pairs",
    )(gap, scores, clicks, lengths)
    t_plus, t_minus, gradients, side = pl.pallas_call(
        lambda_kernel,
        out_shape=(
            pltpu.VMEM((1, POS), f32),
            pltpu.VMEM((1, POS), f32),
            pltpu.VMEM((2, slots), f32),
            pltpu.VMEM((shards // PARTS, 2, 3 * slots // 2), jnp.bfloat16),
        ),
        in_specs=[VMEM, VMEM, VMEM, VMEM, SMEM, VMEM, VMEM],
        out_specs=(VMEM,) * 4,
        scratch_shapes=[
            pltpu.VMEM((queries + 1, 8, POS), f32),
            pltpu.VMEM((2, 3 * slots // 2), f32),
        ],
        name="lambdas",
    )(
        in_vmem(first),
        in_vmem(second),
        in_vmem(own),
        in_vmem(scale),
        in_smem(held),
        in_vmem(leaf.reshape(queries, POS)),
        in_vmem(data),
    )
    alike = [
        [16 * (chip // 4) + 2 * (chip % 4) + 8 * (part // 2) + part % 2 for chip in range(16)]
        for part in range(PARTS)
    ]
    side = lax.all_to_all(side, "doc", 0, 0, axis_index_groups=alike, tiled=True)
    shown = jnp.sum((data[:, 0, :slots] >= 0).astype(f32), axis=1).astype(jnp.int32)
    *plan, t_plus, t_minus, gradients = pl.pallas_call(
        plan_kernel,
        out_shape=(
            pltpu.SMEM((shards * groups + PARTS * 16,), jnp.int32),
            pltpu.SMEM((PARTS,), jnp.int32),
            jax.ShapeDtypeStruct((1, POS), f32),
            jax.ShapeDtypeStruct((1, POS), f32),
            jax.ShapeDtypeStruct((2, slots), f32),
        ),
        in_specs=[SMEM, VMEM, VMEM, VMEM],
        out_specs=(SMEM, SMEM, VMEM, VMEM, VMEM),
        name="plan",
    )((shown + (POS - 1)) // POS, in_vmem(t_plus), in_vmem(t_minus), in_vmem(gradients))
    swap = [[(at, at ^ bit) for at in range(shards)] for bit in (1, 8)]
    index = lax.axis_index("doc")
    own = 2 * lax.rem(index // 8, 2) + lax.rem(index, 2)
    side_far = lax.ppermute(side, "doc", swap[1])
    side_near = lax.ppermute(side, "doc", swap[0])
    side_last = lax.ppermute(side_far, "doc", swap[0])
    partial = hist_of(own, plan, data, side, share=(3, False))
    partial = hist_of(own, plan, data, side, partial, share=(3, True))
    partial = hist_of(lax.bitwise_xor(own, 1), plan, data, side_near, partial)
    across = lax.bitwise_xor(own, 2)
    partial = hist_of(across, plan, data, side_far, partial, share=(2, False))
    partial = hist_of(across, plan, data, side_far, partial, share=(2, True))
    hist = hist_of(lax.bitwise_xor(own, 3), plan, data, side_last, partial, True)
    return (t_plus[0], t_minus[0], gradients, hist)


def solution(mesh):
    placed = (P("doc", None), P("doc", None), P("doc"), P(), P(), P("doc"), P("feat", "doc"))
    return jax.shard_map(
        body,
        mesh=mesh,
        in_specs=placed,
        out_specs=(P(), P(), P(None, "doc"), P(("feat", "doc"), None, None)),
        check_vma=False,
    )
```
